128 devices in a mesh: section: 2 (over z_lo), dp: 8 (over z_hi, y), ctx: 8 (over x, core).
Axes of the slice: x: 4, y: 4, z: 4 (z_hi: 2, z_lo: 2; z = z_hi * 2 + z_lo), core: 2. Of those that a mesh axis runs over, the one named last changes fastest.
Arguments:
- token_ids: int32 [2048], P('ctx'), may hold values from 0 to 511
- embedding: bfloat16 [512, 4096], P(None, 'dp'), may hold values from -6 to 6
- project_in: bfloat16 [2, 4096, 3, 4096], P('section', 'ctx', None, 'dp'), may hold values from -0.09375 to 0.09375
- short_taps: float32 [2, 3, 3, 4096], P('section', None, None, 'dp'), may hold values from -3.5 to 3.5
- filter_taps: float32 [2, 128, 4096], P('section', None, 'dp'), may hold values from -0.5 to 0.5
- decay_rates: float32 [2, 4096], P('section', 'dp'), may hold values from 0.5 to 4
- project_out: bfloat16 [2, 4096, 4096], P('section', 'dp', 'ctx'), may hold values from -0.09375 to 0.09375
- cotangent: bfloat16 [2048, 4096], P('ctx', 'dp'), may hold values from -0.125 to 0.125
Outputs:
- grad_project_in: float32 [2, 4096, 3, 4096], P('section', 'ctx', None, 'dp')
- grad_project_out: float32 [2, 4096, 4096], P('section', 'dp', 'ctx')
- grad_filter: float32 [2, 128, 4096], P('section', None, 'dp')
- grad_decay: float32 [2, 4096], P('section', 'dp')
- grad_short: float32 [2, 3, 3, 4096], P('section', None, None, 'dp')
The draws below stay inside these ranges and needn't reach their ends.
All inputs are finite; a program needn't handle non-finite values.
Results may differ from the reference program's by a relative error of at most 0.03.
Values may be sent and summed in bfloat16 or wider, within the bound.
A program may use at most 128 MiB of HBM per device.

```python
import math
import jax
import jax.numpy as jnp
from jax import lax

D = 4096
C = 4096
L = 128
VOCAB = 512
TOK_DEV = 256
SEQ = 2048
N_SECTION = 2
N_DP = 8
N_CTX = 8


def set_ends(entries, rng, low, top_value):
    dims = entries.shape
    place = [jax.random.randint(jax.random.fold_in(rng, axis), (), 0, dims[axis]) for axis in range(len(dims))]
    entries = entries.at[tuple(place)].set(low)
    longest = dims.index(max(dims))
    place[longest] = (place[longest] + 1) % dims[longest]
    return entries.at[tuple(place)].set(top_value)


def levels(key, shape, split, smallest, largest):
    loudness = 1.0
    for position, blocks in split:
        draws = jax.random.uniform(jax.random.fold_in(jax.random.fold_in(key, 6), position), (blocks,), jnp.float32, smallest / len(split), largest / len(split))
        loudness = loudness * jnp.repeat(jnp.exp(draws), shape[position] // blocks).reshape((-1,) + (1,) * (len(shape) - 1 - position))
    return loudness


def centred(key, shape, width, limit, cuts=(), kind=jnp.bfloat16):
    drawn = width * jax.random.normal(key, shape, jnp.float32)
    if cuts:
        drawn = drawn * levels(key, shape, cuts, -0.22, 0.18)
    return jnp.clip(drawn, -limit, limit).astype(kind)


def setup_inputs(seed: int = 0) -> dict:
    key_list = jax.random.split(jax.random.key(seed), 9)
    token_ids = set_ends(jax.random.randint(key_list[0], (SEQ,), 0, VOCAB), jax.random.fold_in(key_list[0], 1), 0, VOCAB - 1).astype(jnp.int32)
    embedding = centred(key_list[1], (VOCAB, D), 1.0, 6.0, ((1, 8),))
    project_in = centred(key_list[2], (N_SECTION, D, 3, C), D ** -0.5, 0.09375, ((0, 2), (1, 8), (3, 8)))
    short_taps = centred(key_list[3], (N_SECTION, 3, 3, C), 3 ** -0.5, 3.5, ((0, 2), (3, 8)), jnp.float32)
    filter_taps = centred(key_list[4], (N_SECTION, L, C), L ** -0.5, 0.5, ((0, 2), (2, 8)), jnp.float32)
    decay_rates = jnp.clip(jnp.exp(math.log(4.0) - 2.0794415 * jax.random.uniform(key_list[5], (N_SECTION, C), jnp.float32) ** levels(key_list[5], (N_SECTION, C), ((0, 2), (1, 8)), -0.2, 0.2)), 0.5, 4.0)
    project_out = centred(key_list[6], (N_SECTION, C, D), C ** -0.5, 0.09375, ((0, 2), (1, 8), (2, 8)))
    cotangent = centred(key_list[7], (SEQ, D), SEQ ** -0.5, 0.125, ((0, 8), (1, 8)))
    return {"token_ids": token_ids, "embedding": embedding, "project_in": project_in, "short_taps": short_taps, "filter_taps": filter_taps, "decay_rates": decay_rates, "project_out": project_out, "cotangent": cotangent}


EPSILON = 1e-06

def correlate(signal, kernel):
    tap_count = kernel.shape[0]
    out_len = signal.shape[0] - tap_count + 1

    def add_tap(index, total):
        window = lax.dynamic_slice_in_dim(signal, index, out_len, 0)
        weight_row = lax.dynamic_slice_in_dim(kernel, index, 1, 0)
        return total + window * weight_row
    return lax.fori_loop(0, tap_count, add_tap, jnp.zeros((out_len, signal.shape[1]), signal.dtype))

def round_trip(values):
    return lax.optimization_barrier(values.astype(jnp.bfloat16)).astype(jnp.float32)

def forward_block(inputs, project_in, short_taps, filter_taps, decay_rates, project_out):
    seq_len = inputs.shape[0]
    rows_float = inputs.astype(jnp.float32)
    inv_rms = lax.rsqrt(lax.optimization_barrier(jnp.mean(rows_float * rows_float, axis=1, keepdims=True)) + EPSILON)
    normed = (rows_float * inv_rms).astype(jnp.bfloat16)
    projected = jnp.dot(normed, project_in.reshape(D, 3 * C), preferred_element_type=jnp.float32).reshape(seq_len, 3, C)
    padded_proj = jnp.concatenate([jnp.zeros((2, 3, C), jnp.float32), projected], axis=0)
    shortened = short_taps[0] * padded_proj[2:] + short_taps[1] * padded_proj[1:-1] + short_taps[2] * padded_proj[:-2]
    products = shortened[:, 1] * shortened[:, 2]
    padded_prod = jnp.concatenate([jnp.zeros((L - 1, C), jnp.float32), products], axis=0)
    positions = jnp.arange(L).astype(jnp.float32)
    damping = jnp.exp(-decay_rates[None, :] * positions[:, None] / L)
    kernel = filter_taps * damping
    filtered = correlate(padded_prod, kernel[::-1])
    gated_rows = (shortened[:, 0] * filtered).astype(jnp.bfloat16)
    group_width = C // N_DP
    running = jnp.zeros((seq_len, D), jnp.float32)
    for group_index in range(N_DP):
        lower_edge = group_index * group_width
        group_part = jnp.dot(gated_rows[:, lower_edge:lower_edge + group_width], project_out[lower_edge:lower_edge + group_width], preferred_element_type=jnp.float32)
        running = running + round_trip(group_part)
    outputs = (rows_float + running).astype(jnp.bfloat16)
    return (outputs, (rows_float, inv_rms, normed, padded_proj, shortened, padded_prod, filtered, gated_rows, kernel, damping, positions))

def backward_block(saved, grad_rows, project_in, short_taps, filter_taps, project_out, need_input):
    rows_float, inv_rms, normed, padded_proj, shortened, padded_prod, filtered, gated_rows, kernel, damping, positions = saved
    seq_len = grad_rows.shape[0]
    grad_gated = jnp.dot(grad_rows, project_out.T, preferred_element_type=jnp.float32)
    grad_query = grad_gated * filtered
    grad_filtered = grad_gated * shortened[:, 0]
    padded_grad = jnp.concatenate([grad_filtered, jnp.zeros((L - 1, C), jnp.float32)], axis=0)
    grad_prod = correlate(padded_grad, kernel)
    grad_kernel = correlate(padded_prod, grad_filtered)[::-1]
    grad_short_out = jnp.stack([grad_query, grad_prod * shortened[:, 2], grad_prod * shortened[:, 1]], axis=1)
    padded_short = jnp.concatenate([grad_short_out, jnp.zeros((2, 3, C), jnp.float32)], axis=0)
    grad_proj = short_taps[0] * padded_short[:-2] + short_taps[1] * padded_short[1:-1] + short_taps[2] * padded_short[2:]
    grad_taps = jnp.stack([lax.optimization_barrier(jnp.sum(grad_short_out * padded_proj[2:], axis=0)), lax.optimization_barrier(jnp.sum(grad_short_out * padded_proj[1:-1], axis=0)), lax.optimization_barrier(jnp.sum(grad_short_out * padded_proj[:-2], axis=0))], axis=0)
    grad_proj_b = grad_proj.astype(jnp.bfloat16)
    grad_filter = grad_kernel * damping
    grad_decay = -lax.optimization_barrier(jnp.sum(grad_kernel * filter_taps * damping * positions[:, None], axis=0)) / L
    flat_grad = grad_proj_b.reshape(seq_len, 3 * C)
    grad_in = jnp.zeros((D, 3 * C), jnp.float32)
    grad_out = jnp.zeros((C, D), jnp.float32)
    for slice_index in range(N_CTX):
        lower_edge = slice_index * TOK_DEV
        upper_edge = lower_edge + TOK_DEV
        grad_in = grad_in + round_trip(jnp.dot(normed[lower_edge:upper_edge].T, flat_grad[lower_edge:upper_edge], preferred_element_type=jnp.float32))
        grad_out = grad_out + round_trip(jnp.dot(gated_rows[lower_edge:upper_edge].T, grad_rows[lower_edge:upper_edge], preferred_element_type=jnp.float32))
    grad_in = grad_in.reshape(D, 3, C)
    grad_inputs = None
    if need_input:
        group_width = C // N_DP
        grad_normed = jnp.zeros((seq_len, D), jnp.float32)
        for group_index in range(N_DP):
            lower_edge = group_index * group_width
            upper_edge = lower_edge + group_width
            left_part = grad_proj_b[:, :, lower_edge:upper_edge].reshape(seq_len, 3 * group_width)
            right_part = project_in[:, :, lower_edge:upper_edge].reshape(D, 3 * group_width)
            grad_normed = grad_normed + round_trip(jnp.dot(left_part, right_part.T, preferred_element_type=jnp.float32))
        row_stat = lax.optimization_barrier(jnp.mean(rows_float * grad_normed, axis=1, keepdims=True))
        grad_inputs = (grad_rows.astype(jnp.float32) + inv_rms * grad_normed - rows_float * inv_rms ** 3 * row_stat).astype(jnp.bfloat16)
    return (grad_inputs, (grad_in, grad_out, grad_filter, grad_decay, grad_taps))

def reference(token_ids, embedding, project_in, short_taps, filter_taps, decay_rates, project_out, cotangent):
    first_rows = embedding[token_ids]
    middle_rows, saved_first = forward_block(first_rows, project_in[0], short_taps[0], filter_taps[0], decay_rates[0], project_out[0])
    final_rows, saved_second = forward_block(middle_rows, project_in[1], short_taps[1], filter_taps[1], decay_rates[1], project_out[1])
    back_grad, second_grads = backward_block(saved_second, cotangent, project_in[1], short_taps[1], filter_taps[1], project_out[1], True)
    unused_grad, first_grads = backward_block(saved_first, back_grad, project_in[0], short_taps[0], filter_taps[0], project_out[0], False)
    return (jnp.stack([first_grads[0], second_grads[0]]), jnp.stack([first_grads[1], second_grads[1]]), jnp.stack([first_grads[2], second_grads[2]]), jnp.stack([first_grads[3], second_grads[3]]), jnp.stack([first_grads[4], second_grads[4]]))
```

```python
import functools

import jax
import jax.numpy as jnp
from jax import lax
from jax.experimental import pallas as pl
from jax.experimental.pallas import tpu as pltpu
from jax.sharding import PartitionSpec as P

EPSILON = 1e-06
F32 = jnp.float32
BF16 = jnp.bfloat16
MESH = pl.DeviceIdType.MESH
BACK = 136
AHEAD = 1184
KEPT = 1040
RING = 4


class Group:
    def __init__(self, axis):
        self.axis = axis
        me = lax.axis_index(axis)
        if axis == "ctx":
            self.ring, self.pair = me // 2, me % 2
        else:
            self.ring, self.pair = me % RING, me // RING
        self.right = (self.ring + 1) % RING
        self.left = (self.ring + RING - 1) % RING
        self.across = (self.ring + 2) % RING
        self.mate = 1 - self.pair

    def slot(self, ring, pair):
        return ring * 2 + pair if self.axis == "ctx" else pair * RING + ring

    def at(self, ring, pair):
        return {self.axis: self.slot(ring, pair)}

    def neighbours(self):
        return [
            self.at(self.right, self.pair),
            self.at(self.left, self.pair),
            self.at(self.ring, self.mate),
        ]


class Pool:
    def __init__(self, send, recv):
        self.send, self.recv, self.count = send, recv, 0

    def take(self, k):
        first = self.count
        self.count += k
        return [(self.send.at[first + i], self.recv.at[first + i]) for i in range(k)]


def remote(src, dst, sems, device):
    copy = pltpu.make_async_remote_copy(
        src_ref=src,
        dst_ref=dst,
        send_sem=sems[0],
        recv_sem=sems[1],
        device_id=device,
        device_id_type=MESH,
    )
    copy.start()
    return copy


def greet(devices, barrier):
    for device in devices:
        pl.semaphore_signal(barrier, inc=1, device_id=device, device_id_type=MESH)


class Gather:
    def __init__(self, group, src, out, pool, pair_first):
        self.g, self.src, self.out, self.pair_first = group, src, out, pair_first
        self.sems = pool.take(9)
        self.own = pool.take(1)[0]
        self.half = out.shape[1] // 2

    def block(self, ring, pair):
        return self.out.at[self.g.slot(ring, pair)]

    def part(self, ring, pair, second):
        return self.out.at[self.g.slot(ring, pair), pl.ds(self.half * second, self.half)]

    def start(self):
        g, s = self.g, self.sems
        mine = self.block(g.ring, g.pair)
        right, left, mate = g.neighbours()
        self.local = pltpu.make_async_copy(self.src, mine, self.own[0])
        self.local.start()
        first = remote(self.src, mine, s[0], mate)
        self.copies = [first, remote(self.src, mine, s[1], right), remote(self.src, mine, s[2], left)]

    def turn(self, pair, a, b, c, d):
        g, s = self.g, self.sems
        right, left, mate = g.neighbours()
        more = []
        a.wait_recv()
        part = self.part(g.left, pair, 0)
        more.append(remote(part, part, s[c], right))
        if not self.pair_first:
            block = self.block(g.left, pair)
            more.append(remote(block, block, s[5], mate))
        b.wait_recv()
        part = self.part(g.right, pair, 1)
        more.append(remote(part, part, s[d], left))
        if not self.pair_first:
            block = self.block(g.right, pair)
            more.append(remote(block, block, s[6], mate))
        return more

    def middle(self):
        g, s = self.g, self.sems
        right, left, mate = g.neighbours()
        mate_copy, to_right, to_left = self.copies
        rest = self.turn(g.pair, to_right, to_left, 3, 4)
        self.sent = list(self.copies) + rest
        if self.pair_first:
            self.late = list(rest)
            mate_copy.wait_recv()
            block = self.block(g.ring, g.mate)
            a = remote(block, block, s[5], right)
            b = remote(block, block, s[6], left)
            more = self.turn(g.mate, a, b, 7, 8)
            self.sent += [a, b] + more
            self.late += more
        else:
            rest[0].wait_recv()
            rest[2].wait_recv()
            block = self.block(g.across, g.pair)
            last = remote(block, block, s[7], mate)
            self.sent.append(last)
            self.late = [mate_copy, rest[1], rest[3], last]

    def finish(self):
        for copy in self.late:
            copy.wait_recv()
        for copy in self.sent:
            copy.wait_send()
        self.local.wait()


def add_into(out, terms, rows=64):
    @pl.loop(0, out.shape[0] // rows)
    def _(step):
        here = pl.ds(pl.multiple_of(step * rows, rows), rows)
        total = terms[0][here].astype(F32)
        for term in terms[1:]:
            total = total + term[here].astype(F32)
        out[here] = total.astype(out.dtype)


def rows_step(count):
    for rows in (64, 48, 37 * 16, 32, 16):
        if count % rows == 0:
            return rows if rows != 37 * 16 else 16
    return 16


class Around:
    def __init__(self, group, pool, bufs):
        self.g = group
        self.s = pool.take(6)
        self.rel, self.merged, self.came = bufs
        self.half = self.rel.shape[1]

    @staticmethod
    def scratch(rows, lanes):
        half = rows // 2
        return [
            pltpu.VMEM((2, half, lanes), BF16),
            pltpu.VMEM((2, half, lanes), BF16),
            pltpu.VMEM((2, 2, half, lanes), BF16),
        ]

    def halves(self, ref):
        return ref.at[pl.ds(0, self.half)], ref.at[pl.ds(self.half, self.half)]

    def send_across(self, block):
        right, left, _ = self.g.neighbours()
        a, b = self.halves(block)
        self.copies = [remote(a, self.rel.at[0], self.s[0], right), remote(b, self.rel.at[1], self.s[1], left)]

    def send_near(self, to_right, to_left):
        right, left, _ = self.g.neighbours()
        self.to_right, self.to_left = to_right, to_left
        b = self.halves(to_right)[1]
        a = self.halves(to_left)[0]
        self.copies += [
            remote(b, self.came.at[0, 1], self.s[2], right),
            remote(a, self.came.at[1, 0], self.s[3], left),
        ]

    def merge(self):
        right, left, _ = self.g.neighbours()
        step = rows_step(self.half)
        self.copies[0].wait_recv()
        add_into(self.merged.at[0], [self.halves(self.to_right)[0], self.rel.at[0]], step)
        self.copies.append(remote(self.merged.at[0], self.came.at[0, 0], self.s[4], right))
        self.copies[1].wait_recv()
        add_into(self.merged.at[1], [self.halves(self.to_left)[1], self.rel.at[1]], step)
        self.copies.append(remote(self.merged.at[1], self.came.at[1, 1], self.s[5], left))

    def collect(self, out, own):
        step = rows_step(self.half)
        for copy in self.copies[2:]:
            copy.wait_recv()
        for h in range(2):
            piece = pl.ds(h * self.half, self.half)
            add_into(
                out.at[piece],
                [ref.at[piece] for ref in own] + [self.came.at[0, h], self.came.at[1, h]],
                step,
            )

    def finish(self):
        for copy in self.copies:
            copy.wait_send()


class PairThenRing:
    def __init__(self, group, inp, pool, bufs):
        self.g, self.inp = group, inp
        self.got, self.sums = bufs[:2]
        self.ring = Around(group, pool, bufs[2:])
        self.s = pool.take(4)

    @staticmethod
    def scratch(rows, lanes):
        return [pltpu.VMEM((4, rows, lanes), BF16), pltpu.VMEM((4, rows, lanes), BF16)] + Around.scratch(rows, lanes)

    def run(self, out):
        g = self.g
        mate = g.at(g.ring, g.mate)
        order = [g.across, g.right, g.left, g.ring]
        copies = [
            remote(self.inp.at[g.slot(r, g.mate)], self.got.at[k], self.s[k], mate) for k, r in enumerate(order)
        ]
        step = rows_step(self.inp.shape[1])

        def pair_sum(k):
            copies[k].wait_recv()
            add_into(self.sums.at[k], [self.inp.at[g.slot(order[k], g.pair)], self.got.at[k]], step)

        pair_sum(0)
        self.ring.send_across(self.sums.at[0])
        pair_sum(1)
        pair_sum(2)
        self.ring.send_near(self.sums.at[1], self.sums.at[2])
        copies[3].wait_recv()
        self.ring.merge()
        self.ring.collect(out, [self.inp.at[g.slot(g.ring, g.pair)], self.got.at[3]])
        self.ring.finish()
        for copy in copies:
            copy.wait_send()


class RingThenPair:
    def __init__(self, group, inp, pool, bufs):
        self.g, self.inp = group, inp
        self.far, self.got = bufs[:2]
        self.rings = [Around(group, pool, bufs[2:5]), Around(group, pool, bufs[5:8])]
        self.s = pool.take(1)[0]

    @staticmethod
    def scratch(rows, lanes):
        return (
            [pltpu.VMEM((rows, lanes), BF16), pltpu.VMEM((rows, lanes), BF16)]
            + Around.scratch(rows, lanes)
            + Around.scratch(rows, lanes)
        )

    def run(self, out, extra=()):
        g = self.g
        pairs = [g.mate, g.pair]
        blocks = lambda ring, pair: self.inp.at[g.slot(ring, pair)]
        for ring, pair in zip(self.rings, pairs):
            ring.send_across(blocks(g.across, pair))
            ring.send_near(blocks(g.right, pair), blocks(g.left, pair))
        self.rings[0].merge()
        self.rings[1].merge()
        self.rings[0].collect(self.far, [blocks(g.ring, g.mate)])
        copy = remote(self.far, self.got, self.s, g.at(g.ring, g.mate))
        self.rings[1].collect(out, [blocks(g.ring, g.pair)])
        copy.wait_recv()
        add_into(out, [out, self.got] + list(extra), rows_step(out.shape[0]))
        copy.wait_send()
        for ring in self.rings:
            ring.finish()


ANY = pl.BlockSpec(memory_space=pl.ANY)
VMEM = pl.BlockSpec(memory_space=pltpu.VMEM)


def call(body, ident, outs, scratch, sems, *args, in_specs=None, out_specs=None, name=None):
    return pl.pallas_call(
        body,
        out_shape=[jax.ShapeDtypeStruct(shape, dtype) for shape, dtype in outs],
        in_specs=in_specs or [VMEM] * len(args),
        out_specs=out_specs or [VMEM] * len(outs),
        scratch_shapes=list(scratch)
        + [pltpu.SemaphoreType.DMA((sems,)), pltpu.SemaphoreType.DMA((sems,))],
        compiler_params=pltpu.CompilerParams(
            collective_id=ident, has_side_effects=True, vmem_limit_bytes=60 * 1024 * 1024
        ),
        name=name,
    )(*args)


def section_is(k):
    return lax.axis_index("section") == k


def crossing():
    i, j = lax.axis_index("dp"), lax.axis_index("ctx")
    return {"dp": j, "ctx": i}, i != j


def other_section():
    i, j = lax.axis_index("dp"), lax.axis_index("ctx")
    return {"section": 1 - lax.axis_index("section"), "dp": j, "ctx": i}


def begin_kernel(
    emb_ref, w_ref, w_far, cot_ref, tok_ref,
    emb_out, table_out, inv_out, tok_out, w_out, e1_out,
    parts, crossed, half_out, *rest,
):
    bufs, (send, recv) = rest[:-2], rest[-2:]
    barrier = pltpu.get_barrier_semaphore()
    ctx, dp = Group("ctx"), Group("dp")
    partner, apart = crossing()
    greet(ctx.neighbours() + dp.neighbours(), barrier)

    @pl.when(apart)
    def _():
        greet([partner], barrier)

    pl.semaphore_wait(barrier, 6 + jnp.where(apart, 1, 0))

    lane = 128
    strips = RING
    pool = Pool(send, recv)
    cross_sem = pool.take(1)[0]
    same_sem = pool.take(1)[0]
    pair_sems = pool.take(2)

    def cross(src, dst):
        @pl.when(apart)
        def _():
            remote(src, dst, cross_sem, partner).wait()

        @pl.when(jnp.logical_not(apart))
        def _():
            copy = pltpu.make_async_copy(src, dst, same_sem[0])
            copy.start()
            copy.wait()

    @pl.when(section_is(0))
    def _():
        mine = Pool(send, recv)
        mine.count = pool.count
        tokens = Gather(ctx, tok_ref, tok_out, mine, False)
        tokens.start()
        cross(emb_ref, emb_out)
        tokens.middle()
        vocab, width = emb_ref.shape
        hold = vocab // 2
        for core in range(2):
            rows = pl.ds(core * hold, hold)
            values = emb_out[rows].astype(F32)
            square = jnp.broadcast_to(jnp.sum(values * values, axis=1, keepdims=True), (hold, lane)).astype(BF16)
            for strip in range(strips):
                parts[strip * 2 + core, :, 3 * lane :] = square

        @pl.loop(0, 3 * strips)
        def _(k):
            strip, m = k // 3, k % 3
            columns = pl.ds(pl.multiple_of(m * strips * lane + strip * lane, lane), lane)
            product = jnp.dot(emb_out[...], w_ref[:, columns], preferred_element_type=F32).astype(BF16)
            to = pl.ds(pl.multiple_of(m * lane, lane), lane)
            parts[strip * 2, :, to] = product[:hold]
            parts[strip * 2 + 1, :, to] = product[hold:]

        PairThenRing(ctx, parts, mine, bufs).run(half_out)
        here = pl.ds(pl.multiple_of(ctx.pair * hold, hold), hold)
        total = half_out[...]
        inv = lax.rsqrt(total[:, 3 * lane :] / (width * 2 * RING) + EPSILON)
        inv_out[here] = inv
        for m in range(3):
            table_out[here, m * lane : (m + 1) * lane] = (total[:, m * lane : (m + 1) * lane] * inv).astype(BF16)
        mate = ctx.at(ctx.ring, ctx.mate)
        a = remote(inv_out.at[here], inv_out.at[here], pair_sems[0], mate)
        b = remote(table_out.at[here], table_out.at[here], pair_sems[1], mate)
        tokens.finish()
        a.wait()
        b.wait()

    @pl.when(section_is(1))
    def _():
        mine = Pool(send, recv)
        mine.count = pool.count
        weights = Gather(ctx, w_far, w_out, mine, False)
        weights.start()
        cross(cot_ref, crossed)
        cots = Gather(dp, crossed, e1_out, mine, True)
        cots.start()
        cots.middle()
        cots.finish()
        weights.middle()
        weights.finish()


def relay_barrier():
    barrier = pltpu.get_barrier_semaphore()
    dp = Group("dp")
    greet(dp.neighbours() + [other_section()], barrier)
    pl.semaphore_wait(barrier, 4)
    return dp


def forth_kernel(part_ref, first_ref, all_ref, arrived_ref, total, block, *rest):
    bufs, (send, recv) = rest[:-2], rest[-2:]
    dp = relay_barrier()
    pool = Pool(send, recv)
    relay = pool.take(1)[0]

    @pl.when(section_is(0))
    def _():
        RingThenPair(dp, part_ref, pool, bufs).run(total, [first_ref])
        block[...] = total[...].astype(BF16)
        remote(block, arrived_ref, relay, other_section()).wait_send()

    @pl.when(section_is(1))
    def _():
        mine = Pool(send, recv)
        mine.count = 1
        pltpu.make_async_remote_copy(
            src_ref=block, dst_ref=arrived_ref, send_sem=relay[0], recv_sem=relay[1],
            device_id=other_section(), device_id_type=MESH,
        ).wait_recv()
        rows = Gather(dp, arrived_ref, all_ref, mine, True)
        rows.start()
        rows.middle()
        rows.finish()


def back_kernel(
    part_ref, stat_ref, inv_ref, cot_ref, x_ref, all_ref, stats, arrived, total, block, *rest
):
    bufs, (send, recv) = rest[:-2], rest[-2:]
    dp = relay_barrier()
    pool = Pool(send, recv)
    relay = pool.take(1)[0]

    @pl.when(section_is(1))
    def _():
        stat = Gather(dp, stat_ref, stats, pool, True)
        stat.start()
        stat.middle()
        RingThenPair(dp, part_ref, pool, bufs).run(total)
        stat.finish()
        rows, width = total.shape
        lane = 128
        summed = stats[0]
        for k in range(1, 8):
            summed = summed + stats[k]
        eye = lax.broadcasted_iota(jnp.int32, (lane, lane), 0) == lax.broadcasted_iota(jnp.int32, (lane, lane), 1)
        for k in range(rows // lane):
            here = pl.ds(k * lane, lane)
            line = jnp.broadcast_to(summed[k : k + 1], (lane, lane))
            scalar = jnp.sum(jnp.where(eye, line, 0.0), axis=1, keepdims=True)
            inv = inv_ref[here]
            block[here] = (
                cot_ref[here].astype(F32)
                + inv * total[here]
                - x_ref[here].astype(F32) * (inv * inv * scalar / (width * 2 * RING))
            ).astype(BF16)
        remote(block, arrived, relay, other_section()).wait_send()

    @pl.when(section_is(0))
    def _():
        mine = Pool(send, recv)
        mine.count = 1
        pltpu.make_async_remote_copy(
            src_ref=block, dst_ref=arrived, send_sem=relay[0], recv_sem=relay[1],
            device_id=other_section(), device_id_type=MESH,
        ).wait_recv()
        rows = Gather(dp, arrived, all_ref, mine, True)
        rows.start()
        rows.middle()
        rows.finish()


REACH = 128


def lanes_at(first):
    return pl.ds(pl.multiple_of(first, 128), 128)


def shifted(shifts, ref, start, rows, lanes):
    for r in range(8):
        for a in range(0, rows, 64):
            count = min(64, rows - a)
            shifts[r, a : a + count] = ref[start + r + a : start + r + a + count, lanes]


def fir(shifts, kern, lanes, out, out_lanes, tiles, block, backwards):
    @pl.loop(0, tiles // block)
    def _(b):
        first = pl.multiple_of(b * block * 8, 8)

        def step(r, totals):
            totals = list(totals)
            taps = []
            for q in range(REACH // 8):
                u = 8 * q + r
                taps.append(kern[pl.ds(REACH - 1 - u if backwards else u, 8, stride=0), lanes])
            for i in range(block + REACH // 8 - 1):
                x = shifts[r, pl.ds(first + 8 * i, 8)]
                for o in range(block):
                    if 0 <= i - o < REACH // 8:
                        totals[o] = totals[o] + taps[i - o] * x
            return tuple(totals)

        totals = lax.fori_loop(0, 8, step, tuple(jnp.zeros((8, 128), F32) for _ in range(block)))
        for o in range(block):
            out[pl.ds(first + 8 * o, 8), out_lanes] = totals[o]


def lags(shifts, ref, lanes, out, out_lanes, tiles):
    for r in range(8):

        def step(b, totals):
            totals = list(totals)
            first = pl.multiple_of(b * 32, 8)
            own = [ref[pl.ds(first + 8 * o, 8), lanes] for o in range(4)]
            for i in range(4 + REACH // 8 - 1):
                x = shifts[r, pl.ds(first + 8 * i, 8)]
                for o in range(4):
                    if 0 <= i - o < REACH // 8:
                        totals[i - o] = totals[i - o] + own[o] * x
            return tuple(totals)

        totals = lax.fori_loop(0, tiles // 4, step, tuple(jnp.zeros((8, 128), F32) for _ in range(REACH // 8)))
        for q in range(REACH // 8):
            row = REACH - 1 - (8 * q + r)
            out[row : row + 1, out_lanes] = jnp.sum(totals[q], axis=0, keepdims=True)


def chunks(first, last, size):
    for a in range(first, last, size):
        yield a, min(size, last - a)


def short_rows(ref, taps, m, a, count, lanes, tap_lanes):
    total = taps[m : m + 1, tap_lanes] * ref[a : a + count, lanes]
    for j in (1, 2):
        total = total + taps[3 * j + m : 3 * j + m + 1, tap_lanes] * ref[a - j : a - j + count, lanes]
    return total


ALL = slice(0, 128)


def stream(m):
    return slice(m * 128, (m + 1) * 128)


def mix_first(proj, taps, kern, filtered, prod, shifts, gated, part):
    for a, count in chunks(8, BACK + part, 64):
        prod[a : a + count] = short_rows(proj, taps, 1, a, count, stream(1), ALL) * short_rows(
            proj, taps, 2, a, count, stream(2), ALL
        )
    for a, count in chunks(BACK + part, BACK + AHEAD, 64):
        prod[a : a + count] = short_rows(proj, taps, 1, a, count, stream(1), ALL) * short_rows(
            proj, taps, 2, a, count, stream(2), ALL
        )
    shifted(shifts, prod, BACK - REACH + 1, KEPT + REACH, ALL)
    fir(shifts, kern, ALL, filtered, ALL, KEPT // 8, 10, True)
    for a, count in chunks(0, part, 64):
        query = short_rows(proj, taps, 0, BACK + a, count, stream(0), ALL)
        gated[a : a + count] = (query * filtered[a : a + count]).astype(BF16)


def mix_back(gg, proj, taps, kern, filtered, gf, gprod, gs, shifts, gp, part):
    for a, count in chunks(0, AHEAD, 64):
        gf[a : a + count] = gg[a : a + count] * short_rows(proj, taps, 0, BACK + a, count, stream(0), ALL)
    shifted(shifts, gf, 0, KEPT + REACH, ALL)
    fir(shifts, kern, ALL, gprod, ALL, KEPT // 8, 10, False)
    for a, count in chunks(0, KEPT, 64):
        here = slice(a, a + count)
        gs[0, here] = gg[here] * filtered[here]
        gs[1, here] = gprod[here] * short_rows(proj, taps, 2, BACK + a, count, stream(2), ALL)
        gs[2, here] = gprod[here] * short_rows(proj, taps, 1, BACK + a, count, stream(1), ALL)
    for m in range(3):
        for a, count in chunks(0, part, 64):
            total = taps[m : m + 1] * gs[m, a : a + count]
            for j in (1, 2):
                total = total + taps[3 * j + m : 3 * j + m + 1] * gs[m, a + j : a + j + count]
            gp[a : a + count, stream(m)] = total.astype(BF16)


def mix_sums(gf, proj, taps, gs, prod, shifts, out, part):
    for a, count in chunks(8, BACK + part + 8, 64):
        prod[a : a + count] = short_rows(proj, taps, 1, a, count, stream(1), ALL) * short_rows(
            proj, taps, 2, a, count, stream(2), ALL
        )
    shifted(shifts, prod, BACK - REACH + 1, part + REACH, ALL)
    lags(shifts, gf, ALL, out, ALL, part // 8)
    out[REACH:] = jnp.zeros((16, 128), F32)
    for m in range(3):
        for j in range(3):
            total = jnp.zeros((8, 128), F32)
            for a, count in chunks(0, part, 64):
                term = gs[m, a : a + count] * proj[BACK - j + a : BACK - j + a + count, stream(m)]
                total = total + jnp.sum(term.reshape(count // 8, 8, 128), axis=0)
            row = REACH + 3 * j + m
            out[row : row + 1] = jnp.sum(total, axis=0, keepdims=True)


def second_kernel(proj, taps, kern, part_ref, all_ref, gg_ref, filtered, prod, shifts, gated, *rest):
    bufs, (send, recv) = rest[:-2], rest[-2:]
    barrier = pltpu.get_barrier_semaphore()
    ctx = Group("ctx")
    greet(ctx.neighbours(), barrier)
    pl.semaphore_wait(barrier, 3)
    part = gated.shape[0]

    @pl.when(section_is(0))
    def _():
        mix_first(proj, taps, kern, filtered, prod, shifts, gated, part)
        job = Gather(ctx, gated, all_ref, Pool(send, recv), False)
        job.block = lambda ring, pair: all_ref.at[
            pl.ds(pl.multiple_of(pair * part, part), part), lanes_at(ring * 128)
        ]
        job.half = part // 2
        job.part = lambda ring, pair, second: all_ref.at[
            pl.ds(pl.multiple_of(pair * part + second * job.half, job.half), job.half), lanes_at(ring * 128)
        ]
        job.start()
        job.middle()
        job.finish()

    @pl.when(section_is(1))
    def _():
        PairThenRing(ctx, part_ref, Pool(send, recv), bufs).run(gg_ref)


def last_kernel(
    gg, proj, taps, kern, filtered, looked, gtab_all, taps_all,
    gf, gprod, gs, prod, shifts, gp, gtab, sums, got, block, send, recv,
):
    barrier = pltpu.get_barrier_semaphore()
    ctx = Group("ctx")
    greet(ctx.neighbours(), barrier)
    pl.semaphore_wait(barrier, 3)

    @pl.when(section_is(0))
    def _():
        pool = Pool(send, recv)
        sem = pool.take(1)[0]
        hold = got.shape[0]
        part = gp.shape[0]
        mix_back(gg, proj, taps, kern, filtered, gf, gprod, gs, shifts, gp, part)

        @pl.loop(0, 4)
        def _(k):
            here = pl.ds(pl.multiple_of(k * 128, 128), 128)
            gtab[here] = jnp.dot(looked[here], gp[...], preferred_element_type=F32).astype(BF16)

        halves = lambda p: gtab.at[pl.ds(pl.multiple_of(p * hold, hold), hold)]
        copy = remote(halves(ctx.mate), got, sem, ctx.at(ctx.ring, ctx.mate))
        copy.wait()
        add_into(block, [halves(ctx.pair), got])
        table = Gather(ctx, block, gtab_all, pool, False)
        table.start()
        mix_sums(gf, proj, taps, gs, prod, shifts, sums, part)
        job = Gather(ctx, sums, taps_all, pool, False)
        job.start()
        table.middle()
        job.middle()
        table.finish()
        job.finish()


def middle_kernel(
    proj, gg, taps, kern, gp_out, gated_out, stat_out, sums_out, gf, prod,
    kg, pp, query, filtered, gprod, gs, shifts, ptail, qtail, ghead, gfar, sfar, gfpad, row_sum, qsend, gsend, send, recv,
):
    n = 2 * RING
    me = lax.axis_index("ctx")
    after, before = {"ctx": (me + 1) % n}, {"ctx": (me + n - 1) % n}
    barrier = pltpu.get_barrier_semaphore()
    greet([after, before], barrier)
    pl.semaphore_wait(barrier, 2)
    rows, width = gg.shape

    @pl.when(section_is(1))
    def _():
        pool = Pool(send, recv)
        sems = pool.take(4)
        first = (me > 0).astype(F32)
        final = (me < n - 1).astype(F32)
        a_copy = remote(proj.at[pl.ds(rows - 8, 8)], ptail, sems[0], after)
        for a, count in chunks(0, rows, 32):
            pp[8 + a : 8 + a + count] = proj[a : a + count]

        def products(a, count, group):
            tl = lanes_at(group * 128)
            k = short_rows(pp, taps, 1, a, count, lanes_at(width + group * 128), tl)
            v = short_rows(pp, taps, 2, a, count, lanes_at(2 * width + group * 128), tl)
            return k * v

        @pl.loop(0, 4)
        def _(group):
            tl = lanes_at(group * 128)
            for a, count in chunks(rows // 2, rows, 64):
                value = products(8 + a, count, group)
                prod[REACH + a : REACH + a + count, tl] = value
                qsend[a - rows // 2 : a - rows // 2 + count, tl] = value.astype(BF16)

        b_copy = remote(qsend, qtail, sems[1], after)
        a_copy.wait_recv()
        pp[0:8] = jnp.where(me > 0, ptail[...], 0.0)

        @pl.loop(0, 4)
        def _(group):
            tl = lanes_at(group * 128)
            for a, count in chunks(0, rows, 64):
                value = short_rows(pp, taps, 0, 8 + a, count, tl, tl)
                query[a : a + count, tl] = value
                value = value * gg[a : a + count, tl]
                gf[a : a + count, tl] = value
                gfpad[a : a + count, tl] = value
                if a < REACH:
                    ghead[a : a + count, tl] = value.astype(BF16)
            for a, count in chunks(0, rows // 2, 64):
                prod[REACH + a : REACH + a + count, tl] = products(8 + a, count, group)

        c_copy = remote(ghead, gfar, sems[2], before)
        b_copy.wait_recv()
        for a, count in chunks(0, REACH, 32):
            prod[a : a + count] = jnp.where(me > 0, qtail[a : a + count].astype(F32), 0.0)

        @pl.loop(0, 4)
        def _(group):
            tl = lanes_at(group * 128)
            shifted(shifts, prod, 1, rows + REACH - 8, tl)
            kg[...] = kern[:, tl]
            fir(shifts, kg, ALL, filtered, tl, rows // 8, 8, True)
            for a, count in chunks(0, rows, 64):
                gated_out[a : a + count, tl] = (query[a : a + count, tl] * filtered[a : a + count, tl]).astype(BF16)

        c_copy.wait_recv()
        for a, count in chunks(0, REACH, 32):
            gfpad[rows + a : rows + a + count] = jnp.where(me < n - 1, gfar[a : a + count].astype(F32), 0.0)

        @pl.loop(0, 4)
        def _(group):
            tl = lanes_at(group * 128)
            shifted(shifts, gfpad, 0, rows + REACH - 8, tl)
            kg[...] = kern[:, tl]
            fir(shifts, kg, ALL, gprod, tl, rows // 8, 8, False)
            for a, count in chunks(0, rows, 64):
                here = slice(a, a + count)
                gs[here, tl] = gg[here, tl] * filtered[here, tl]
                k = short_rows(pp, taps, 1, 8 + a, count, lanes_at(width + group * 128), tl)
                v = short_rows(pp, taps, 2, 8 + a, count, lanes_at(2 * width + group * 128), tl)
                gs[here, lanes_at(width + group * 128)] = gprod[here, tl] * v
                gs[here, lanes_at(2 * width + group * 128)] = gprod[here, tl] * k

        for m in range(3):
            gsend[:, m * width : (m + 1) * width] = gs[0:8, m * width : (m + 1) * width]
        d_copy = remote(gsend, sfar, sems[3], before)
        d_copy.wait_recv()
        gs[rows : rows + 8] = jnp.where(me < n - 1, sfar[...], 0.0)
        row_sum[...] = jnp.zeros_like(row_sum)

        @pl.loop(0, 4)
        def _(group):
            tl = lanes_at(group * 128)
            for m in range(3):
                ml = lanes_at(m * width + group * 128)
                sums = [jnp.zeros((8, 128), F32) for _ in range(3)]
                for a, count in chunks(0, rows, 64):
                    total = taps[m : m + 1, tl] * gs[a : a + count, ml]
                    for j in (1, 2):
                        total = total + taps[3 * j + m : 3 * j + m + 1, tl] * gs[a + j : a + j + count, ml]
                    gp_out[a : a + count, ml] = total.astype(BF16)
                    row_sum[a : a + count] += total * pp[8 + a : 8 + a + count, ml]
                    for j in range(3):
                        term = gs[a : a + count, ml] * pp[8 - j + a : 8 - j + a + count, ml]
                        sums[j] = sums[j] + jnp.sum(term.reshape(count // 8, 8, 128), axis=0)
                for j in range(3):
                    sums_out[3 * j + m : 3 * j + m + 1, tl] = jnp.sum(sums[j], axis=0, keepdims=True)

        eye = lax.broadcasted_iota(jnp.int32, (128, 128), 0) == lax.broadcasted_iota(jnp.int32, (128, 128), 1)
        stat_out[...] = jnp.zeros_like(stat_out)
        for k in range(rows // 128):
            column = jnp.sum(row_sum[k * 128 : (k + 1) * 128], axis=1, keepdims=True)
            line = jnp.sum(jnp.where(eye, jnp.broadcast_to(column, (128, 128)), 0.0), axis=0, keepdims=True)
            stat_out[k : k + 1] = line
        for copy in (a_copy, b_copy, c_copy, d_copy):
            copy.wait_send()


def late_kernel(
    part_ref, gp_ref, gated_ref, normed_ref, gf, prod, sums_ref,
    gg_ref, gp_all, gated_all, normed_all, taps_all, shifts, taps_own, *rest,
):
    bufs, (send, recv) = rest[:-2], rest[-2:]
    barrier = pltpu.get_barrier_semaphore()
    ctx = Group("ctx")
    me = lax.axis_index("ctx")
    everyone = [{"ctx": (me + k) % (2 * RING)} for k in range(1, 2 * RING)]
    greet(everyone, barrier)
    pl.semaphore_wait(barrier, 2 * RING - 1)

    @pl.when(section_is(0))
    def _():
        PairThenRing(ctx, part_ref, Pool(send, recv), bufs).run(gg_ref)

    @pl.when(section_is(1))
    def _():
        pool = Pool(send, recv)
        jobs = [
            Gather(ctx, gp_ref, gp_all, pool, False),
            Gather(ctx, gated_ref, gated_all, pool, False),
        ]
        for job in jobs:
            job.start()
        sems = pool.take(8)
        width = normed_all.shape[2]
        columns = lambda k: pl.ds(pl.multiple_of(k * width, width), width)
        own = pltpu.make_async_copy(normed_ref.at[:, columns(me)], normed_all.at[me], sems[7][0])
        own.start()
        sends = []
        for k, device in enumerate(everyone):
            target = (me + k + 1) % (2 * RING)
            sends.append(remote(normed_ref.at[:, columns(target)], normed_all.at[me], sems[k], device))

        @pl.loop(0, 4)
        def _(group):
            tl = lanes_at(group * 128)
            shifted(shifts, prod, 1, gf.shape[0] + REACH - 8, tl)
            lags(shifts, gf, tl, taps_own, tl, gf.shape[0] // 8)

        taps_own[REACH:] = sums_ref[...]
        jobs.append(Gather(ctx, taps_own, taps_all, pool, False))
        jobs[-1].start()
        for job in jobs:
            job.middle()
        for job in jobs:
            job.finish()
        own.wait()
        for copy in sends:
            copy.wait()


def dot(a, b, dims=(((1,), (0,)), ((), ()))):
    return lax.dot_general(a, b, dims, preferred_element_type=F32)


TRANS_B = (((1,), (1,)), ((), ()))
TRANS_A = (((0,), (0,)), ((), ()))


def onehot(ids, count):
    return (ids[:, None] == jnp.arange(count, dtype=jnp.int32)[None, :]).astype(BF16)


def local(
    token_ids, embedding, project_in, short_taps, filter_taps, decay_rates, project_out, cotangent
):
    section_zero = lax.axis_index("section") == 0
    n = lax.axis_size("ctx")
    vocab = embedding.shape[0]
    rows = token_ids.shape[0]
    seq = rows * n
    part = seq // 2
    width = embedding.shape[1]
    chans = project_in.shape[3]
    lane = chans // RING
    taps_all = short_taps[0]
    filter_all = filter_taps[0]
    tap_count = filter_all.shape[0]
    place = lax.axis_index("ctx")
    core, strip = place % 2, place // 2
    base = core * part

    w_flat = project_in[0].reshape(width, 3 * chans)
    w_out = project_out[0]
    positions = jnp.arange(tap_count).astype(F32)
    damping_all = jnp.exp(-decay_rates[0][None, :] * positions[:, None] / tap_count)
    kernel_all = filter_all * damping_all

    own_tokens = jnp.tile(token_ids.reshape(rows // lane, lane), (16 * lane // rows, 1))
    emb, table, inv_table, tokens, w_full, e1 = call(
        begin_kernel,
        1,
        [
            ((vocab, width), BF16),
            ((vocab, 3 * lane), BF16),
            ((vocab, lane), F32),
            ((n, 16, lane), jnp.int32),
            ((n, width, 3 * chans), BF16),
            ((n, rows, width), BF16),
        ],
        [
            pltpu.VMEM((n, vocab // 2, 4 * lane), BF16),
            pltpu.VMEM((rows, width), BF16),
            pltpu.VMEM((vocab // 2, 4 * lane), F32),
        ]
        + PairThenRing.scratch(vocab // 2, 4 * lane),
        32,
        embedding, w_flat, w_flat, cotangent, own_tokens,
        in_specs=[VMEM, VMEM, ANY, VMEM, VMEM],
        out_specs=[VMEM, VMEM, VMEM, VMEM, ANY, VMEM],
        name="begin",
    )
    tokens = tokens[:, : rows // lane].reshape(seq)
    w_full = w_full.reshape(n * width, 3 * chans)

    def strip_of(a):
        return lax.dynamic_slice_in_dim(a, strip * lane, lane, a.ndim - 1)

    taps0, kernel0 = strip_of(taps_all), strip_of(kernel_all)
    at = BACK - 2

    taps0 = taps0.reshape(9, lane)
    taps1 = taps_all.reshape(9, chans)
    rows_id = jnp.arange(vocab, dtype=jnp.int32)

    def own_block0():
        padded = jnp.concatenate(
            [jnp.full((BACK,), -1, jnp.int32), tokens, jnp.full((AHEAD - part,), -1, jnp.int32)]
        )
        seen = lax.dynamic_slice_in_dim(padded, base, BACK + AHEAD, 0)
        proj = dot(onehot(seen, vocab), table)
        mine = lax.dynamic_slice_in_dim(tokens, lax.axis_index("dp") * rows, rows, 0)
        first = dot(onehot(mine, vocab), emb).astype(BF16)
        looked = (rows_id[:, None] == lax.dynamic_slice_in_dim(tokens, base, part, 0)[None, :]).astype(BF16)
        return proj, first, looked, e1

    def own_block1():
        shapes = jax.eval_shape(own_block0)
        blank = jax.tree.map(lambda s: jnp.zeros(s.shape, s.dtype), shapes[:-1])
        grad_part = dot(e1.reshape(seq, width), w_out, TRANS_B).astype(BF16)
        return *blank, grad_part.reshape(n, rows, chans)

    proj0, first, looked, gg1_part = lax.cond(section_zero, own_block0, own_block1)
    gated0_all, gg1, filtered0 = call(
        second_kernel,
        2,
        [((seq, chans), BF16), ((rows, chans), F32), ((KEPT, lane), F32)],
        [
            pltpu.VMEM((BACK + AHEAD, lane), F32),
            pltpu.VMEM((8, KEPT + REACH, lane), F32),
            pltpu.VMEM((part, lane), BF16),
        ]
        + PairThenRing.scratch(rows, chans),
        16,
        proj0, taps0, kernel0, gg1_part,
        name="second",
    )
    out_part = dot(gated0_all, w_out).astype(BF16)
    rows_all, arrived = call(
        forth_kernel,
        3,
        [((n, rows, width), BF16), ((rows, width), BF16)],
        [pltpu.VMEM((rows, width), F32), pltpu.VMEM((rows, width), BF16)]
        + RingThenPair.scratch(rows, width),
        24,
        out_part.reshape(n, rows, width), first,
        name="forth",
    )

    rows_all = jnp.transpose(rows_all, (1, 0, 2)).reshape(rows, n * width)
    rows_float = rows_all.astype(F32)
    inv_rms = lax.rsqrt(jnp.mean(rows_float * rows_float, axis=1, keepdims=True) + EPSILON)
    normed = (rows_float * inv_rms).astype(BF16)
    proj1 = dot(normed, w_full)
    gp1, gated1, stat, sums1, gf1, prod1 = call(
        middle_kernel,
        7,
        [
            ((rows, 3 * chans), BF16),
            ((rows, chans), BF16),
            ((16, lane), F32),
            ((16, chans), F32),
            ((rows, chans), F32),
            ((rows + REACH, chans), F32),
        ],
        [
            pltpu.VMEM((REACH, 128), F32),
            pltpu.VMEM((rows + 8, 3 * chans), F32),
            pltpu.VMEM((rows, chans), F32),
            pltpu.VMEM((rows, chans), F32),
            pltpu.VMEM((rows, chans), F32),
            pltpu.VMEM((rows + 8, 3 * chans), F32),
            pltpu.VMEM((8, rows + REACH, 128), F32),
            pltpu.VMEM((8, 3 * chans), F32),
            pltpu.VMEM((REACH, chans), BF16),
            pltpu.VMEM((REACH, chans), BF16),
            pltpu.VMEM((REACH, chans), BF16),
            pltpu.VMEM((8, 3 * chans), F32),
            pltpu.VMEM((rows + REACH, chans), F32),
            pltpu.VMEM((rows, 128), F32),
            pltpu.VMEM((REACH, chans), BF16),
            pltpu.VMEM((8, 3 * chans), F32),
        ],
        4,
        proj1, gg1, taps1, kernel_all,
        name="middle",
    )
    back_part = dot(gp1, w_full, TRANS_B).astype(BF16)
    back_part = jnp.transpose(back_part.reshape(rows, n, width), (1, 0, 2))
    (e0,) = call(
        back_kernel,
        4,
        [((n, rows, width), BF16)],
        [
            pltpu.VMEM((n, 16, lane), F32),
            pltpu.VMEM((rows, width), BF16),
            pltpu.VMEM((rows, width), F32),
            pltpu.VMEM((rows, width), BF16),
        ]
        + RingThenPair.scratch(rows, width),
        32,
        back_part, stat, inv_rms, cotangent, arrived,
        name="back",
    )
    e0_all = e0.reshape(seq, width)

    gg0_part = dot(e0_all, w_out, TRANS_B).astype(BF16)
    gg0_part = jnp.concatenate([gg0_part, jnp.zeros((AHEAD - part, chans), BF16)], axis=0)
    blocks = jnp.stack(
        [
            gg0_part[c * part : c * part + AHEAD, s * lane : (s + 1) * lane]
            for s in range(RING)
            for c in range(2)
        ]
    )
    gg0, gp1_all, gated1_all, normed1, taps1_all = call(
        late_kernel,
        5,
        [
            ((AHEAD, lane), F32),
            ((n, rows, 3 * chans), BF16),
            ((n, rows, chans), BF16),
            ((n, rows, width), BF16),
            ((n, 144, chans), F32),
        ],
        [pltpu.VMEM((8, rows + REACH, 128), F32), pltpu.VMEM((144, chans), F32)]
        + PairThenRing.scratch(AHEAD, lane),
        40,
        blocks, gp1, gated1, normed, gf1, prod1, sums1,
        in_specs=[VMEM, ANY, ANY, ANY, VMEM, VMEM, VMEM],
        out_specs=[VMEM, ANY, ANY, ANY, VMEM],
        name="late",
    )
    gtab, sums0 = call(
        last_kernel,
        6,
        [((n, vocab // 2, 3 * lane), BF16), ((n, 144, lane), F32)],
        [
            pltpu.VMEM((AHEAD, lane), F32),
            pltpu.VMEM((KEPT, lane), F32),
            pltpu.VMEM((3, KEPT, lane), F32),
            pltpu.VMEM((BACK + AHEAD, lane), F32),
            pltpu.VMEM((8, KEPT + REACH, lane), F32),
            pltpu.VMEM((part, 3 * lane), BF16),
            pltpu.VMEM((vocab, 3 * lane), BF16),
            pltpu.VMEM((144, lane), F32),
            pltpu.VMEM((vocab // 2, 3 * lane), BF16),
            pltpu.VMEM((vocab // 2, 3 * lane), BF16),
        ],
        24,
        gg0, proj0, taps0, kernel0, filtered0, looked,
        name="last",
    )

    def end0():
        table_rows = jnp.transpose(gtab.reshape(RING, 2, vocab // 2, 3, lane), (1, 2, 3, 0, 4))
        normed_table = (emb.astype(F32) * inv_table[:, :1]).astype(BF16)
        sums = sums0.reshape(RING, 2, 144, lane).sum(axis=1)
        return (
            dot(normed_table, table_rows.reshape(vocab, 3 * chans), TRANS_A),
            dot(gated0_all, e0_all, TRANS_A),
            jnp.transpose(sums, (1, 0, 2)).reshape(144, chans),
        )

    def end1():
        return (
            dot(normed1.reshape(seq, width), gp1_all.reshape(seq, 3 * chans), TRANS_A),
            dot(gated1_all.reshape(seq, chans), e1.reshape(seq, width), TRANS_A),
            taps1_all.sum(axis=0),
        )

    grad_in, grad_out, sums = lax.cond(section_zero, end0, end1)
    grad_in = grad_in.reshape(width, 3, chans)
    gk, gt = sums[:tap_count], sums[tap_count : tap_count + 9].reshape(3, 3, chans)
    grad_filter = gk * damping_all
    grad_decay = -jnp.sum(gk * kernel_all * positions[:, None], axis=0) / tap_count
    return (grad_in[None], grad_out[None], grad_filter[None], grad_decay[None], gt[None])


def solution(mesh):
    return jax.shard_map(
        local,
        mesh=mesh,
        in_specs=(
            P("ctx"),
            P(None, "dp"),
            P("section", "ctx", None, "dp"),
            P("section", None, None, "dp"),
            P("section", None, "dp"),
            P("section", "dp"),
            P("section", "dp", "ctx"),
            P("ctx", "dp"),
        ),
        out_specs=(
            P("section", "ctx", None, "dp"),
            P("section", "dp", "ctx"),
            P("section", None, "dp"),
            P("section", "dp"),
            P("section", None, None, "dp"),
        ),
        check_vma=False,
    )
```

```python
import functools

import jax
import jax.numpy as jnp
from jax import lax
from jax.experimental import pallas as pl
from jax.experimental.pallas import tpu as pltpu
from jax.sharding import PartitionSpec as P

EPSILON = 1e-06
F32 = jnp.float32
BF16 = jnp.bfloat16
MESH = pl.DeviceIdType.MESH
BACK = 136
AHEAD = 1184
KEPT = 1040
RING = 4


class Group:
    def __init__(self, axis):
        self.axis = axis
        me = lax.axis_index(axis)
        if axis == "ctx":
            self.ring, self.pair = me // 2, me % 2
        else:
            self.ring, self.pair = me % RING, me // RING
        self.right = (self.ring + 1) % RING
        self.left = (self.ring + RING - 1) % RING
        self.across = (self.ring + 2) % RING
        self.mate = 1 - self.pair

    def slot(self, ring, pair):
        return ring * 2 + pair if self.axis == "ctx" else pair * RING + ring

    def at(self, ring, pair):
        return {self.axis: self.slot(ring, pair)}

    def neighbours(self):
        return [
            self.at(self.right, self.pair),
            self.at(self.left, self.pair),
            self.at(self.ring, self.mate),
        ]


class Pool:
    def __init__(self, send, recv):
        self.send, self.recv, self.count = send, recv, 0

    def take(self, k):
        first = self.count
        self.count += k
        return [(self.send.at[first + i], self.recv.at[first + i]) for i in range(k)]


def remote(src, dst, sems, device):
    copy = pltpu.make_async_remote_copy(
        src_ref=src,
        dst_ref=dst,
        send_sem=sems[0],
        recv_sem=sems[1],
        device_id=device,
        device_id_type=MESH,
    )
    copy.start()
    return copy


def greet(devices, barrier):
    for device in devices:
        pl.semaphore_signal(barrier, inc=1, device_id=device, device_id_type=MESH)


class Gather:
    def __init__(self, group, src, out, pool, pair_first):
        self.g, self.src, self.out, self.pair_first = group, src, out, pair_first
        self.sems = pool.take(9)
        self.own = pool.take(1)[0]
        self.half = out.shape[1] // 2

    def block(self, ring, pair):
        return self.out.at[self.g.slot(ring, pair)]

    def part(self, ring, pair, second):
        return self.out.at[self.g.slot(ring, pair), pl.ds(self.half * second, self.half)]

    def start(self):
        g, s = self.g, self.sems
        mine = self.block(g.ring, g.pair)
        right, left, mate = g.neighbours()
        self.local = pltpu.make_async_copy(self.src, mine, self.own[0])
        self.local.start()
        first = remote(self.src, mine, s[0], mate)
        self.copies = [first, remote(self.src, mine, s[1], right), remote(self.src, mine, s[2], left)]

    def turn(self, pair, a, b, c, d):
        g, s = self.g, self.sems
        right, left, mate = g.neighbours()
        more = []
        a.wait_recv()
        part = self.part(g.left, pair, 0)
        more.append(remote(part, part, s[c], right))
        if not self.pair_first:
            block = self.block(g.left, pair)
            more.append(remote(block, block, s[5], mate))
        b.wait_recv()
        part = self.part(g.right, pair, 1)
        more.append(remote(part, part, s[d], left))
        if not self.pair_first:
            block = self.block(g.right, pair)
            more.append(remote(block, block, s[6], mate))
        return more

    def middle(self):
        g, s = self.g, self.sems
        right, left, mate = g.neighbours()
        mate_copy, to_right, to_left = self.copies
        rest = self.turn(g.pair, to_right, to_left, 3, 4)
        self.sent = list(self.copies) + rest
        if self.pair_first:
            self.late = list(rest)
            mate_copy.wait_recv()
            block = self.block(g.ring, g.mate)
            a = remote(block, block, s[5], right)
            b = remote(block, block, s[6], left)
            more = self.turn(g.mate, a, b, 7, 8)
            self.sent += [a, b] + more
            self.late += more
        else:
            rest[0].wait_recv()
            rest[2].wait_recv()
            block = self.block(g.across, g.pair)
            last = remote(block, block, s[7], mate)
            self.sent.append(last)
            self.late = [mate_copy, rest[1], rest[3], last]

    def finish(self):
        for copy in self.late:
            copy.wait_recv()
        for copy in self.sent:
            copy.wait_send()
        self.local.wait()


def add_into(out, terms, rows=64):
    @pl.loop(0, out.shape[0] // rows)
    def _(step):
        here = pl.ds(pl.multiple_of(step * rows, rows), rows)
        total = terms[0][here].astype(F32)
        for term in terms[1:]:
            total = total + term[here].astype(F32)
        out[here] = total.astype(out.dtype)


def rows_step(count):
    for rows in (64, 48, 37 * 16, 32, 16):
        if count % rows == 0:
            return rows if rows != 37 * 16 else 16
    return 16


class Around:
    def __init__(self, group, pool, bufs):
        self.g = group
        self.s = pool.take(6)
        self.rel, self.merged, self.came = bufs
        self.half = self.rel.shape[1]

    @staticmethod
    def scratch(rows, lanes):
        half = rows // 2
        return [
            pltpu.VMEM((2, half, lanes), BF16),
            pltpu.VMEM((2, half, lanes), BF16),
            pltpu.VMEM((2, 2, half, lanes), BF16),
        ]

    def halves(self, ref):
        return ref.at[pl.ds(0, self.half)], ref.at[pl.ds(self.half, self.half)]

    def send_across(self, block):
        right, left, _ = self.g.neighbours()
        a, b = self.halves(block)
        self.copies = [remote(a, self.rel.at[0], self.s[0], right), remote(b, self.rel.at[1], self.s[1], left)]

    def send_near(self, to_right, to_left):
        right, left, _ = self.g.neighbours()
        self.to_right, self.to_left = to_right, to_left
        b = self.halves(to_right)[1]
        a = self.halves(to_left)[0]
        self.copies += [
            remote(b, self.came.at[0, 1], self.s[2], right),
            remote(a, self.came.at[1, 0], self.s[3], left),
        ]

    def merge(self):
        right, left, _ = self.g.neighbours()
        step = rows_step(self.half)
        self.copies[0].wait_recv()
        add_into(self.merged.at[0], [self.halves(self.to_right)[0], self.rel.at[0]], step)
        self.copies.append(remote(self.merged.at[0], self.came.at[0, 0], self.s[4], right))
        self.copies[1].wait_recv()
        add_into(self.merged.at[1], [self.halves(self.to_left)[1], self.rel.at[1]], step)
        self.copies.append(remote(self.merged.at[1], self.came.at[1, 1], self.s[5], left))

    def collect(self, out, own):
        step = rows_step(self.half)
        for copy in self.copies[2:]:
            copy.wait_recv()
        for h in range(2):
            piece = pl.ds(h * self.half, self.half)
            add_into(
                out.at[piece],
                [ref.at[piece] for ref in own] + [self.came.at[0, h], self.came.at[1, h]],
                step,
            )

    def finish(self):
        for copy in self.copies:
            copy.wait_send()


class PairThenRing:
    def __init__(self, group, inp, pool, bufs):
        self.g, self.inp = group, inp
        self.got, self.sums = bufs[:2]
        self.ring = Around(group, pool, bufs[2:])
        self.s = pool.take(4)

    @staticmethod
    def scratch(rows, lanes):
        return [pltpu.VMEM((4, rows, lanes), BF16), pltpu.VMEM((4, rows, lanes), BF16)] + Around.scratch(rows, lanes)

    def run(self, out):
        g = self.g
        mate = g.at(g.ring, g.mate)
        order = [g.across, g.right, g.left, g.ring]
        copies = [
            remote(self.inp.at[g.slot(r, g.mate)], self.got.at[k], self.s[k], mate) for k, r in enumerate(order)
        ]
        step = rows_step(self.inp.shape[1])

        def pair_sum(k):
            copies[k].wait_recv()
            add_into(self.sums.at[k], [self.inp.at[g.slot(order[k], g.pair)], self.got.at[k]], step)

        pair_sum(0)
        self.ring.send_across(self.sums.at[0])
        pair_sum(1)
        pair_sum(2)
        self.ring.send_near(self.sums.at[1], self.sums.at[2])
        copies[3].wait_recv()
        self.ring.merge()
        self.ring.collect(out, [self.inp.at[g.slot(g.ring, g.pair)], self.got.at[3]])
        self.ring.finish()
        for copy in copies:
            copy.wait_send()


class RingThenPair:
    def __init__(self, group, inp, pool, bufs):
        self.g, self.inp = group, inp
        self.far, self.got = bufs[:2]
        self.rings = [Around(group, pool, bufs[2:5]), Around(group, pool, bufs[5:8])]
        self.s = pool.take(1)[0]

    @staticmethod
    def scratch(rows, lanes):
        return (
            [pltpu.VMEM((rows, lanes), BF16), pltpu.VMEM((rows, lanes), BF16)]
            + Around.scratch(rows, lanes)
            + Around.scratch(rows, lanes)
        )

    def run(self, out, extra=()):
        g = self.g
        pairs = [g.mate, g.pair]
        blocks = lambda ring, pair: self.inp.at[g.slot(ring, pair)]
        for ring, pair in zip(self.rings, pairs):
            ring.send_across(blocks(g.across, pair))
            ring.send_near(blocks(g.right, pair), blocks(g.left, pair))
        self.rings[0].merge()
        self.rings[1].merge()
        self.rings[0].collect(self.far, [blocks(g.ring, g.mate)])
        copy = remote(self.far, self.got, self.s, g.at(g.ring, g.mate))
        self.rings[1].collect(out, [blocks(g.ring, g.pair)])
        copy.wait_recv()
        add_into(out, [out, self.got] + list(extra), rows_step(out.shape[0]))
        copy.wait_send()
        for ring in self.rings:
            ring.finish()


ANY = pl.BlockSpec(memory_space=pl.ANY)
VMEM = pl.BlockSpec(memory_space=pltpu.VMEM)


def call(body, ident, outs, scratch, sems, *args, in_specs=None, out_specs=None, name=None):
    return pl.pallas_call(
        body,
        out_shape=[jax.ShapeDtypeStruct(shape, dtype) for shape, dtype in outs],
        in_specs=in_specs or [VMEM] * len(args),
        out_specs=out_specs or [VMEM] * len(outs),
        scratch_shapes=list(scratch)
        + [pltpu.SemaphoreType.DMA((sems,)), pltpu.SemaphoreType.DMA((sems,))],
        compiler_params=pltpu.CompilerParams(
            collective_id=ident, has_side_effects=True, vmem_limit_bytes=60 * 1024 * 1024
        ),
        name=name,
    )(*args)


def section_is(k):
    return lax.axis_index("section") == k


def crossing():
    i, j = lax.axis_index("dp"), lax.axis_index("ctx")
    return {"dp": j, "ctx": i}, i != j


def other_section():
    i, j = lax.axis_index("dp"), lax.axis_index("ctx")
    return {"section": 1 - lax.axis_index("section"), "dp": j, "ctx": i}


def begin_kernel(
    emb_ref, w_ref, w_far, cot_ref, tok_ref,
    emb_out, table_out, inv_out, tok_out, w_out, e1_out,
    parts, crossed, half_out, piece, *rest,
):
    bufs, (send, recv) = rest[:-2], rest[-2:]
    barrier = pltpu.get_barrier_semaphore()
    ctx, dp = Group("ctx"), Group("dp")
    partner, apart = crossing()
    n = 2 * RING
    me = lax.axis_index("dp")
    others = [{"dp": (me + k) % n} for k in range(1, n)]
    greet(ctx.neighbours() + others, barrier)

    @pl.when(apart)
    def _():
        greet([partner], barrier)

    pl.semaphore_wait(barrier, n + 2 + jnp.where(apart, 1, 0))
    lane = 128
    strips = RING
    pool = Pool(send, recv)
    cross_sem = pool.take(1)[0]
    same_sem = pool.take(1)[0]
    pair_sems = pool.take(2)

    @pl.when(section_is(0))
    def _():
        mine = Pool(send, recv)
        mine.count = pool.count
        tokens = Gather(ctx, tok_ref, tok_out, mine, False)
        tokens.start()
        spread = mine.take(n - 1)
        share = piece.shape[0]
        share_of = lambda k: emb_ref.at[pl.ds(pl.multiple_of(k * share, share), share)]
        keep = pltpu.make_async_copy(share_of(me), piece, same_sem[0])
        copies = [
            pltpu.make_async_remote_copy(
                src_ref=share_of((me + k + 1) % n), dst_ref=piece, send_sem=spread[k][0],
                recv_sem=cross_sem[1], device_id=device, device_id_type=MESH,
            )
            for k, device in enumerate(others)
        ]

        @pl.when(jnp.logical_not(apart))
        def _():
            for copy in copies:
                copy.start()
            keep.start()
            keep.wait()

        @pl.when(apart)
        def _():
            copies[0].wait_recv()

        table_rows = Gather(dp, piece, emb_out, mine, True)
        table_rows.start()
        tokens.middle()
        table_rows.middle()
        table_rows.finish()

        @pl.when(jnp.logical_not(apart))
        def _():
            for copy in copies:
                copy.wait_send()

        vocab, width = emb_ref.shape
        hold = vocab // 2
        for core in range(2):
            values = emb_out[core * RING : (core + 1) * RING].reshape(hold, width).astype(F32)
            square = jnp.broadcast_to(jnp.sum(values * values, axis=1, keepdims=True), (hold, lane)).astype(BF16)
            for strip in range(strips):
                parts[strip * 2 + core, :, 3 * lane :] = square

        @pl.loop(0, 3 * strips)
        def _(k):
            strip, m = k // 3, k % 3
            columns = pl.ds(pl.multiple_of(m * strips * lane + strip * lane, lane), lane)
            product = jnp.dot(emb_out[...].reshape(vocab, width), w_ref[:, columns], preferred_element_type=F32).astype(BF16)
            to = pl.ds(pl.multiple_of(m * lane, lane), lane)
            parts[strip * 2, :, to] = product[:hold]
            parts[strip * 2 + 1, :, to] = product[hold:]

        PairThenRing(ctx, parts, mine, bufs).run(half_out)
        here = pl.ds(pl.multiple_of(ctx.pair * hold, hold), hold)
        total = half_out[...]
        inv = lax.rsqrt(total[:, 3 * lane :] / (width * 2 * RING) + EPSILON)
        inv_out[here] = inv
        for m in range(3):
            table_out[here, m * lane : (m + 1) * lane] = (total[:, m * lane : (m + 1) * lane] * inv).astype(BF16)
        mate = ctx.at(ctx.ring, ctx.mate)
        a = remote(inv_out.at[here], inv_out.at[here], pair_sems[0], mate)
        b = remote(table_out.at[here], table_out.at[here], pair_sems[1], mate)
        tokens.finish()
        a.wait()
        b.wait()

    @pl.when(section_is(1))
    def _():
        mine = Pool(send, recv)
        mine.count = pool.count
        weights = Gather(ctx, w_far, w_out, mine, False)
        weights.start()
        there = pltpu.make_async_remote_copy(
            src_ref=cot_ref, dst_ref=crossed, send_sem=cross_sem[0], recv_sem=cross_sem[1],
            device_id=partner, device_id_type=MESH,
        )
        here = pltpu.make_async_copy(cot_ref, crossed, same_sem[0])
        pl.when(apart)(there.start)
        pl.when(jnp.logical_not(apart))(here.start)
        weights.middle()
        pl.when(apart)(there.wait)
        pl.when(jnp.logical_not(apart))(here.wait)
        cots = Gather(dp, crossed, e1_out, mine, True)
        cots.start()
        cots.middle()
        cots.finish()
        weights.finish()


def relay_barrier():
    barrier = pltpu.get_barrier_semaphore()
    dp = Group("dp")
    greet(dp.neighbours() + [other_section()], barrier)
    pl.semaphore_wait(barrier, 4)
    return dp


def reduce_kernel(part_ref, first_ref, out_ref, total, *rest):
    bufs, (send, recv) = rest[:-2], rest[-2:]
    barrier = pltpu.get_barrier_semaphore()
    dp = Group("dp")

    @pl.when(section_is(0))
    def _():
        greet(dp.neighbours(), barrier)
        pl.semaphore_wait(barrier, 3)
        RingThenPair(dp, part_ref, Pool(send, recv), bufs).run(total, [first_ref])
        out_ref[...] = total[...].astype(BF16)


def forth_kernel(block, all_ref, arrived_ref, send, recv):
    dp = relay_barrier()
    pool = Pool(send, recv)
    relay = pool.take(1)[0]
    copy = pltpu.make_async_remote_copy(
        src_ref=block, dst_ref=arrived_ref, send_sem=relay[0], recv_sem=relay[1],
        device_id=other_section(), device_id_type=MESH,
    )

    @pl.when(section_is(0))
    def _():
        copy.start()
        copy.wait_send()

    @pl.when(section_is(1))
    def _():
        copy.wait_recv()
        rows = Gather(dp, arrived_ref, all_ref, pool, True)
        rows.start()
        rows.middle()
        rows.finish()


def back_kernel(
    part_ref, stat_ref, inv_ref, cot_ref, x_ref, all_ref, stats, arrived, total, block, *rest
):
    bufs, (send, recv) = rest[:-2], rest[-2:]
    dp = relay_barrier()
    pool = Pool(send, recv)
    relay = pool.take(1)[0]

    @pl.when(section_is(1))
    def _():
        stat = Gather(dp, stat_ref, stats, pool, True)
        stat.start()
        stat.middle()
        RingThenPair(dp, part_ref, pool, bufs).run(total)
        stat.finish()
        rows, width = total.shape
        lane = 128
        summed = stats[0]
        for k in range(1, 8):
            summed = summed + stats[k]
        eye = lax.broadcasted_iota(jnp.int32, (lane, lane), 0) == lax.broadcasted_iota(jnp.int32, (lane, lane), 1)
        for k in range(rows // lane):
            here = pl.ds(k * lane, lane)
            line = jnp.broadcast_to(summed[k : k + 1], (lane, lane))
            scalar = jnp.sum(jnp.where(eye, line, 0.0), axis=1, keepdims=True)
            inv = inv_ref[here]
            block[here] = (
                cot_ref[here].astype(F32)
                + inv * total[here]
                - x_ref[here].astype(F32) * (inv * inv * scalar / (width * 2 * RING))
            ).astype(BF16)
        remote(block, arrived, relay, other_section()).wait_send()

    @pl.when(section_is(0))
    def _():
        mine = Pool(send, recv)
        mine.count = 1
        pltpu.make_async_remote_copy(
            src_ref=block, dst_ref=arrived, send_sem=relay[0], recv_sem=relay[1],
            device_id=other_section(), device_id_type=MESH,
        ).wait_recv()
        rows = Gather(dp, arrived, all_ref, mine, True)
        rows.start()
        rows.middle()
        rows.finish()


REACH = 128


def lanes_at(first):
    return pl.ds(pl.multiple_of(first, 128), 128)


def shifted(shifts, ref, start, rows, lanes):
    for r in range(8):
        for a in range(0, rows, 64):
            count = min(64, rows - a)
            shifts[r, a : a + count] = ref[start + r + a : start + r + a + count, lanes]


def fir(shifts, kern, lanes, out, out_lanes, tiles, block, backwards):
    @pl.loop(0, tiles // block)
    def _(b):
        first = pl.multiple_of(b * block * 8, 8)

        def step(r, totals):
            totals = list(totals)
            taps = []
            for q in range(REACH // 8):
                u = 8 * q + r
                taps.append(kern[pl.ds(REACH - 1 - u if backwards else u, 8, stride=0), lanes])
            for i in range(block + REACH // 8 - 1):
                x = shifts[r, pl.ds(first + 8 * i, 8)]
                for o in range(block):
                    if 0 <= i - o < REACH // 8:
                        totals[o] = totals[o] + taps[i - o] * x
            return tuple(totals)

        totals = lax.fori_loop(0, 8, step, tuple(jnp.zeros((8, 128), F32) for _ in range(block)))
        for o in range(block):
            out[pl.ds(first + 8 * o, 8), out_lanes] = totals[o]


def lags(shifts, ref, lanes, out, out_lanes, tiles):
    for r in range(8):

        def step(b, totals):
            totals = list(totals)
            first = pl.multiple_of(b * 32, 8)
            own = [ref[pl.ds(first + 8 * o, 8), lanes] for o in range(4)]
            for i in range(4 + REACH // 8 - 1):
                x = shifts[r, pl.ds(first + 8 * i, 8)]
                for o in range(4):
                    if 0 <= i - o < REACH // 8:
                        totals[i - o] = totals[i - o] + own[o] * x
            return tuple(totals)

        totals = lax.fori_loop(0, tiles // 4, step, tuple(jnp.zeros((8, 128), F32) for _ in range(REACH // 8)))
        for q in range(REACH // 8):
            row = REACH - 1 - (8 * q + r)
            out[row : row + 1, out_lanes] = jnp.sum(totals[q], axis=0, keepdims=True)


def chunks(first, last, size):
    for a in range(first, last, size):
        yield a, min(size, last - a)


def short_rows(ref, taps, m, a, count, lanes, tap_lanes):
    total = taps[m : m + 1, tap_lanes] * ref[a : a + count, lanes]
    for j in (1, 2):
        total = total + taps[3 * j + m : 3 * j + m + 1, tap_lanes] * ref[a - j : a - j + count, lanes]
    return total


ALL = slice(0, 128)


def stream(m):
    return slice(m * 128, (m + 1) * 128)


def mix_first(proj, taps, kern, filtered, prod, shifts, gated, part):
    for a, count in chunks(8, BACK + part, 64):
        prod[a : a + count] = short_rows(proj, taps, 1, a, count, stream(1), ALL) * short_rows(
            proj, taps, 2, a, count, stream(2), ALL
        )
    for a, count in chunks(BACK + part, BACK + AHEAD, 64):
        prod[a : a + count] = short_rows(proj, taps, 1, a, count, stream(1), ALL) * short_rows(
            proj, taps, 2, a, count, stream(2), ALL
        )
    shifted(shifts, prod, BACK - REACH + 1, KEPT + REACH, ALL)
    fir(shifts, kern, ALL, filtered, ALL, KEPT // 8, 10, True)
    for a, count in chunks(0, part, 64):
        query = short_rows(proj, taps, 0, BACK + a, count, stream(0), ALL)
        gated[a : a + count] = (query * filtered[a : a + count]).astype(BF16)


def mix_back(gg, proj, taps, kern, filtered, gf, gprod, gs, shifts, gp, part):
    for a, count in chunks(0, AHEAD, 64):
        gf[a : a + count] = gg[a : a + count] * short_rows(proj, taps, 0, BACK + a, count, stream(0), ALL)
    shifted(shifts, gf, 0, KEPT + REACH, ALL)
    fir(shifts, kern, ALL, gprod, ALL, KEPT // 8, 10, False)
    for a, count in chunks(0, KEPT, 64):
        here = slice(a, a + count)
        gs[0, here] = gg[here] * filtered[here]
        gs[1, here] = gprod[here] * short_rows(proj, taps, 2, BACK + a, count, stream(2), ALL)
        gs[2, here] = gprod[here] * short_rows(proj, taps, 1, BACK + a, count, stream(1), ALL)
    for m in range(3):
        for a, count in chunks(0, part, 64):
            total = taps[m : m + 1] * gs[m, a : a + count]
            for j in (1, 2):
                total = total + taps[3 * j + m : 3 * j + m + 1] * gs[m, a + j : a + j + count]
            gp[a : a + count, stream(m)] = total.astype(BF16)


def mix_sums(gf, proj, taps, gs, prod, shifts, out, part):
    for a, count in chunks(8, BACK + part + 8, 64):
        prod[a : a + count] = short_rows(proj, taps, 1, a, count, stream(1), ALL) * short_rows(
            proj, taps, 2, a, count, stream(2), ALL
        )
    shifted(shifts, prod, BACK - REACH + 1, part + REACH, ALL)
    lags(shifts, gf, ALL, out, ALL, part // 8)
    out[REACH:] = jnp.zeros((16, 128), F32)
    for m in range(3):
        for j in range(3):
            total = jnp.zeros((8, 128), F32)
            for a, count in chunks(0, part, 64):
                term = gs[m, a : a + count] * proj[BACK - j + a : BACK - j + a + count, stream(m)]
                total = total + jnp.sum(term.reshape(count // 8, 8, 128), axis=0)
            row = REACH + 3 * j + m
            out[row : row + 1] = jnp.sum(total, axis=0, keepdims=True)


def second_kernel(proj, taps, kern, part_ref, all_ref, gg_ref, filtered, prod, shifts, gated, *rest):
    bufs, (send, recv) = rest[:-2], rest[-2:]
    barrier = pltpu.get_barrier_semaphore()
    ctx = Group("ctx")
    greet(ctx.neighbours(), barrier)
    pl.semaphore_wait(barrier, 3)
    part = gated.shape[0]

    @pl.when(section_is(0))
    def _():
        mix_first(proj, taps, kern, filtered, prod, shifts, gated, part)
        job = Gather(ctx, gated, all_ref, Pool(send, recv), False)
        job.block = lambda ring, pair: all_ref.at[
            pl.ds(pl.multiple_of(pair * part, part), part), lanes_at(ring * 128)
        ]
        job.half = part // 2
        job.part = lambda ring, pair, second: all_ref.at[
            pl.ds(pl.multiple_of(pair * part + second * job.half, job.half), job.half), lanes_at(ring * 128)
        ]
        job.start()
        job.middle()
        job.finish()

    @pl.when(section_is(1))
    def _():
        PairThenRing(ctx, part_ref, Pool(send, recv), bufs).run(gg_ref)


def last_kernel(
    gg, proj, taps, kern, filtered, looked, gtab_all, taps_all,
    gf, gprod, gs, prod, shifts, gp, gtab, sums, got, block, send, recv,
):
    barrier = pltpu.get_barrier_semaphore()
    ctx = Group("ctx")
    greet(ctx.neighbours(), barrier)
    pl.semaphore_wait(barrier, 3)

    @pl.when(section_is(0))
    def _():
        pool = Pool(send, recv)
        sem = pool.take(1)[0]
        hold = got.shape[0]
        part = gp.shape[0]
        mix_back(gg, proj, taps, kern, filtered, gf, gprod, gs, shifts, gp, part)

        @pl.loop(0, 4)
        def _(k):
            here = pl.ds(pl.multiple_of(k * 128, 128), 128)
            gtab[here] = jnp.dot(looked[here], gp[...], preferred_element_type=F32).astype(BF16)

        halves = lambda p: gtab.at[pl.ds(pl.multiple_of(p * hold, hold), hold)]
        copy = remote(halves(ctx.mate), got, sem, ctx.at(ctx.ring, ctx.mate))
        copy.wait()
        add_into(block, [halves(ctx.pair), got])
        table = Gather(ctx, block, gtab_all, pool, False)
        table.start()
        mix_sums(gf, proj, taps, gs, prod, shifts, sums, part)
        job = Gather(ctx, sums, taps_all, pool, False)
        job.start()
        table.middle()
        job.middle()
        table.finish()
        job.finish()


def middle_kernel(
    proj, gg, taps, kern, gp_out, gated_out, stat_out, sums_out, gf, prod,
    kg, pp, query, filtered, gprod, gs, shifts, ptail, qtail, ghead, gfar, sfar, gfpad, row_sum, qsend, gsend, send, recv,
):
    n = 2 * RING
    me = lax.axis_index("ctx")
    after, before = {"ctx": (me + 1) % n}, {"ctx": (me + n - 1) % n}
    barrier = pltpu.get_barrier_semaphore()
    greet([after, before], barrier)
    pl.semaphore_wait(barrier, 2)
    rows, width = gg.shape

    @pl.when(section_is(1))
    def _():
        pool = Pool(send, recv)
        sems = pool.take(4)
        first = (me > 0).astype(F32)
        final = (me < n - 1).astype(F32)
        a_copy = remote(proj.at[pl.ds(rows - 8, 8)], ptail, sems[0], after)
        for a, count in chunks(0, rows, 32):
            pp[8 + a : 8 + a + count] = proj[a : a + count]

        def products(a, count, group):
            tl = lanes_at(group * 128)
            k = short_rows(pp, taps, 1, a, count, lanes_at(width + group * 128), tl)
            v = short_rows(pp, taps, 2, a, count, lanes_at(2 * width + group * 128), tl)
            return k * v

        @pl.loop(0, 4)
        def _(group):
            tl = lanes_at(group * 128)
            for a, count in chunks(rows // 2, rows, 64):
                value = products(8 + a, count, group)
                prod[REACH + a : REACH + a + count, tl] = value
                qsend[a - rows // 2 : a - rows // 2 + count, tl] = value.astype(BF16)

        b_copy = remote(qsend, qtail, sems[1], after)
        a_copy.wait_recv()
        pp[0:8] = jnp.where(me > 0, ptail[...], 0.0)

        @pl.loop(0, 4)
        def _(group):
            tl = lanes_at(group * 128)
            for a, count in chunks(0, rows, 64):
                value = short_rows(pp, taps, 0, 8 + a, count, tl, tl)
                query[a : a + count, tl] = value
                value = value * gg[a : a + count, tl]
                gf[a : a + count, tl] = value
                gfpad[a : a + count, tl] = value
                if a < REACH:
                    ghead[a : a + count, tl] = value.astype(BF16)
            for a, count in chunks(0, rows // 2, 64):
                prod[REACH + a : REACH + a + count, tl] = products(8 + a, count, group)

        c_copy = remote(ghead, gfar, sems[2], before)
        b_copy.wait_recv()
        for a, count in chunks(0, REACH, 32):
            prod[a : a + count] = jnp.where(me > 0, qtail[a : a + count].astype(F32), 0.0)

        @pl.loop(0, 4)
        def _(group):
            tl = lanes_at(group * 128)
            shifted(shifts, prod, 1, rows + REACH - 8, tl)
            kg[...] = kern[:, tl]
            fir(shifts, kg, ALL, filtered, tl, rows // 8, 8, True)
            for a, count in chunks(0, rows, 64):
                gated_out[a : a + count, tl] = (query[a : a + count, tl] * filtered[a : a + count, tl]).astype(BF16)

        c_copy.wait_recv()
        for a, count in chunks(0, REACH, 32):
            gfpad[rows + a : rows + a + count] = jnp.where(me < n - 1, gfar[a : a + count].astype(F32), 0.0)

        @pl.loop(0, 4)
        def _(group):
            tl = lanes_at(group * 128)
            shifted(shifts, gfpad, 0, rows + REACH - 8, tl)
            kg[...] = kern[:, tl]
            fir(shifts, kg, ALL, gprod, tl, rows // 8, 8, False)
            for a, count in chunks(0, rows, 64):
                here = slice(a, a + count)
                gs[here, tl] = gg[here, tl] * filtered[here, tl]
                k = short_rows(pp, taps, 1, 8 + a, count, lanes_at(width + group * 128), tl)
                v = short_rows(pp, taps, 2, 8 + a, count, lanes_at(2 * width + group * 128), tl)
                gs[here, lanes_at(width + group * 128)] = gprod[here, tl] * v
                gs[here, lanes_at(2 * width + group * 128)] = gprod[here, tl] * k

        for m in range(3):
            gsend[:, m * width : (m + 1) * width] = gs[0:8, m * width : (m + 1) * width]
        d_copy = remote(gsend, sfar, sems[3], before)
        d_copy.wait_recv()
        gs[rows : rows + 8] = jnp.where(me < n - 1, sfar[...], 0.0)
        row_sum[...] = jnp.zeros_like(row_sum)

        @pl.loop(0, 4)
        def _(group):
            tl = lanes_at(group * 128)
            for m in range(3):
                ml = lanes_at(m * width + group * 128)
                sums = [jnp.zeros((8, 128), F32) for _ in range(3)]
                for a, count in chunks(0, rows, 64):
                    total = taps[m : m + 1, tl] * gs[a : a + count, ml]
                    for j in (1, 2):
                        total = total + taps[3 * j + m : 3 * j + m + 1, tl] * gs[a + j : a + j + count, ml]
                    gp_out[a : a + count, ml] = total.astype(BF16)
                    row_sum[a : a + count] += total * pp[8 + a : 8 + a + count, ml]
                    for j in range(3):
                        term = gs[a : a + count, ml] * pp[8 - j + a : 8 - j + a + count, ml]
                        sums[j] = sums[j] + jnp.sum(term.reshape(count // 8, 8, 128), axis=0)
                for j in range(3):
                    sums_out[3 * j + m : 3 * j + m + 1, tl] = jnp.sum(sums[j], axis=0, keepdims=True)

        eye = lax.broadcasted_iota(jnp.int32, (128, 128), 0) == lax.broadcasted_iota(jnp.int32, (128, 128), 1)
        stat_out[...] = jnp.zeros_like(stat_out)
        for k in range(rows // 128):
            column = jnp.sum(row_sum[k * 128 : (k + 1) * 128], axis=1, keepdims=True)
            line = jnp.sum(jnp.where(eye, jnp.broadcast_to(column, (128, 128)), 0.0), axis=0, keepdims=True)
            stat_out[k : k + 1] = line
        for copy in (a_copy, b_copy, c_copy, d_copy):
            copy.wait_send()


def late_kernel(
    e0_ref, w_ref, gp_ref, gated_ref, normed_ref, gf, prod, sums_ref,
    gg_ref, gp_all, gated_all, normed_all, taps_all, shifts, taps_own, part_ref, *rest,
):
    bufs, (send, recv) = rest[:-2], rest[-2:]
    barrier = pltpu.get_barrier_semaphore()
    ctx = Group("ctx")
    me = lax.axis_index("ctx")
    everyone = [{"ctx": (me + k) % (2 * RING)} for k in range(1, 2 * RING)]
    greet(everyone, barrier)
    pl.semaphore_wait(barrier, 2 * RING - 1)

    @pl.when(section_is(0))
    def _():
        count, rows, _ = e0_ref.shape
        for k in range(count):
            product = dot(e0_ref[k], w_ref[...], TRANS_B).astype(BF16)
            core, first = divmod(k * rows, count // 2 * rows)
            for strip in range(RING):
                part = product[:, strip * 128 : (strip + 1) * 128]
                part_ref[strip * 2 + core, first : first + rows] = part
                if core == 1 and first == 0:
                    part_ref[strip * 2, count // 2 * rows : AHEAD] = part[: AHEAD - count // 2 * rows]
        over = AHEAD - count // 2 * rows
        for strip in range(RING):
            part_ref[strip * 2 + 1, count // 2 * rows : AHEAD] = jnp.zeros((over, 128), BF16)
        PairThenRing(ctx, part_ref, Pool(send, recv), bufs).run(gg_ref)

    @pl.when(section_is(1))
    def _():
        pool = Pool(send, recv)
        jobs = [
            Gather(ctx, gp_ref, gp_all, pool, False),
            Gather(ctx, gated_ref, gated_all, pool, False),
        ]
        for job in jobs:
            job.start()
        sems = pool.take(8)
        width = normed_all.shape[2]
        columns = lambda k: pl.ds(pl.multiple_of(k * width, width), width)
        own = pltpu.make_async_copy(normed_ref.at[:, columns(me)], normed_all.at[me], sems[7][0])
        own.start()
        sends = []
        for k, device in enumerate(everyone):
            target = (me + k + 1) % (2 * RING)
            sends.append(remote(normed_ref.at[:, columns(target)], normed_all.at[me], sems[k], device))

        @pl.loop(0, 4)
        def _(group):
            tl = lanes_at(group * 128)
            shifted(shifts, prod, 1, gf.shape[0] + REACH - 8, tl)
            lags(shifts, gf, tl, taps_own, tl, gf.shape[0] // 8)

        taps_own[REACH:] = sums_ref[...]
        jobs.append(Gather(ctx, taps_own, taps_all, pool, False))
        jobs[-1].start()
        for job in jobs:
            job.middle()
        for job in jobs:
            job.finish()
        own.wait()
        for copy in sends:
            copy.wait()


def dot(a, b, dims=(((1,), (0,)), ((), ()))):
    return lax.dot_general(a, b, dims, preferred_element_type=F32)


TRANS_B = (((1,), (1,)), ((), ()))
TRANS_A = (((0,), (0,)), ((), ()))


def onehot(ids, count):
    return (ids[:, None] == jnp.arange(count, dtype=jnp.int32)[None, :]).astype(BF16)


def local(
    token_ids, embedding, project_in, short_taps, filter_taps, decay_rates, project_out, cotangent
):
    section_zero = lax.axis_index("section") == 0
    n = lax.axis_size("ctx")
    vocab = embedding.shape[0]
    rows = token_ids.shape[0]
    seq = rows * n
    part = seq // 2
    width = embedding.shape[1]
    chans = project_in.shape[3]
    lane = chans // RING
    taps_all = short_taps[0]
    filter_all = filter_taps[0]
    tap_count = filter_all.shape[0]
    place = lax.axis_index("ctx")
    core, strip = place % 2, place // 2
    base = core * part

    w_flat = project_in[0].reshape(width, 3 * chans)
    w_out = project_out[0]
    positions = jnp.arange(tap_count).astype(F32)
    damping_all = jnp.exp(-decay_rates[0][None, :] * positions[:, None] / tap_count)
    kernel_all = filter_all * damping_all

    own_tokens = jnp.tile(token_ids.reshape(rows // lane, lane), (16 * lane // rows, 1))
    emb, table, inv_table, tokens, w_full, e1 = call(
        begin_kernel,
        1,
        [
            ((n, vocab // n, width), BF16),
            ((vocab, 3 * lane), BF16),
            ((vocab, lane), F32),
            ((n, 16, lane), jnp.int32),
            ((n, width, 3 * chans), BF16),
            ((n, rows, width), BF16),
        ],
        [
            pltpu.VMEM((n, vocab // 2, 4 * lane), BF16),
            pltpu.VMEM((rows, width), BF16),
            pltpu.VMEM((vocab // 2, 4 * lane), F32),
            pltpu.VMEM((vocab // n, width), BF16),
        ]
        + PairThenRing.scratch(vocab // 2, 4 * lane),
        48,
        embedding, w_flat, w_flat, cotangent, own_tokens,
        in_specs=[VMEM, VMEM, ANY, VMEM, VMEM],
        out_specs=[VMEM, VMEM, VMEM, VMEM, ANY, VMEM],
        name="begin",
    )
    tokens = tokens[:, : rows // lane].reshape(seq)
    w_full = w_full.reshape(n * width, 3 * chans)
    emb = emb.reshape(vocab, width)

    def strip_of(a):
        return lax.dynamic_slice_in_dim(a, strip * lane, lane, a.ndim - 1)

    taps0, kernel0 = strip_of(taps_all), strip_of(kernel_all)
    at = BACK - 2

    taps0 = taps0.reshape(9, lane)
    taps1 = taps_all.reshape(9, chans)
    rows_id = jnp.arange(vocab, dtype=jnp.int32)

    def own_block0():
        padded = jnp.concatenate(
            [jnp.full((BACK,), -1, jnp.int32), tokens, jnp.full((AHEAD - part,), -1, jnp.int32)]
        )
        seen = lax.dynamic_slice_in_dim(padded, base, BACK + AHEAD, 0)
        proj = dot(onehot(seen, vocab), table)
        mine = lax.dynamic_slice_in_dim(tokens, lax.axis_index("dp") * rows, rows, 0)
        first = dot(onehot(mine, vocab), emb).astype(BF16)
        looked = (rows_id[:, None] == lax.dynamic_slice_in_dim(tokens, base, part, 0)[None, :]).astype(BF16)
        return proj, first, looked, e1

    def own_block1():
        shapes = jax.eval_shape(own_block0)
        blank = jax.tree.map(lambda s: jnp.zeros(s.shape, s.dtype), shapes[:-1])
        grad_part = dot(e1.reshape(seq, width), w_out, TRANS_B).astype(BF16)
        return *blank, grad_part.reshape(n, rows, chans)

    proj0, first, looked, gg1_part = lax.cond(section_zero, own_block0, own_block1)
    gated0_all, gg1, filtered0 = call(
        second_kernel,
        2,
        [((seq, chans), BF16), ((rows, chans), F32), ((KEPT, lane), F32)],
        [
            pltpu.VMEM((BACK + AHEAD, lane), F32),
            pltpu.VMEM((8, KEPT + REACH, lane), F32),
            pltpu.VMEM((part, lane), BF16),
        ]
        + PairThenRing.scratch(rows, chans),
        16,
        proj0, taps0, kernel0, gg1_part,
        name="second",
    )
    out_part = dot(gated0_all, w_out).astype(BF16)
    (second,) = call(
        reduce_kernel,
        3,
        [((rows, width), BF16)],
        [pltpu.VMEM((rows, width), F32)] + RingThenPair.scratch(rows, width),
        24,
        out_part.reshape(n, rows, width), first,
        name="reduce",
    )
    rows_all, arrived = call(
        forth_kernel,
        8,
        [((n, rows, width), BF16), ((rows, width), BF16)],
        [],
        24,
        second,
        name="forth",
    )

    rows_all = jnp.transpose(rows_all, (1, 0, 2)).reshape(rows, n * width)
    rows_float = rows_all.astype(F32)
    inv_rms = lax.rsqrt(jnp.mean(rows_float * rows_float, axis=1, keepdims=True) + EPSILON)
    normed = (rows_float * inv_rms).astype(BF16)
    proj1 = dot(normed, w_full)
    gp1, gated1, stat, sums1, gf1, prod1 = call(
        middle_kernel,
        7,
        [
            ((rows, 3 * chans), BF16),
            ((rows, chans), BF16),
            ((16, lane), F32),
            ((16, chans), F32),
            ((rows, chans), F32),
            ((rows + REACH, chans), F32),
        ],
        [
            pltpu.VMEM((REACH, 128), F32),
            pltpu.VMEM((rows + 8, 3 * chans), F32),
            pltpu.VMEM((rows, chans), F32),
            pltpu.VMEM((rows, chans), F32),
            pltpu.VMEM((rows, chans), F32),
            pltpu.VMEM((rows + 8, 3 * chans), F32),
            pltpu.VMEM((8, rows + REACH, 128), F32),
            pltpu.VMEM((8, 3 * chans), F32),
            pltpu.VMEM((REACH, chans), BF16),
            pltpu.VMEM((REACH, chans), BF16),
            pltpu.VMEM((REACH, chans), BF16),
            pltpu.VMEM((8, 3 * chans), F32),
            pltpu.VMEM((rows + REACH, chans), F32),
            pltpu.VMEM((rows, 128), F32),
            pltpu.VMEM((REACH, chans), BF16),
            pltpu.VMEM((8, 3 * chans), F32),
        ],
        4,
        proj1, gg1, taps1, kernel_all,
        name="middle",
    )
    back_part = dot(gp1, w_full, TRANS_B).astype(BF16)
    back_part = jnp.transpose(back_part.reshape(rows, n, width), (1, 0, 2))
    (e0,) = call(
        back_kernel,
        4,
        [((n, rows, width), BF16)],
        [
            pltpu.VMEM((n, 16, lane), F32),
            pltpu.VMEM((rows, width), BF16),
            pltpu.VMEM((rows, width), F32),
            pltpu.VMEM((rows, width), BF16),
        ]
        + RingThenPair.scratch(rows, width),
        32,
        back_part, stat, inv_rms, cotangent, arrived,
        name="back",
    )
    e0_all = e0.reshape(seq, width)

    gg0, gp1_all, gated1_all, normed1, taps1_all = call(
        late_kernel,
        5,
        [
            ((AHEAD, lane), F32),
            ((n, rows, 3 * chans), BF16),
            ((n, rows, chans), BF16),
            ((n, rows, width), BF16),
            ((n, 144, chans), F32),
        ],
        [pltpu.VMEM((8, rows + REACH, 128), F32), pltpu.VMEM((144, chans), F32), pltpu.VMEM((n, AHEAD, lane), BF16)]
        + PairThenRing.scratch(AHEAD, lane),
        40,
        e0, w_out, gp1, gated1, normed, gf1, prod1, sums1,
        in_specs=[VMEM, VMEM, ANY, ANY, ANY, VMEM, VMEM, VMEM],
        out_specs=[VMEM, ANY, ANY, ANY, VMEM],
        name="late",
    )
    gtab, sums0 = call(
        last_kernel,
        6,
        [((n, vocab // 2, 3 * lane), BF16), ((n, 144, lane), F32)],
        [
            pltpu.VMEM((AHEAD, lane), F32),
            pltpu.VMEM((KEPT, lane), F32),
            pltpu.VMEM((3, KEPT, lane), F32),
            pltpu.VMEM((BACK + AHEAD, lane), F32),
            pltpu.VMEM((8, KEPT + REACH, lane), F32),
            pltpu.VMEM((part, 3 * lane), BF16),
            pltpu.VMEM((vocab, 3 * lane), BF16),
            pltpu.VMEM((144, lane), F32),
            pltpu.VMEM((vocab // 2, 3 * lane), BF16),
            pltpu.VMEM((vocab // 2, 3 * lane), BF16),
        ],
        24,
        gg0, proj0, taps0, kernel0, filtered0, looked,
        name="last",
    )

    def end0():
        table_rows = jnp.transpose(gtab.reshape(RING, 2, vocab // 2, 3, lane), (1, 2, 3, 0, 4))
        normed_table = (emb.astype(F32) * inv_table[:, :1]).astype(BF16)
        sums = sums0.reshape(RING, 2, 144, lane).sum(axis=1)
        return (
            dot(normed_table, table_rows.reshape(vocab, 3 * chans), TRANS_A),
            dot(gated0_all, e0_all, TRANS_A),
            jnp.transpose(sums, (1, 0, 2)).reshape(144, chans),
        )

    def end1():
        return (
            dot(normed1.reshape(seq, width), gp1_all.reshape(seq, 3 * chans), TRANS_A),
            dot(gated1_all.reshape(seq, chans), e1.reshape(seq, width), TRANS_A),
            taps1_all.sum(axis=0),
        )

    grad_in, grad_out, sums = lax.cond(section_zero, end0, end1)
    grad_in = grad_in.reshape(width, 3, chans)
    gk, gt = sums[:tap_count], sums[tap_count : tap_count + 9].reshape(3, 3, chans)
    grad_filter = gk * damping_all
    grad_decay = -jnp.sum(gk * kernel_all * positions[:, None], axis=0) / tap_count
    return (grad_in[None], grad_out[None], grad_filter[None], grad_decay[None], gt[None])


def solution(mesh):
    return jax.shard_map(
        local,
        mesh=mesh,
        in_specs=(
            P("ctx"),
            P(None, "dp"),
            P("section", "ctx", None, "dp"),
            P("section", None, None, "dp"),
            P("section", None, "dp"),
            P("section", "dp"),
            P("section", "dp", "ctx"),
            P("ctx", "dp"),
        ),
        out_specs=(
            P("section", "ctx", None, "dp"),
            P("section", "dp", "ctx"),
            P("section", None, "dp"),
            P("section", "dp"),
            P("section", None, None, "dp"),
        ),
        check_vma=False,
    )
```

```python
import functools

import jax
import jax.numpy as jnp
from jax import lax
from jax.experimental import pallas as pl
from jax.experimental.pallas import tpu as pltpu
from jax.sharding import PartitionSpec as P

EPSILON = 1e-06
F32 = jnp.float32
BF16 = jnp.bfloat16
MESH = pl.DeviceIdType.MESH
BACK = 136
AHEAD = 1184
KEPT = 1040
RING = 4


class Group:
    def __init__(self, axis):
        self.axis = axis
        me = lax.axis_index(axis)
        if axis == "ctx":
            self.ring, self.pair = me // 2, me % 2
        else:
            self.ring, self.pair = me % RING, me // RING
        self.right = (self.ring + 1) % RING
        self.left = (self.ring + RING - 1) % RING
        self.across = (self.ring + 2) % RING
        self.mate = 1 - self.pair

    def slot(self, ring, pair):
        return ring * 2 + pair if self.axis == "ctx" else pair * RING + ring

    def at(self, ring, pair):
        return {self.axis: self.slot(ring, pair)}

    def neighbours(self):
        return [
            self.at(self.right, self.pair),
            self.at(self.left, self.pair),
            self.at(self.ring, self.mate),
        ]


class Pool:
    def __init__(self, send, recv):
        self.send, self.recv, self.count = send, recv, 0

    def take(self, k):
        first = self.count
        self.count += k
        return [(self.send.at[first + i], self.recv.at[first + i]) for i in range(k)]


def remote(src, dst, sems, device):
    copy = pltpu.make_async_remote_copy(
        src_ref=src,
        dst_ref=dst,
        send_sem=sems[0],
        recv_sem=sems[1],
        device_id=device,
        device_id_type=MESH,
    )
    copy.start()
    return copy


def greet(devices, barrier):
    for device in devices:
        pl.semaphore_signal(barrier, inc=1, device_id=device, device_id_type=MESH)


class Gather:
    def __init__(self, group, src, out, pool, pair_first):
        self.g, self.src, self.out, self.pair_first = group, src, out, pair_first
        self.sems = pool.take(9)
        self.own = pool.take(1)[0]
        self.half = out.shape[1] // 2

    def block(self, ring, pair):
        return self.out.at[self.g.slot(ring, pair)]

    def part(self, ring, pair, second):
        return self.out.at[self.g.slot(ring, pair), pl.ds(self.half * second, self.half)]

    def start(self):
        g, s = self.g, self.sems
        mine = self.block(g.ring, g.pair)
        right, left, mate = g.neighbours()
        self.local = pltpu.make_async_copy(self.src, mine, self.own[0])
        self.local.start()
        first = remote(self.src, mine, s[0], mate)
        self.copies = [first, remote(self.src, mine, s[1], right), remote(self.src, mine, s[2], left)]

    def turn(self, pair, a, b, c, d):
        g, s = self.g, self.sems
        right, left, mate = g.neighbours()
        more = []
        a.wait_recv()
        part = self.part(g.left, pair, 0)
        more.append(remote(part, part, s[c], right))
        if not self.pair_first:
            block = self.block(g.left, pair)
            more.append(remote(block, block, s[5], mate))
        b.wait_recv()
        part = self.part(g.right, pair, 1)
        more.append(remote(part, part, s[d], left))
        if not self.pair_first:
            block = self.block(g.right, pair)
            more.append(remote(block, block, s[6], mate))
        return more

    def middle(self):
        g, s = self.g, self.sems
        right, left, mate = g.neighbours()
        mate_copy, to_right, to_left = self.copies
        rest = self.turn(g.pair, to_right, to_left, 3, 4)
        self.sent = list(self.copies) + rest
        if self.pair_first:
            self.late = list(rest)
            mate_copy.wait_recv()
            block = self.block(g.ring, g.mate)
            a = remote(block, block, s[5], right)
            b = remote(block, block, s[6], left)
            more = self.turn(g.mate, a, b, 7, 8)
            self.sent += [a, b] + more
            self.late += more
        else:
            rest[0].wait_recv()
            rest[2].wait_recv()
            block = self.block(g.across, g.pair)
            last = remote(block, block, s[7], mate)
            self.sent.append(last)
            self.late = [mate_copy, rest[1], rest[3], last]

    def finish(self):
        for copy in self.late:
            copy.wait_recv()
        for copy in self.sent:
            copy.wait_send()
        self.local.wait()


def add_into(out, terms, rows=64):
    @pl.loop(0, out.shape[0] // rows)
    def _(step):
        here = pl.ds(pl.multiple_of(step * rows, rows), rows)
        total = terms[0][here].astype(F32)
        for term in terms[1:]:
            total = total + term[here].astype(F32)
        out[here] = total.astype(out.dtype)


def rows_step(count):
    for rows in (64, 48, 37 * 16, 32, 16):
        if count % rows == 0:
            return rows if rows != 37 * 16 else 16
    return 16


class Around:
    def __init__(self, group, pool, bufs):
        self.g = group
        self.s = pool.take(6)
        self.rel, self.merged, self.came = bufs
        self.half = self.rel.shape[1]

    @staticmethod
    def scratch(rows, lanes):
        half = rows // 2
        return [
            pltpu.VMEM((2, half, lanes), BF16),
            pltpu.VMEM((2, half, lanes), BF16),
            pltpu.VMEM((2, 2, half, lanes), BF16),
        ]

    def halves(self, ref):
        return ref.at[pl.ds(0, self.half)], ref.at[pl.ds(self.half, self.half)]

    def send_across(self, block):
        right, left, _ = self.g.neighbours()
        a, b = self.halves(block)
        self.copies = [remote(a, self.rel.at[0], self.s[0], right), remote(b, self.rel.at[1], self.s[1], left)]

    def send_near(self, to_right, to_left):
        right, left, _ = self.g.neighbours()
        self.to_right, self.to_left = to_right, to_left
        b = self.halves(to_right)[1]
        a = self.halves(to_left)[0]
        self.copies += [
            remote(b, self.came.at[0, 1], self.s[2], right),
            remote(a, self.came.at[1, 0], self.s[3], left),
        ]

    def merge(self):
        right, left, _ = self.g.neighbours()
        step = rows_step(self.half)
        self.copies[0].wait_recv()
        add_into(self.merged.at[0], [self.halves(self.to_right)[0], self.rel.at[0]], step)
        self.copies.append(remote(self.merged.at[0], self.came.at[0, 0], self.s[4], right))
        self.copies[1].wait_recv()
        add_into(self.merged.at[1], [self.halves(self.to_left)[1], self.rel.at[1]], step)
        self.copies.append(remote(self.merged.at[1], self.came.at[1, 1], self.s[5], left))

    def collect(self, out, own):
        step = rows_step(self.half)
        for copy in self.copies[2:]:
            copy.wait_recv()
        for h in range(2):
            piece = pl.ds(h * self.half, self.half)
            add_into(
                out.at[piece],
                [ref.at[piece] for ref in own] + [self.came.at[0, h], self.came.at[1, h]],
                step,
            )

    def finish(self):
        for copy in self.copies:
            copy.wait_send()


class PairThenRing:
    def __init__(self, group, inp, pool, bufs):
        self.g, self.inp = group, inp
        self.got, self.sums = bufs[:2]
        self.ring = Around(group, pool, bufs[2:])
        self.s = pool.take(4)

    @staticmethod
    def scratch(rows, lanes):
        return [pltpu.VMEM((4, rows, lanes), BF16), pltpu.VMEM((4, rows, lanes), BF16)] + Around.scratch(rows, lanes)

    def run(self, out):
        g = self.g
        mate = g.at(g.ring, g.mate)
        order = [g.across, g.right, g.left, g.ring]
        copies = [
            remote(self.inp.at[g.slot(r, g.mate)], self.got.at[k], self.s[k], mate) for k, r in enumerate(order)
        ]
        step = rows_step(self.inp.shape[1])

        def pair_sum(k):
            copies[k].wait_recv()
            add_into(self.sums.at[k], [self.inp.at[g.slot(order[k], g.pair)], self.got.at[k]], step)

        pair_sum(0)
        self.ring.send_across(self.sums.at[0])
        pair_sum(1)
        pair_sum(2)
        self.ring.send_near(self.sums.at[1], self.sums.at[2])
        copies[3].wait_recv()
        self.ring.merge()
        self.ring.collect(out, [self.inp.at[g.slot(g.ring, g.pair)], self.got.at[3]])
        self.ring.finish()
        for copy in copies:
            copy.wait_send()


class RingThenPair:
    def __init__(self, group, inp, pool, bufs):
        self.g, self.inp = group, inp
        self.far, self.got = bufs[:2]
        self.rings = [Around(group, pool, bufs[2:5]), Around(group, pool, bufs[5:8])]
        self.s = pool.take(1)[0]

    @staticmethod
    def scratch(rows, lanes):
        return (
            [pltpu.VMEM((rows, lanes), BF16), pltpu.VMEM((rows, lanes), BF16)]
            + Around.scratch(rows, lanes)
            + Around.scratch(rows, lanes)
        )

    def run(self, out, extra=(), produce=lambda slot: None):
        g = self.g
        pairs = [g.mate, g.pair]
        blocks = lambda ring, pair: self.inp.at[g.slot(ring, pair)]
        for ring, pair in zip(self.rings, pairs):
            produce(g.slot(g.across, pair))
            ring.send_across(blocks(g.across, pair))
            produce(g.slot(g.right, pair))
            produce(g.slot(g.left, pair))
            ring.send_near(blocks(g.right, pair), blocks(g.left, pair))
            produce(g.slot(g.ring, pair))
        self.rings[0].merge()
        self.rings[1].merge()
        self.rings[0].collect(self.far, [blocks(g.ring, g.mate)])
        copy = remote(self.far, self.got, self.s, g.at(g.ring, g.mate))
        self.rings[1].collect(out, [blocks(g.ring, g.pair)])
        copy.wait_recv()
        add_into(out, [out, self.got] + list(extra), rows_step(out.shape[0]))
        copy.wait_send()
        for ring in self.rings:
            ring.finish()


ANY = pl.BlockSpec(memory_space=pl.ANY)
VMEM = pl.BlockSpec(memory_space=pltpu.VMEM)


def call(body, ident, outs, scratch, sems, *args, in_specs=None, out_specs=None, name=None, local=0):
    return pl.pallas_call(
        body,
        out_shape=[jax.ShapeDtypeStruct(shape, dtype) for shape, dtype in outs],
        in_specs=in_specs or [VMEM] * len(args),
        out_specs=out_specs or [VMEM] * len(outs),
        scratch_shapes=list(scratch)
        + [pltpu.SemaphoreType.DMA((sems,)), pltpu.SemaphoreType.DMA((sems,))]
        + ([pltpu.SemaphoreType.DMA((local,))] if local else []),
        compiler_params=pltpu.CompilerParams(
            collective_id=ident, has_side_effects=True, vmem_limit_bytes=60 * 1024 * 1024
        ),
        name=name,
    )(*args)


def section_is(k):
    return lax.axis_index("section") == k


def crossing():
    i, j = lax.axis_index("dp"), lax.axis_index("ctx")
    return {"dp": j, "ctx": i}, i != j


def other_section():
    i, j = lax.axis_index("dp"), lax.axis_index("ctx")
    return {"section": 1 - lax.axis_index("section"), "dp": j, "ctx": i}


def begin_kernel(
    emb_ref, w_ref, w_far, cot_ref, tok_ref,
    emb_out, table_out, inv_out, tok_out, w_out, e1_out,
    parts, crossed, half_out, piece, *rest,
):
    bufs, (send, recv) = rest[:-2], rest[-2:]
    barrier = pltpu.get_barrier_semaphore()
    ctx, dp = Group("ctx"), Group("dp")
    partner, apart = crossing()
    n = 2 * RING
    me = lax.axis_index("dp")
    others = [{"dp": (me + k) % n} for k in range(1, n)]
    greet(ctx.neighbours() + others, barrier)

    @pl.when(apart)
    def _():
        greet([partner], barrier)

    pl.semaphore_wait(barrier, n + 2 + jnp.where(apart, 1, 0))
    lane = 128
    strips = RING
    pool = Pool(send, recv)
    cross_sem = pool.take(1)[0]
    same_sem = pool.take(1)[0]
    pair_sems = pool.take(2)

    @pl.when(section_is(0))
    def _():
        mine = Pool(send, recv)
        mine.count = pool.count
        tokens = Gather(ctx, tok_ref, tok_out, mine, False)
        tokens.start()
        spread = mine.take(n - 1)
        share = piece.shape[0]
        share_of = lambda k: emb_ref.at[pl.ds(pl.multiple_of(k * share, share), share)]
        keep = pltpu.make_async_copy(share_of(me), piece, same_sem[0])
        copies = [
            pltpu.make_async_remote_copy(
                src_ref=share_of((me + k + 1) % n), dst_ref=piece, send_sem=spread[k][0],
                recv_sem=cross_sem[1], device_id=device, device_id_type=MESH,
            )
            for k, device in enumerate(others)
        ]

        @pl.when(jnp.logical_not(apart))
        def _():
            for copy in copies:
                copy.start()
            keep.start()
            keep.wait()

        @pl.when(apart)
        def _():
            copies[0].wait_recv()

        table_rows = Gather(dp, piece, emb_out, mine, True)
        table_rows.start()
        tokens.middle()
        table_rows.middle()
        table_rows.finish()

        @pl.when(jnp.logical_not(apart))
        def _():
            for copy in copies:
                copy.wait_send()

        vocab, width = emb_ref.shape
        hold = vocab // 2
        for core in range(2):
            values = emb_out[core * RING : (core + 1) * RING].reshape(hold, width).astype(F32)
            square = jnp.broadcast_to(jnp.sum(values * values, axis=1, keepdims=True), (hold, lane)).astype(BF16)
            for strip in range(strips):
                parts[strip * 2 + core, :, 3 * lane :] = square

        @pl.loop(0, 3 * strips)
        def _(k):
            strip, m = k // 3, k % 3
            columns = pl.ds(pl.multiple_of(m * strips * lane + strip * lane, lane), lane)
            product = jnp.dot(emb_out[...].reshape(vocab, width), w_ref[:, columns], preferred_element_type=F32).astype(BF16)
            to = pl.ds(pl.multiple_of(m * lane, lane), lane)
            parts[strip * 2, :, to] = product[:hold]
            parts[strip * 2 + 1, :, to] = product[hold:]

        PairThenRing(ctx, parts, mine, bufs).run(half_out)
        here = pl.ds(pl.multiple_of(ctx.pair * hold, hold), hold)
        total = half_out[...]
        inv = lax.rsqrt(total[:, 3 * lane :] / (width * 2 * RING) + EPSILON)
        inv_out[here] = inv
        for m in range(3):
            table_out[here, m * lane : (m + 1) * lane] = (total[:, m * lane : (m + 1) * lane] * inv).astype(BF16)
        mate = ctx.at(ctx.ring, ctx.mate)
        a = remote(inv_out.at[here], inv_out.at[here], pair_sems[0], mate)
        b = remote(table_out.at[here], table_out.at[here], pair_sems[1], mate)
        tokens.finish()
        a.wait()
        b.wait()

    @pl.when(section_is(1))
    def _():
        mine = Pool(send, recv)
        mine.count = pool.count
        weights = Gather(ctx, w_far, w_out, mine, False)
        there = pltpu.make_async_remote_copy(
            src_ref=cot_ref, dst_ref=crossed, send_sem=cross_sem[0], recv_sem=cross_sem[1],
            device_id=partner, device_id_type=MESH,
        )
        here = pltpu.make_async_copy(cot_ref, crossed, same_sem[0])
        pl.when(apart)(there.start)
        pl.when(jnp.logical_not(apart))(here.start)
        pl.when(apart)(there.wait)
        pl.when(jnp.logical_not(apart))(here.wait)
        weights.start()
        cots = Gather(dp, crossed, e1_out, mine, True)
        cots.start()
        cots.middle()
        cots.finish()
        weights.middle()
        weights.finish()


def reduce_kernel(part_ref, first_ref, out_ref, total, *rest):
    bufs, (send, recv) = rest[:-2], rest[-2:]
    barrier = pltpu.get_barrier_semaphore()
    dp = Group("dp")

    @pl.when(section_is(0))
    def _():
        greet(dp.neighbours(), barrier)
        pl.semaphore_wait(barrier, 3)
        RingThenPair(dp, part_ref, Pool(send, recv), bufs).run(total, [first_ref])
        out_ref[...] = total[...].astype(BF16)


REACH = 128


def lanes_at(first):
    return pl.ds(pl.multiple_of(first, 128), 128)


def shifted(shifts, ref, start, rows, lanes):
    for r in range(8):
        for a in range(0, rows, 64):
            count = min(64, rows - a)
            shifts[r, a : a + count] = ref[start + r + a : start + r + a + count, lanes]


def fir(shifts, kern, lanes, out, out_lanes, tiles, block, backwards):
    @pl.loop(0, tiles // block)
    def _(b):
        first = pl.multiple_of(b * block * 8, 8)

        def step(r, totals):
            totals = list(totals)
            taps = []
            for q in range(REACH // 8):
                u = 8 * q + r
                taps.append(kern[pl.ds(REACH - 1 - u if backwards else u, 8, stride=0), lanes])
            for i in range(block + REACH // 8 - 1):
                x = shifts[r, pl.ds(first + 8 * i, 8)]
                for o in range(block):
                    if 0 <= i - o < REACH // 8:
                        totals[o] = totals[o] + taps[i - o] * x
            return tuple(totals)

        totals = lax.fori_loop(0, 8, step, tuple(jnp.zeros((8, 128), F32) for _ in range(block)))
        for o in range(block):
            out[pl.ds(first + 8 * o, 8), out_lanes] = totals[o]


def lags(shifts, ref, lanes, out, out_lanes, tiles):
    for r in range(8):

        def step(b, totals):
            totals = list(totals)
            first = pl.multiple_of(b * 32, 8)
            own = [ref[pl.ds(first + 8 * o, 8), lanes] for o in range(4)]
            for i in range(4 + REACH // 8 - 1):
                x = shifts[r, pl.ds(first + 8 * i, 8)]
                for o in range(4):
                    if 0 <= i - o < REACH // 8:
                        totals[i - o] = totals[i - o] + own[o] * x
            return tuple(totals)

        totals = lax.fori_loop(0, tiles // 4, step, tuple(jnp.zeros((8, 128), F32) for _ in range(REACH // 8)))
        for q in range(REACH // 8):
            row = REACH - 1 - (8 * q + r)
            out[row : row + 1, out_lanes] = jnp.sum(totals[q], axis=0, keepdims=True)


def chunks(first, last, size):
    for a in range(first, last, size):
        yield a, min(size, last - a)


def short_rows(ref, taps, m, a, count, lanes, tap_lanes):
    total = taps[m : m + 1, tap_lanes] * ref[a : a + count, lanes]
    for j in (1, 2):
        total = total + taps[3 * j + m : 3 * j + m + 1, tap_lanes] * ref[a - j : a - j + count, lanes]
    return total


ALL = slice(0, 128)


def stream(m):
    return slice(m * 128, (m + 1) * 128)


def mix_first(proj, taps, kern, filtered, prod, shifts, gated, part):
    for a, count in chunks(8, BACK + part, 64):
        prod[a : a + count] = short_rows(proj, taps, 1, a, count, stream(1), ALL) * short_rows(
            proj, taps, 2, a, count, stream(2), ALL
        )
    for a, count in chunks(BACK + part, BACK + AHEAD, 64):
        prod[a : a + count] = short_rows(proj, taps, 1, a, count, stream(1), ALL) * short_rows(
            proj, taps, 2, a, count, stream(2), ALL
        )
    shifted(shifts, prod, BACK - REACH + 1, KEPT + REACH, ALL)
    fir(shifts, kern, ALL, filtered, ALL, KEPT // 8, 10, True)
    for a, count in chunks(0, part, 64):
        query = short_rows(proj, taps, 0, BACK + a, count, stream(0), ALL)
        gated[a : a + count] = (query * filtered[a : a + count]).astype(BF16)


def mix_back(gg, proj, taps, kern, filtered, gf, gprod, gs, shifts, gp, part):
    for a, count in chunks(0, AHEAD, 64):
        gf[a : a + count] = gg[a : a + count] * short_rows(proj, taps, 0, BACK + a, count, stream(0), ALL)
    shifted(shifts, gf, 0, KEPT + REACH, ALL)
    fir(shifts, kern, ALL, gprod, ALL, KEPT // 8, 10, False)
    for a, count in chunks(0, KEPT, 64):
        here = slice(a, a + count)
        gs[0, here] = gg[here] * filtered[here]
        gs[1, here] = gprod[here] * short_rows(proj, taps, 2, BACK + a, count, stream(2), ALL)
        gs[2, here] = gprod[here] * short_rows(proj, taps, 1, BACK + a, count, stream(1), ALL)
    for m in range(3):
        for a, count in chunks(0, part, 64):
            total = taps[m : m + 1] * gs[m, a : a + count]
            for j in (1, 2):
                total = total + taps[3 * j + m : 3 * j + m + 1] * gs[m, a + j : a + j + count]
            gp[a : a + count, stream(m)] = total.astype(BF16)


def mix_sums(gf, proj, taps, gs, prod, shifts, out, part):
    for a, count in chunks(8, BACK + part + 8, 64):
        prod[a : a + count] = short_rows(proj, taps, 1, a, count, stream(1), ALL) * short_rows(
            proj, taps, 2, a, count, stream(2), ALL
        )
    shifted(shifts, prod, BACK - REACH + 1, part + REACH, ALL)
    lags(shifts, gf, ALL, out, ALL, part // 8)
    out[REACH:] = jnp.zeros((16, 128), F32)
    for m in range(3):
        for j in range(3):
            total = jnp.zeros((8, 128), F32)
            for a, count in chunks(0, part, 64):
                term = gs[m, a : a + count] * proj[BACK - j + a : BACK - j + a + count, stream(m)]
                total = total + jnp.sum(term.reshape(count // 8, 8, 128), axis=0)
            row = REACH + 3 * j + m
            out[row : row + 1] = jnp.sum(total, axis=0, keepdims=True)


def second_kernel(proj, taps, kern, part_ref, all_ref, gg_ref, filtered, prod, shifts, gated, *rest):
    bufs, (send, recv) = rest[:-2], rest[-2:]
    barrier = pltpu.get_barrier_semaphore()
    ctx = Group("ctx")
    greet(ctx.neighbours(), barrier)
    pl.semaphore_wait(barrier, 3)
    part = gated.shape[0]

    @pl.when(section_is(0))
    def _():
        mix_first(proj, taps, kern, filtered, prod, shifts, gated, part)
        job = Gather(ctx, gated, all_ref, Pool(send, recv), False)
        job.block = lambda ring, pair: all_ref.at[
            pl.ds(pl.multiple_of(pair * part, part), part), lanes_at(ring * 128)
        ]
        job.half = part // 2
        job.part = lambda ring, pair, second: all_ref.at[
            pl.ds(pl.multiple_of(pair * part + second * job.half, job.half), job.half), lanes_at(ring * 128)
        ]
        job.start()
        job.middle()
        job.finish()

    @pl.when(section_is(1))
    def _():
        PairThenRing(ctx, part_ref, Pool(send, recv), bufs).run(gg_ref)


def last_kernel(
    gg, proj, taps, kern, filtered, looked, gtab_all, taps_all,
    gf, gprod, gs, prod, shifts, gp, gtab, sums, got, block, send, recv,
):
    barrier = pltpu.get_barrier_semaphore()
    ctx = Group("ctx")
    greet(ctx.neighbours(), barrier)
    pl.semaphore_wait(barrier, 3)

    @pl.when(section_is(0))
    def _():
        pool = Pool(send, recv)
        sem = pool.take(1)[0]
        hold = got.shape[0]
        part = gp.shape[0]
        mix_back(gg, proj, taps, kern, filtered, gf, gprod, gs, shifts, gp, part)

        @pl.loop(0, 4)
        def _(k):
            here = pl.ds(pl.multiple_of(k * 128, 128), 128)
            gtab[here] = jnp.dot(looked[here], gp[...], preferred_element_type=F32).astype(BF16)

        halves = lambda p: gtab.at[pl.ds(pl.multiple_of(p * hold, hold), hold)]
        copy = remote(halves(ctx.mate), got, sem, ctx.at(ctx.ring, ctx.mate))
        copy.wait()
        add_into(block, [halves(ctx.pair), got])
        table = Gather(ctx, block, gtab_all, pool, False)
        table.start()
        mix_sums(gf, proj, taps, gs, prod, shifts, sums, part)
        job = Gather(ctx, sums, taps_all, pool, False)
        job.start()
        table.middle()
        job.middle()
        table.finish()
        job.finish()


def block1_kernel(
    x_ref, w_far, gg, cot, taps, kern,
    all_ref, e0_ref, gp_out, gated_out, sums_out, gf, prod,
    arrived, returned, wv, square, inv_ref, gpb, part, stats, stat_own, total_ref, block,
    kg, pp, query, filtered, gprod, gs, shifts, ptail, qtail, ghead, gfar, sfar, gfpad, row_sum, qsend, gsend, *rest,
):
    bufs, (send, recv, local_sem) = rest[:-3], rest[-3:]
    n = 2 * RING
    me = lax.axis_index("ctx")
    dp = Group("dp")
    after, before = {"ctx": (me + 1) % n}, {"ctx": (me + n - 1) % n}
    barrier = pltpu.get_barrier_semaphore()
    greet([after, before] + dp.neighbours() + [other_section()], barrier)
    pl.semaphore_wait(barrier, 6)
    rows, width = gg.shape
    pool = Pool(send, recv)
    relay = pool.take(2)
    forth = pltpu.make_async_remote_copy(
        src_ref=x_ref, dst_ref=arrived, send_sem=relay[0][0], recv_sem=relay[0][1],
        device_id=other_section(), device_id_type=MESH,
    )
    back = pltpu.make_async_remote_copy(
        src_ref=block, dst_ref=returned, send_sem=relay[1][0], recv_sem=relay[1][1],
        device_id=other_section(), device_id_type=MESH,
    )

    @pl.when(section_is(0))
    def _():
        mine = Pool(send, recv)
        mine.count = 2
        forth.start()
        back.wait_recv()
        gather = Gather(dp, returned, e0_ref, mine, True)
        gather.start()
        gather.middle()
        gather.finish()
        forth.wait_send()

    @pl.when(section_is(1))
    def _():
        load = pltpu.make_async_copy(w_far, wv, local_sem.at[0])
        load.start()
        forth.wait_recv()
        gather = Gather(dp, arrived, all_ref, pool, True)
        gather.start()
        load.wait()

        def use(ref, slot, begin=False):
            values = ref[...]
            for m in range(3):
                ml = slice(m * width, (m + 1) * width)
                term = dot(values, wv[slot, :, ml])
                pp[8:, ml] = term if begin else pp[8:, ml] + term
            term = jnp.zeros((rows, 128), F32)
            for g in range(width // 128):
                v = values[:, g * 128 : (g + 1) * 128].astype(F32)
                term = term + v * v
            square[...] = term if begin else square[...] + term

        use(arrived, dp.slot(dp.ring, dp.pair), True)
        gather.middle()
        for ring, pair in ((dp.left, dp.pair), (dp.right, dp.pair), (dp.ring, dp.mate), (dp.left, dp.mate), (dp.right, dp.mate)):
            use(gather.block(ring, pair), dp.slot(ring, pair))
        gather.finish()
        for pair in (dp.pair, dp.mate):
            use(gather.block(dp.across, pair), dp.slot(dp.across, pair))
        inv = lax.rsqrt(jnp.sum(square[...], axis=1, keepdims=True) / (width * n) + EPSILON)
        inv_ref[...] = jnp.broadcast_to(inv, (rows, 128))
        for a, count in chunks(0, rows, 32):
            pp[8 + a : 8 + a + count] = pp[8 + a : 8 + a + count] * inv_ref[a : a + count, :1]

        sems = pool.take(4)
        a_copy = remote(pp.at[pl.ds(rows, 8)], ptail, sems[0], after)

        def products(a, count, group):
            tl = lanes_at(group * 128)
            k = short_rows(pp, taps, 1, a, count, lanes_at(width + group * 128), tl)
            v = short_rows(pp, taps, 2, a, count, lanes_at(2 * width + group * 128), tl)
            return k * v

        @pl.loop(0, 4)
        def _(group):
            tl = lanes_at(group * 128)
            for a, count in chunks(rows // 2, rows, 64):
                value = products(8 + a, count, group)
                prod[REACH + a : REACH + a + count, tl] = value
                qsend[a - rows // 2 : a - rows // 2 + count, tl] = value.astype(BF16)

        b_copy = remote(qsend, qtail, sems[1], after)
        a_copy.wait_recv()
        pp[0:8] = jnp.where(me > 0, ptail[...], 0.0)

        @pl.loop(0, 4)
        def _(group):
            tl = lanes_at(group * 128)
            for a, count in chunks(0, rows, 64):
                value = short_rows(pp, taps, 0, 8 + a, count, tl, tl)
                query[a : a + count, tl] = value
                value = value * gg[a : a + count, tl]
                gf[a : a + count, tl] = value
                gfpad[a : a + count, tl] = value
                if a < REACH:
                    ghead[a : a + count, tl] = value.astype(BF16)
            for a, count in chunks(0, rows // 2, 64):
                prod[REACH + a : REACH + a + count, tl] = products(8 + a, count, group)

        c_copy = remote(ghead, gfar, sems[2], before)
        b_copy.wait_recv()
        for a, count in chunks(0, REACH, 32):
            prod[a : a + count] = jnp.where(me > 0, qtail[a : a + count].astype(F32), 0.0)

        @pl.loop(0, 4)
        def _(group):
            tl = lanes_at(group * 128)
            shifted(shifts, prod, 1, rows + REACH - 8, tl)
            kg[...] = kern[:, tl]
            fir(shifts, kg, ALL, filtered, tl, rows // 8, 8, True)
            for a, count in chunks(0, rows, 64):
                gated_out[a : a + count, tl] = (query[a : a + count, tl] * filtered[a : a + count, tl]).astype(BF16)

        c_copy.wait_recv()
        for a, count in chunks(0, REACH, 32):
            gfpad[rows + a : rows + a + count] = jnp.where(me < n - 1, gfar[a : a + count].astype(F32), 0.0)

        @pl.loop(0, 4)
        def _(group):
            tl = lanes_at(group * 128)
            shifted(shifts, gfpad, 0, rows + REACH - 8, tl)
            kg[...] = kern[:, tl]
            fir(shifts, kg, ALL, gprod, tl, rows // 8, 8, False)
            for a, count in chunks(0, rows, 64):
                here = slice(a, a + count)
                gs[here, tl] = gg[here, tl] * filtered[here, tl]
                k = short_rows(pp, taps, 1, 8 + a, count, lanes_at(width + group * 128), tl)
                v = short_rows(pp, taps, 2, 8 + a, count, lanes_at(2 * width + group * 128), tl)
                gs[here, lanes_at(width + group * 128)] = gprod[here, tl] * v
                gs[here, lanes_at(2 * width + group * 128)] = gprod[here, tl] * k

        for m in range(3):
            gsend[:, m * width : (m + 1) * width] = gs[0:8, m * width : (m + 1) * width]
        d_copy = remote(gsend, sfar, sems[3], before)
        d_copy.wait_recv()
        gs[rows : rows + 8] = jnp.where(me < n - 1, sfar[...], 0.0)
        row_sum[...] = jnp.zeros_like(row_sum)

        @pl.loop(0, 4)
        def _(group):
            tl = lanes_at(group * 128)
            for m in range(3):
                ml = lanes_at(m * width + group * 128)
                sums = [jnp.zeros((8, 128), F32) for _ in range(3)]
                for a, count in chunks(0, rows, 64):
                    total = taps[m : m + 1, tl] * gs[a : a + count, ml]
                    for j in (1, 2):
                        total = total + taps[3 * j + m : 3 * j + m + 1, tl] * gs[a + j : a + j + count, ml]
                    gpb[a : a + count, ml] = total.astype(BF16)
                    gp_out[a : a + count, ml] = (total * inv_ref[a : a + count]).astype(BF16)
                    row_sum[a : a + count] += total * pp[8 + a : 8 + a + count, ml]
                    for j in range(3):
                        term = gs[a : a + count, ml] * pp[8 - j + a : 8 - j + a + count, ml]
                        sums[j] = sums[j] + jnp.sum(term.reshape(count // 8, 8, 128), axis=0)
                for j in range(3):
                    sums_out[3 * j + m : 3 * j + m + 1, tl] = jnp.sum(sums[j], axis=0, keepdims=True)

        eye = lax.broadcasted_iota(jnp.int32, (128, 128), 0) == lax.broadcasted_iota(jnp.int32, (128, 128), 1)
        stat_own[...] = jnp.zeros_like(stat_own)
        for k in range(rows // 128):
            column = jnp.sum(row_sum[k * 128 : (k + 1) * 128], axis=1, keepdims=True)
            line = jnp.sum(jnp.where(eye, jnp.broadcast_to(column, (128, 128)), 0.0), axis=0, keepdims=True)
            stat_own[k : k + 1] = line
        stat = Gather(dp, stat_own, stats, pool, True)
        stat.start()

        def produce(slot):
            part[slot] = dot(gpb[...], wv[slot], TRANS_B).astype(BF16)

        RingThenPair(dp, part, pool, bufs).run(total_ref, produce=produce)
        stat.middle()
        stat.finish()
        summed = stats[0]
        for k in range(1, n):
            summed = summed + stats[k]
        for k in range(rows // 128):
            here = pl.ds(k * 128, 128)
            line = jnp.broadcast_to(summed[k : k + 1], (128, 128))
            scalar = jnp.sum(jnp.where(eye, line, 0.0), axis=1, keepdims=True)
            inv = inv_ref[here, :1]
            block[here] = (
                cot[here].astype(F32)
                + inv * total_ref[here]
                - arrived[here].astype(F32) * (inv * inv * scalar / (width * n))
            ).astype(BF16)
        back.start()
        for copy in (a_copy, b_copy, c_copy, d_copy):
            copy.wait_send()
        back.wait_send()


def late_kernel(
    e0_ref, w_ref, gp_ref, gated_ref, normed_ref, gf, prod, sums_ref,
    gg_ref, gp_all, gated_all, normed_all, taps_all, shifts, taps_own, part_ref, *rest,
):
    bufs, (send, recv) = rest[:-2], rest[-2:]
    barrier = pltpu.get_barrier_semaphore()
    ctx = Group("ctx")
    me = lax.axis_index("ctx")
    everyone = [{"ctx": (me + k) % (2 * RING)} for k in range(1, 2 * RING)]
    greet(everyone, barrier)
    pl.semaphore_wait(barrier, 2 * RING - 1)

    @pl.when(section_is(0))
    def _():
        count, rows, _ = e0_ref.shape
        for k in range(count):
            product = dot(e0_ref[k], w_ref[...], TRANS_B).astype(BF16)
            core, first = divmod(k * rows, count // 2 * rows)
            for strip in range(RING):
                part = product[:, strip * 128 : (strip + 1) * 128]
                part_ref[strip * 2 + core, first : first + rows] = part
                if core == 1 and first == 0:
                    part_ref[strip * 2, count // 2 * rows : AHEAD] = part[: AHEAD - count // 2 * rows]
        over = AHEAD - count // 2 * rows
        for strip in range(RING):
            part_ref[strip * 2 + 1, count // 2 * rows : AHEAD] = jnp.zeros((over, 128), BF16)
        PairThenRing(ctx, part_ref, Pool(send, recv), bufs).run(gg_ref)

    @pl.when(section_is(1))
    def _():
        pool = Pool(send, recv)
        jobs = [
            Gather(ctx, gp_ref, gp_all, pool, False),
            Gather(ctx, gated_ref, gated_all, pool, False),
        ]
        for job in jobs:
            job.start()
        sems = pool.take(8)
        own = pltpu.make_async_copy(normed_ref.at[me], normed_all.at[me], sems[7][0])
        own.start()
        sends = []
        for k, device in enumerate(everyone):
            target = (me + k + 1) % (2 * RING)
            sends.append(remote(normed_ref.at[target], normed_all.at[me], sems[k], device))

        @pl.loop(0, 4)
        def _(group):
            tl = lanes_at(group * 128)
            shifted(shifts, prod, 1, gf.shape[0] + REACH - 8, tl)
            lags(shifts, gf, tl, taps_own, tl, gf.shape[0] // 8)

        taps_own[REACH:] = sums_ref[...]
        jobs.append(Gather(ctx, taps_own, taps_all, pool, False))
        jobs[-1].start()
        for job in jobs:
            job.middle()
        for job in jobs:
            job.finish()
        own.wait()
        for copy in sends:
            copy.wait()


def dot(a, b, dims=(((1,), (0,)), ((), ()))):
    return lax.dot_general(a, b, dims, preferred_element_type=F32)


TRANS_B = (((1,), (1,)), ((), ()))
TRANS_A = (((0,), (0,)), ((), ()))


def onehot(ids, count):
    return (ids[:, None] == jnp.arange(count, dtype=jnp.int32)[None, :]).astype(BF16)


def local(
    token_ids, embedding, project_in, short_taps, filter_taps, decay_rates, project_out, cotangent
):
    section_zero = lax.axis_index("section") == 0
    n = lax.axis_size("ctx")
    vocab = embedding.shape[0]
    rows = token_ids.shape[0]
    seq = rows * n
    part = seq // 2
    width = embedding.shape[1]
    chans = project_in.shape[3]
    lane = chans // RING
    taps_all = short_taps[0]
    filter_all = filter_taps[0]
    tap_count = filter_all.shape[0]
    place = lax.axis_index("ctx")
    core, strip = place % 2, place // 2
    base = core * part

    w_flat = project_in[0].reshape(width, 3 * chans)
    w_out = project_out[0]
    positions = jnp.arange(tap_count).astype(F32)
    damping_all = jnp.exp(-decay_rates[0][None, :] * positions[:, None] / tap_count)
    kernel_all = filter_all * damping_all

    own_tokens = jnp.tile(token_ids.reshape(rows // lane, lane), (16 * lane // rows, 1))
    emb, table, inv_table, tokens, w_full, e1 = call(
        begin_kernel,
        1,
        [
            ((n, vocab // n, width), BF16),
            ((vocab, 3 * lane), BF16),
            ((vocab, lane), F32),
            ((n, 16, lane), jnp.int32),
            ((n, width, 3 * chans), BF16),
            ((n, rows, width), BF16),
        ],
        [
            pltpu.VMEM((n, vocab // 2, 4 * lane), BF16),
            pltpu.VMEM((rows, width), BF16),
            pltpu.VMEM((vocab // 2, 4 * lane), F32),
            pltpu.VMEM((vocab // n, width), BF16),
        ]
        + PairThenRing.scratch(vocab // 2, 4 * lane),
        48,
        embedding, w_flat, w_flat, cotangent, own_tokens,
        in_specs=[VMEM, VMEM, ANY, VMEM, VMEM],
        out_specs=[VMEM, VMEM, VMEM, VMEM, ANY, VMEM],
        name="begin",
    )
    tokens = tokens[:, : rows // lane].reshape(seq)
    emb = emb.reshape(vocab, width)

    def strip_of(a):
        return lax.dynamic_slice_in_dim(a, strip * lane, lane, a.ndim - 1)

    taps0, kernel0 = strip_of(taps_all), strip_of(kernel_all)
    at = BACK - 2

    taps0 = taps0.reshape(9, lane)
    taps1 = taps_all.reshape(9, chans)
    rows_id = jnp.arange(vocab, dtype=jnp.int32)

    def own_block0():
        padded = jnp.concatenate(
            [jnp.full((BACK,), -1, jnp.int32), tokens, jnp.full((AHEAD - part,), -1, jnp.int32)]
        )
        seen = lax.dynamic_slice_in_dim(padded, base, BACK + AHEAD, 0)
        proj = dot(onehot(seen, vocab), table)
        mine = lax.dynamic_slice_in_dim(tokens, lax.axis_index("dp") * rows, rows, 0)
        first = dot(onehot(mine, vocab), emb).astype(BF16)
        looked = (rows_id[:, None] == lax.dynamic_slice_in_dim(tokens, base, part, 0)[None, :]).astype(BF16)
        return proj, first, looked, e1

    def own_block1():
        shapes = jax.eval_shape(own_block0)
        blank = jax.tree.map(lambda s: jnp.zeros(s.shape, s.dtype), shapes[:-1])
        grad_part = dot(e1.reshape(seq, width), w_out, TRANS_B).astype(BF16)
        return *blank, grad_part.reshape(n, rows, chans)

    proj0, first, looked, gg1_part = lax.cond(section_zero, own_block0, own_block1)
    gated0_all, gg1, filtered0 = call(
        second_kernel,
        2,
        [((seq, chans), BF16), ((rows, chans), F32), ((KEPT, lane), F32)],
        [
            pltpu.VMEM((BACK + AHEAD, lane), F32),
            pltpu.VMEM((8, KEPT + REACH, lane), F32),
            pltpu.VMEM((part, lane), BF16),
        ]
        + PairThenRing.scratch(rows, chans),
        16,
        proj0, taps0, kernel0, gg1_part,
        name="second",
    )
    out_part = dot(gated0_all, w_out).astype(BF16)
    (second,) = call(
        reduce_kernel,
        3,
        [((rows, width), BF16)],
        [pltpu.VMEM((rows, width), F32)] + RingThenPair.scratch(rows, width),
        24,
        out_part.reshape(n, rows, width), first,
        name="reduce",
    )
    rows_all, e0, gp1, gated1, sums1, gf1, prod1 = call(
        block1_kernel,
        4,
        [
            ((n, rows, width), BF16),
            ((n, rows, width), BF16),
            ((rows, 3 * chans), BF16),
            ((rows, chans), BF16),
            ((16, chans), F32),
            ((rows, chans), F32),
            ((rows + REACH, chans), F32),
        ],
        [
            pltpu.VMEM((rows, width), BF16),
            pltpu.VMEM((rows, width), BF16),
            pltpu.VMEM((n, width, 3 * chans), BF16),
            pltpu.VMEM((rows, 128), F32),
            pltpu.VMEM((rows, 128), F32),
            pltpu.VMEM((rows, 3 * chans), BF16),
            pltpu.VMEM((n, rows, width), BF16),
            pltpu.VMEM((n, 16, 128), F32),
            pltpu.VMEM((16, 128), F32),
            pltpu.VMEM((rows, width), F32),
            pltpu.VMEM((rows, width), BF16),
            pltpu.VMEM((REACH, 128), F32),
            pltpu.VMEM((rows + 8, 3 * chans), F32),
            pltpu.VMEM((rows, chans), F32),
            pltpu.VMEM((rows, chans), F32),
            pltpu.VMEM((rows, chans), F32),
            pltpu.VMEM((rows + 8, 3 * chans), F32),
            pltpu.VMEM((8, rows + REACH, 128), F32),
            pltpu.VMEM((8, 3 * chans), F32),
            pltpu.VMEM((REACH, chans), BF16),
            pltpu.VMEM((REACH, chans), BF16),
            pltpu.VMEM((REACH, chans), BF16),
            pltpu.VMEM((8, 3 * chans), F32),
            pltpu.VMEM((rows + REACH, chans), F32),
            pltpu.VMEM((rows, 128), F32),
            pltpu.VMEM((REACH, chans), BF16),
            pltpu.VMEM((8, 3 * chans), F32),
        ]
        + RingThenPair.scratch(rows, width),
        48,
        second, w_full, gg1, cotangent, taps1, kernel_all,
        in_specs=[VMEM, ANY, VMEM, VMEM, VMEM, VMEM],
        local=1,
        name="block1",
    )

    e0_all = e0.reshape(seq, width)

    gg0, gp1_all, gated1_all, normed1, taps1_all = call(
        late_kernel,
        5,
        [
            ((AHEAD, lane), F32),
            ((n, rows, 3 * chans), BF16),
            ((n, rows, chans), BF16),
            ((n, rows, width), BF16),
            ((n, 144, chans), F32),
        ],
        [pltpu.VMEM((8, rows + REACH, 128), F32), pltpu.VMEM((144, chans), F32), pltpu.VMEM((n, AHEAD, lane), BF16)]
        + PairThenRing.scratch(AHEAD, lane),
        40,
        e0, w_out, gp1, gated1, rows_all, gf1, prod1, sums1,
        in_specs=[VMEM, VMEM, ANY, ANY, ANY, VMEM, VMEM, VMEM],
        out_specs=[VMEM, ANY, ANY, ANY, VMEM],
        name="late",
    )
    gtab, sums0 = call(
        last_kernel,
        6,
        [((n, vocab // 2, 3 * lane), BF16), ((n, 144, lane), F32)],
        [
            pltpu.VMEM((AHEAD, lane), F32),
            pltpu.VMEM((KEPT, lane), F32),
            pltpu.VMEM((3, KEPT, lane), F32),
            pltpu.VMEM((BACK + AHEAD, lane), F32),
            pltpu.VMEM((8, KEPT + REACH, lane), F32),
            pltpu.VMEM((part, 3 * lane), BF16),
            pltpu.VMEM((vocab, 3 * lane), BF16),
            pltpu.VMEM((144, lane), F32),
            pltpu.VMEM((vocab // 2, 3 * lane), BF16),
            pltpu.VMEM((vocab // 2, 3 * lane), BF16),
        ],
        24,
        gg0, proj0, taps0, kernel0, filtered0, looked,
        name="last",
    )

    def end0():
        table_rows = jnp.transpose(gtab.reshape(RING, 2, vocab // 2, 3, lane), (1, 2, 3, 0, 4))
        normed_table = (emb.astype(F32) * inv_table[:, :1]).astype(BF16)
        sums = sums0.reshape(RING, 2, 144, lane).sum(axis=1)
        return (
            dot(normed_table, table_rows.reshape(vocab, 3 * chans), TRANS_A),
            dot(gated0_all, e0_all, TRANS_A),
            jnp.transpose(sums, (1, 0, 2)).reshape(144, chans),
        )

    def end1():
        return (
            dot(normed1.reshape(seq, width), gp1_all.reshape(seq, 3 * chans), TRANS_A),
            dot(gated1_all.reshape(seq, chans), e1.reshape(seq, width), TRANS_A),
            taps1_all.sum(axis=0),
        )

    grad_in, grad_out, sums = lax.cond(section_zero, end0, end1)
    grad_in = grad_in.reshape(width, 3, chans)
    gk, gt = sums[:tap_count], sums[tap_count : tap_count + 9].reshape(3, 3, chans)
    grad_filter = gk * damping_all
    grad_decay = -jnp.sum(gk * kernel_all * positions[:, None], axis=0) / tap_count
    return (grad_in[None], grad_out[None], grad_filter[None], grad_decay[None], gt[None])


def solution(mesh):
    return jax.shard_map(
        local,
        mesh=mesh,
        in_specs=(
            P("ctx"),
            P(None, "dp"),
            P("section", "ctx", None, "dp"),
            P("section", None, None, "dp"),
            P("section", None, "dp"),
            P("section", "dp"),
            P("section", "dp", "ctx"),
            P("ctx", "dp"),
        ),
        out_specs=(
            P("section", "ctx", None, "dp"),
            P("section", "dp", "ctx"),
            P("section", None, "dp"),
            P("section", "dp"),
            P("section", None, None, "dp"),
        ),
        check_vma=False,
    )
```

```python
import functools

import jax
import jax.numpy as jnp
from jax import lax
from jax.experimental import pallas as pl
from jax.experimental.pallas import tpu as pltpu
from jax.sharding import PartitionSpec as P

EPSILON = 1e-06
F32 = jnp.float32
BF16 = jnp.bfloat16
MESH = pl.DeviceIdType.MESH
BACK = 256
AHEAD = 1184
KEPT = 1040
RING = 4
REACH = 128


class Group:
    def __init__(self, axis):
        self.axis = axis
        me = lax.axis_index(axis)
        if axis == "ctx":
            self.ring, self.pair = me // 2, me % 2
        else:
            self.ring, self.pair = me % RING, me // RING
        self.right = (self.ring + 1) % RING
        self.left = (self.ring + RING - 1) % RING
        self.across = (self.ring + 2) % RING
        self.mate = 1 - self.pair

    def slot(self, ring, pair):
        return ring * 2 + pair if self.axis == "ctx" else pair * RING + ring

    def at(self, ring, pair):
        return {self.axis: self.slot(ring, pair)}

    def neighbours(self):
        return [
            self.at(self.right, self.pair),
            self.at(self.left, self.pair),
            self.at(self.ring, self.mate),
        ]


class Pool:
    def __init__(self, send, recv):
        self.send, self.recv, self.count = send, recv, 0

    def take(self, k):
        first = self.count
        self.count += k
        return [(self.send.at[first + i], self.recv.at[first + i]) for i in range(k)]


def remote(src, dst, sems, device):
    copy = pltpu.make_async_remote_copy(
        src_ref=src,
        dst_ref=dst,
        send_sem=sems[0],
        recv_sem=sems[1],
        device_id=device,
        device_id_type=MESH,
    )
    copy.start()
    return copy


def greet(devices, barrier):
    for device in devices:
        pl.semaphore_signal(barrier, inc=1, device_id=device, device_id_type=MESH)


class Gather:
    def __init__(self, group, src, out, pool, pair_first, place=None):
        self.g, self.src, self.out, self.pair_first = group, src, out, pair_first
        self.sems = pool.take(9)
        self.own = pool.take(1)[0]
        self.rows = src.shape[0]
        self.half = self.rows // 2
        self.place = place or (lambda ring, pair, first, rows: out.at[group.slot(ring, pair), pl.ds(first, rows)])

    def block(self, ring, pair):
        return self.place(ring, pair, 0, self.rows)

    def part(self, ring, pair, second):
        return self.place(ring, pair, self.half * second, self.half)

    def start(self):
        g, s = self.g, self.sems
        mine = self.block(g.ring, g.pair)
        right, left, mate = g.neighbours()
        self.local = pltpu.make_async_copy(self.src, mine, self.own[0])
        self.local.start()
        first = remote(self.src, mine, s[0], mate)
        self.copies = [first, remote(self.src, mine, s[1], right), remote(self.src, mine, s[2], left)]

    def turn(self, pair, a, b, c, d):
        g, s = self.g, self.sems
        right, left, mate = g.neighbours()
        more = []
        a.wait_recv()
        part = self.part(g.left, pair, 0)
        more.append(remote(part, part, s[c], right))
        if not self.pair_first:
            block = self.block(g.left, pair)
            more.append(remote(block, block, s[5], mate))
        b.wait_recv()
        part = self.part(g.right, pair, 1)
        more.append(remote(part, part, s[d], left))
        if not self.pair_first:
            block = self.block(g.right, pair)
            more.append(remote(block, block, s[6], mate))
        return more

    def middle(self):
        g, s = self.g, self.sems
        right, left, mate = g.neighbours()
        mate_copy, to_right, to_left = self.copies
        rest = self.turn(g.pair, to_right, to_left, 3, 4)
        self.sent = list(self.copies) + rest
        if self.pair_first:
            self.late = list(rest)
            mate_copy.wait_recv()
            block = self.block(g.ring, g.mate)
            a = remote(block, block, s[5], right)
            b = remote(block, block, s[6], left)
            more = self.turn(g.mate, a, b, 7, 8)
            self.sent += [a, b] + more
            self.late += more
        else:
            rest[0].wait_recv()
            rest[2].wait_recv()
            block = self.block(g.across, g.pair)
            last = remote(block, block, s[7], mate)
            self.sent.append(last)
            self.late = [mate_copy, rest[1], rest[3], last]

    def finish(self):
        for copy in self.late:
            copy.wait_recv()
        for copy in self.sent:
            copy.wait_send()
        self.local.wait()


def add_into(out, terms, rows=64):
    @pl.loop(0, out.shape[0] // rows)
    def _(step):
        here = pl.ds(pl.multiple_of(step * rows, rows), rows)
        total = terms[0][here].astype(F32)
        for term in terms[1:]:
            total = total + term[here].astype(F32)
        out[here] = total.astype(out.dtype)


def rows_step(count):
    for rows in (64, 48, 37 * 16, 32, 16):
        if count % rows == 0:
            return rows if rows != 37 * 16 else 16
    return 16


class Around:
    def __init__(self, group, pool, bufs):
        self.g = group
        self.s = pool.take(6)
        self.rel, self.merged, self.came = bufs
        self.half = self.rel.shape[1]

    @staticmethod
    def scratch(rows, lanes):
        half = rows // 2
        return [
            pltpu.VMEM((2, half, lanes), BF16),
            pltpu.VMEM((2, half, lanes), BF16),
            pltpu.VMEM((2, 2, half, lanes), BF16),
        ]

    def halves(self, ref):
        return ref.at[pl.ds(0, self.half)], ref.at[pl.ds(self.half, self.half)]

    def send_across(self, block):
        right, left, _ = self.g.neighbours()
        a, b = self.halves(block)
        self.copies = [remote(a, self.rel.at[0], self.s[0], right), remote(b, self.rel.at[1], self.s[1], left)]

    def send_near(self, to_right, to_left):
        right, left, _ = self.g.neighbours()
        self.to_right, self.to_left = to_right, to_left
        b = self.halves(to_right)[1]
        a = self.halves(to_left)[0]
        self.copies += [
            remote(b, self.came.at[0, 1], self.s[2], right),
            remote(a, self.came.at[1, 0], self.s[3], left),
        ]

    def merge(self):
        right, left, _ = self.g.neighbours()
        step = rows_step(self.half)
        self.copies[0].wait_recv()
        add_into(self.merged.at[0], [self.halves(self.to_right)[0], self.rel.at[0]], step)
        self.copies.append(remote(self.merged.at[0], self.came.at[0, 0], self.s[4], right))
        self.copies[1].wait_recv()
        add_into(self.merged.at[1], [self.halves(self.to_left)[1], self.rel.at[1]], step)
        self.copies.append(remote(self.merged.at[1], self.came.at[1, 1], self.s[5], left))

    def collect(self, out, own):
        step = rows_step(self.half)
        for copy in self.copies[2:]:
            copy.wait_recv()
        for h in range(2):
            piece = pl.ds(h * self.half, self.half)
            add_into(
                out.at[piece],
                [ref.at[piece] for ref in own] + [self.came.at[0, h], self.came.at[1, h]],
                step,
            )

    def finish(self):
        for copy in self.copies:
            copy.wait_send()


class PairThenRing:
    def __init__(self, group, inp, pool, bufs):
        self.g, self.inp = group, inp
        self.got, self.sums = bufs[:2]
        self.ring = Around(group, pool, bufs[2:])
        self.s = pool.take(4)

    @staticmethod
    def scratch(rows, lanes):
        return [pltpu.VMEM((4, rows, lanes), BF16), pltpu.VMEM((4, rows, lanes), BF16)] + Around.scratch(rows, lanes)

    def run(self, out):
        g = self.g
        mate = g.at(g.ring, g.mate)
        order = [g.across, g.right, g.left, g.ring]
        copies = [
            remote(self.inp.at[g.slot(r, g.mate)], self.got.at[k], self.s[k], mate) for k, r in enumerate(order)
        ]
        step = rows_step(self.inp.shape[1])

        def pair_sum(k):
            copies[k].wait_recv()
            add_into(self.sums.at[k], [self.inp.at[g.slot(order[k], g.pair)], self.got.at[k]], step)

        pair_sum(0)
        self.ring.send_across(self.sums.at[0])
        pair_sum(1)
        pair_sum(2)
        self.ring.send_near(self.sums.at[1], self.sums.at[2])
        copies[3].wait_recv()
        self.ring.merge()
        self.ring.collect(out, [self.inp.at[g.slot(g.ring, g.pair)], self.got.at[3]])
        self.ring.finish()
        for copy in copies:
            copy.wait_send()


class RingThenPair:
    def __init__(self, group, inp, pool, bufs):
        self.g, self.inp = group, inp
        self.far, self.got = bufs[:2]
        self.rings = [Around(group, pool, bufs[2:5]), Around(group, pool, bufs[5:8])]
        self.s = pool.take(1)[0]

    @staticmethod
    def scratch(rows, lanes):
        return (
            [pltpu.VMEM((rows, lanes), BF16), pltpu.VMEM((rows, lanes), BF16)]
            + Around.scratch(rows, lanes)
            + Around.scratch(rows, lanes)
        )

    def run(self, out, extra=(), produce=lambda slot: None):
        g = self.g
        pairs = [g.mate, g.pair]
        blocks = lambda ring, pair: self.inp.at[g.slot(ring, pair)]
        for ring, pair in zip(self.rings, pairs):
            produce(g.slot(g.across, pair))
            ring.send_across(blocks(g.across, pair))
            produce(g.slot(g.right, pair))
            produce(g.slot(g.left, pair))
            ring.send_near(blocks(g.right, pair), blocks(g.left, pair))
            produce(g.slot(g.ring, pair))
        self.rings[0].merge()
        self.rings[1].merge()
        self.rings[0].collect(self.far, [blocks(g.ring, g.mate)])
        copy = remote(self.far, self.got, self.s, g.at(g.ring, g.mate))
        self.rings[1].collect(out, [blocks(g.ring, g.pair)])
        copy.wait_recv()
        add_into(out, [out, self.got] + list(extra), rows_step(out.shape[0]))
        copy.wait_send()
        for ring in self.rings:
            ring.finish()


ANY = pl.BlockSpec(memory_space=pl.ANY)
VMEM = pl.BlockSpec(memory_space=pltpu.VMEM)


def call(body, ident, outs, scratch, sems, *args, in_specs=None, out_specs=None, name=None, local=0):
    return pl.pallas_call(
        body,
        out_shape=[jax.ShapeDtypeStruct(shape, dtype) for shape, dtype in outs],
        in_specs=in_specs or [VMEM] * len(args),
        out_specs=out_specs or [VMEM] * len(outs),
        scratch_shapes=list(scratch)
        + [pltpu.SemaphoreType.DMA((sems,)), pltpu.SemaphoreType.DMA((sems,))]
        + ([pltpu.SemaphoreType.DMA((local,))] if local else []),
        compiler_params=pltpu.CompilerParams(
            collective_id=ident, has_side_effects=True, vmem_limit_bytes=60 * 1024 * 1024
        ),
        name=name,
    )(*args)


def section_is(k):
    return lax.axis_index("section") == k


def crossing():
    i, j = lax.axis_index("dp"), lax.axis_index("ctx")
    return {"dp": j, "ctx": i}, i != j


def other_section():
    i, j = lax.axis_index("dp"), lax.axis_index("ctx")
    return {"section": 1 - lax.axis_index("section"), "dp": j, "ctx": i}


def lanes_at(first):
    return pl.ds(pl.multiple_of(first, 128), 128)


def shifted(shifts, ref, start, rows, lanes):
    for r in range(8):
        for a in range(0, rows, 64):
            count = min(64, rows - a)
            shifts[r, a : a + count] = ref[start + r + a : start + r + a + count, lanes]


def fir(shifts, kern, lanes, out, out_lanes, tiles, block, backwards):
    @pl.loop(0, tiles // block)
    def _(b):
        first = pl.multiple_of(b * block * 8, 8)

        def step(r, totals):
            totals = list(totals)
            taps = []
            for q in range(REACH // 8):
                u = 8 * q + r
                taps.append(kern[pl.ds(REACH - 1 - u if backwards else u, 8, stride=0), lanes])
            for i in range(block + REACH // 8 - 1):
                x = shifts[r, pl.ds(first + 8 * i, 8)]
                for o in range(block):
                    if 0 <= i - o < REACH // 8:
                        totals[o] = totals[o] + taps[i - o] * x
            return tuple(totals)

        totals = lax.fori_loop(0, 8, step, tuple(jnp.zeros((8, 128), F32) for _ in range(block)))
        for o in range(block):
            out[pl.ds(first + 8 * o, 8), out_lanes] = totals[o]


def lags(shifts, ref, lanes, out, out_lanes, tiles):
    for r in range(8):

        def step(b, totals):
            totals = list(totals)
            first = pl.multiple_of(b * 32, 8)
            own = [ref[pl.ds(first + 8 * o, 8), lanes] for o in range(4)]
            for i in range(4 + REACH // 8 - 1):
                x = shifts[r, pl.ds(first + 8 * i, 8)]
                for o in range(4):
                    if 0 <= i - o < REACH // 8:
                        totals[i - o] = totals[i - o] + own[o] * x
            return tuple(totals)

        totals = lax.fori_loop(0, tiles // 4, step, tuple(jnp.zeros((8, 128), F32) for _ in range(REACH // 8)))
        for q in range(REACH // 8):
            row = REACH - 1 - (8 * q + r)
            out[row : row + 1, out_lanes] = jnp.sum(totals[q], axis=0, keepdims=True)


def chunks(first, last, size):
    for a in range(first, last, size):
        yield a, min(size, last - a)


def short_rows(ref, taps, m, a, count, lanes, tap_lanes):
    total = taps[m : m + 1, tap_lanes] * ref[a : a + count, lanes]
    for j in (1, 2):
        total = total + taps[3 * j + m : 3 * j + m + 1, tap_lanes] * ref[a - j : a - j + count, lanes]
    return total


ALL = slice(0, 128)


def stream(m):
    return slice(m * 128, (m + 1) * 128)


def mix_first(proj, taps, kern, filtered, prod, shifts, gated, part):
    for a, count in chunks(BACK - REACH, BACK + part, 64):
        prod[a : a + count] = short_rows(proj, taps, 1, a, count, stream(1), ALL) * short_rows(
            proj, taps, 2, a, count, stream(2), ALL
        )
    for a, count in chunks(BACK + part, BACK + AHEAD, 64):
        prod[a : a + count] = short_rows(proj, taps, 1, a, count, stream(1), ALL) * short_rows(
            proj, taps, 2, a, count, stream(2), ALL
        )
    shifted(shifts, prod, BACK - REACH + 1, KEPT + REACH, ALL)
    fir(shifts, kern, ALL, filtered, ALL, KEPT // 8, 10, True)
    for a, count in chunks(0, part, 64):
        query = short_rows(proj, taps, 0, BACK + a, count, stream(0), ALL)
        gated[a : a + count] = (query * filtered[a : a + count]).astype(BF16)


def mix_back(gg, proj, taps, kern, filtered, gf, gprod, gs, shifts, gp, part):
    for a, count in chunks(0, AHEAD, 64):
        gf[a : a + count] = gg[a : a + count] * short_rows(proj, taps, 0, BACK + a, count, stream(0), ALL)
    shifted(shifts, gf, 0, KEPT + REACH, ALL)
    fir(shifts, kern, ALL, gprod, ALL, KEPT // 8, 10, False)
    for a, count in chunks(0, KEPT, 64):
        here = slice(a, a + count)
        gs[0, here] = gg[here] * filtered[here]
        gs[1, here] = gprod[here] * short_rows(proj, taps, 2, BACK + a, count, stream(2), ALL)
        gs[2, here] = gprod[here] * short_rows(proj, taps, 1, BACK + a, count, stream(1), ALL)
    for m in range(3):
        for a, count in chunks(0, part, 64):
            total = taps[m : m + 1] * gs[m, a : a + count]
            for j in (1, 2):
                total = total + taps[3 * j + m : 3 * j + m + 1] * gs[m, a + j : a + j + count]
            gp[a : a + count, stream(m)] = total.astype(BF16)


def mix_sums(gf, proj, taps, gs, prod, shifts, out, part):
    for a, count in chunks(BACK - REACH, BACK + part + 8, 64):
        prod[a : a + count] = short_rows(proj, taps, 1, a, count, stream(1), ALL) * short_rows(
            proj, taps, 2, a, count, stream(2), ALL
        )
    shifted(shifts, prod, BACK - REACH + 1, part + REACH, ALL)
    lags(shifts, gf, ALL, out, ALL, part // 8)
    out[REACH:] = jnp.zeros((16, 128), F32)
    for m in range(3):
        for j in range(3):
            total = jnp.zeros((8, 128), F32)
            for a, count in chunks(0, part, 64):
                term = gs[m, a : a + count] * proj[BACK - j + a : BACK - j + a + count, stream(m)]
                total = total + jnp.sum(term.reshape(count // 8, 8, 128), axis=0)
            row = REACH + 3 * j + m
            out[row : row + 1] = jnp.sum(total, axis=0, keepdims=True)


def by_rows(group, out, rows):
    def place(ring, pair, first, count):
        start = group.slot(ring, pair) * rows + first
        return out.at[pl.ds(pl.multiple_of(start, count), count)]

    return place


def by_strip(out, part):
    def place(ring, pair, first, count):
        return out.at[pl.ds(pl.multiple_of(pair * part + first, count), count), lanes_at(ring * 128)]

    return place


def marks(tok, q, vocab):
    inside = jnp.clip(q, 0, 4 * RING - 1)
    ids = tok[inside // 2, pl.ds(inside % 2, 1)]
    ids = jnp.where(q == inside, ids, -1)
    return jnp.where(lax.broadcasted_iota(jnp.int32, (vocab, 128), 0) == ids, 1.0, 0.0).astype(BF16)


def main_kernel(
    emb_ref, w_ref, w_far, cot_ref, tok_ref, w_proj, taps0, kern0, taps1, kern1,
    emb_out, inv_out, tok_out, e_all, gated_all, proj0, filtered0, x_all, gp_all, sums_all,
    part, crossed, half_out, piece, table, prod0, shifts, gated0, first_rows, total, x_block,
    wv, gg, arrived, returned, all_ref, x_col, square, inv_rows, gp_out, gpb, gated_out, stats, stat_own, block, sums_own, gf, prod,
    kg, pp, query, filtered, gprod, gs, ptail, qtail, ghead, gfar, sfar, gfpad, row_sum, qsend, gsend, *rest,
):
    pair_bufs, ring_bufs = rest[: len(PAIR)], rest[len(PAIR) : -2]
    send, recv = rest[-2:]
    barrier = pltpu.get_barrier_semaphore()
    ctx, dp = Group("ctx"), Group("dp")
    partner, apart = crossing()
    n = 2 * RING
    me = lax.axis_index("dp")
    place = lax.axis_index("ctx")
    others = [{"dp": (me + k) % n} for k in range(1, n)]
    after, before = {"ctx": (place + 1) % n}, {"ctx": (place + n - 1) % n}
    beyond = {"ctx": (place + n - 1 + 2 * ctx.pair) % n}
    opposite = {"section": 1 - lax.axis_index("section")}
    greet(ctx.neighbours() + [beyond] + others + [other_section(), opposite], barrier)

    @pl.when(apart)
    def _():
        greet([partner], barrier)

    pl.semaphore_wait(barrier, n + 5 + jnp.where(apart, 1, 0))
    lane = 128
    strips = RING
    common = Pool(send, recv)
    cross_sem = common.take(1)[0]
    same_sem = common.take(1)[0]
    pair_sems = common.take(2)
    relay = common.take(3)
    forth = pltpu.make_async_remote_copy(
        src_ref=x_block, dst_ref=arrived, send_sem=relay[0][0], recv_sem=relay[0][1],
        device_id=other_section(), device_id_type=MESH,
    )
    back = pltpu.make_async_remote_copy(
        src_ref=block, dst_ref=returned, send_sem=relay[1][0], recv_sem=relay[1][1],
        device_id=other_section(), device_id_type=MESH,
    )
    straight = pltpu.make_async_remote_copy(
        src_ref=x_block, dst_ref=x_col, send_sem=relay[2][0], recv_sem=relay[2][1],
        device_id=opposite, device_id_type=MESH,
    )

    @pl.when(section_is(0))
    def _():
        pool = Pool(send, recv)
        pool.count = common.count
        tokens = Gather(ctx, tok_ref, tok_out, pool, False)
        tokens.start()
        spread = pool.take(n - 1)
        share = piece.shape[0]
        share_of = lambda k: emb_ref.at[pl.ds(pl.multiple_of(k * share, share), share)]
        keep = pltpu.make_async_copy(share_of(me), piece, same_sem[0])
        copies = [
            pltpu.make_async_remote_copy(
                src_ref=share_of((me + k + 1) % n), dst_ref=piece, send_sem=spread[k][0],
                recv_sem=cross_sem[1], device_id=device, device_id_type=MESH,
            )
            for k, device in enumerate(others)
        ]

        @pl.when(jnp.logical_not(apart))
        def _():
            for copy in copies:
                copy.start()
            keep.start()
            keep.wait()

        @pl.when(apart)
        def _():
            copies[0].wait_recv()

        table_rows = Gather(dp, piece, emb_out, pool, True)
        table_rows.start()
        tokens.middle()
        table_rows.middle()
        table_rows.finish()

        @pl.when(jnp.logical_not(apart))
        def _():
            for copy in copies:
                copy.wait_send()

        vocab, width = emb_ref.shape
        hold = vocab // 2
        for core in range(2):
            values = emb_out[core * RING : (core + 1) * RING].reshape(hold, width).astype(F32)
            square = jnp.broadcast_to(jnp.sum(values * values, axis=1, keepdims=True), (hold, lane)).astype(BF16)
            for strip in range(strips):
                part[strip * 2 + core, :, 3 * lane :] = square

        @pl.loop(0, 3 * strips)
        def _(k):
            strip, m = k // 3, k % 3
            columns = pl.ds(pl.multiple_of(m * strips * lane + strip * lane, lane), lane)
            product = jnp.dot(emb_out[...].reshape(vocab, width), w_ref[:, columns], preferred_element_type=F32).astype(BF16)
            to = pl.ds(pl.multiple_of(m * lane, lane), lane)
            part[strip * 2, :, to] = product[:hold]
            part[strip * 2 + 1, :, to] = product[hold:]

        PairThenRing(ctx, part, pool, pair_bufs).run(half_out)
        here = pl.ds(pl.multiple_of(ctx.pair * hold, hold), hold)
        whole = half_out[...]
        inv = lax.rsqrt(whole[:, 3 * lane :] / (width * 2 * RING) + EPSILON)
        inv_out[here] = inv
        for m in range(3):
            table[here, m * lane : (m + 1) * lane] = (whole[:, m * lane : (m + 1) * lane] * inv).astype(BF16)
        mate = ctx.at(ctx.ring, ctx.mate)
        a = remote(inv_out.at[here], inv_out.at[here], pair_sems[0], mate)
        b = remote(table.at[here], table.at[here], pair_sems[1], mate)
        tokens.finish()
        a.wait()
        b.wait()


        @pl.loop(0, (BACK + 1280) // 128)
        def _(c):
            hot = marks(tok_out, ctx.pair * (n * 128 // 128) - BACK // 128 + c, vocab)
            proj0[pl.ds(pl.multiple_of(c * 128, 128), 128)] = dot(hot, table[...], TRANS_A)

        for k in range(2):
            hot = marks(tok_out, 2 * me + k, vocab)
            first_rows[k * 128 : (k + 1) * 128] = dot(hot, emb_out[...].reshape(vocab, width), TRANS_A).astype(BF16)
        span = gated0.shape[0]
        mix_first(proj0, taps0, kern0, filtered0, prod0, shifts, gated0, span)
        job = Gather(ctx, gated0, gated_all, pool, False, by_strip(gated_all, span))
        job.start()
        job.middle()
        job.finish()
        rows = x_block.shape[0]

        def produce(slot):
            here = pl.ds(pl.multiple_of(slot * rows, rows), rows)
            part[slot] = dot(gated_all[here], w_proj[...]).astype(BF16)

        RingThenPair(dp, part, pool, ring_bufs).run(total, [first_rows], produce)
        x_block[...] = total[...].astype(BF16)
        forth.start()
        straight.start()
        back.wait_recv()
        gather = Gather(dp, returned, e_all, pool, True)
        gather.start()
        gather.middle()
        gather.finish()
        forth.wait_send()
        straight.wait_send()

    @pl.when(section_is(1))
    def _():
        pool = Pool(send, recv)
        pool.count = common.count
        rows, width = gg.shape
        me = lax.axis_index("ctx")
        cot = cot_ref
        weights = Gather(ctx, w_far, wv, pool, False)
        there = pltpu.make_async_remote_copy(
            src_ref=cot_ref, dst_ref=crossed, send_sem=cross_sem[0], recv_sem=cross_sem[1],
            device_id=partner, device_id_type=MESH,
        )
        here = pltpu.make_async_copy(cot_ref, crossed, same_sem[0])
        pl.when(apart)(there.start)
        pl.when(jnp.logical_not(apart))(here.start)
        pl.when(apart)(there.wait)
        pl.when(jnp.logical_not(apart))(here.wait)
        weights.start()
        cots = Gather(dp, crossed, e_all, pool, True)
        cots.start()
        cots.middle()
        cots.finish()
        weights.middle()
        weights.finish()

        for k in range(n):
            part[k] = dot(e_all[k], w_proj[...], TRANS_B).astype(BF16)
        PairThenRing(ctx, part, pool, pair_bufs).run(gg)
        sums_own[REACH:] = jnp.zeros((16, width), F32)
        forth.wait_recv()
        gather = Gather(dp, arrived, all_ref, pool, True)
        gather.start()

        def use(ref, slot, begin=False):
            values = ref[...]
            for m in range(3):
                ml = slice(m * width, (m + 1) * width)
                term = dot(values, wv[slot, :, ml])
                pp[8:, ml] = term if begin else pp[8:, ml] + term
            term = jnp.zeros((rows, 128), F32)
            for g in range(width // 128):
                v = values[:, g * 128 : (g + 1) * 128].astype(F32)
                term = term + v * v
            square[...] = term if begin else square[...] + term

        use(arrived, dp.slot(dp.ring, dp.pair), True)
        gather.middle()
        for ring, pair in ((dp.left, dp.pair), (dp.right, dp.pair), (dp.ring, dp.mate), (dp.left, dp.mate), (dp.right, dp.mate)):
            use(gather.block(ring, pair), dp.slot(ring, pair))
        gather.finish()
        for pair in (dp.pair, dp.mate):
            use(gather.block(dp.across, pair), dp.slot(dp.across, pair))
        inv = lax.rsqrt(jnp.sum(square[...], axis=1, keepdims=True) / (width * n) + EPSILON)
        inv_rows[...] = jnp.broadcast_to(inv, (rows, 128))
        for a, count in chunks(0, rows, 32):
            pp[8 + a : 8 + a + count] = pp[8 + a : 8 + a + count] * inv_rows[a : a + count, :1]

        sems = pool.take(4)
        a_copy = remote(pp.at[pl.ds(rows, 8)], ptail, sems[0], after)

        def products(a, count, group):
            tl = lanes_at(group * 128)
            k = short_rows(pp, taps1, 1, a, count, lanes_at(width + group * 128), tl)
            v = short_rows(pp, taps1, 2, a, count, lanes_at(2 * width + group * 128), tl)
            return k * v

        @pl.loop(0, 4)
        def _(group):
            tl = lanes_at(group * 128)
            for a, count in chunks(rows // 2, rows, 64):
                value = products(8 + a, count, group)
                prod[REACH + a : REACH + a + count, tl] = value
                qsend[a - rows // 2 : a - rows // 2 + count, tl] = value.astype(BF16)

        b_copy = remote(qsend, qtail, sems[1], after)
        a_copy.wait_recv()
        pp[0:8] = jnp.where(me > 0, ptail[...], 0.0)

        @pl.loop(0, 4)
        def _(group):
            tl = lanes_at(group * 128)
            for a, count in chunks(0, rows, 64):
                value = short_rows(pp, taps1, 0, 8 + a, count, tl, tl)
                query[a : a + count, tl] = value
                value = value * gg[a : a + count, tl]
                gf[a : a + count, tl] = value
                gfpad[a : a + count, tl] = value
                if a < REACH:
                    ghead[a : a + count, tl] = value.astype(BF16)
            for a, count in chunks(0, rows // 2, 64):
                prod[REACH + a : REACH + a + count, tl] = products(8 + a, count, group)

        c_copy = remote(ghead, gfar, sems[2], before)
        b_copy.wait_recv()
        for a, count in chunks(0, REACH, 32):
            prod[a : a + count] = jnp.where(me > 0, qtail[a : a + count].astype(F32), 0.0)

        @pl.loop(0, 4)
        def _(group):
            tl = lanes_at(group * 128)
            shifted(shifts, prod, 1, rows + REACH - 8, tl)
            kg[...] = kern1[:, tl]
            fir(shifts, kg, ALL, filtered, tl, rows // 8, 8, True)
            for a, count in chunks(0, rows, 64):
                gated_out[a : a + count, tl] = (query[a : a + count, tl] * filtered[a : a + count, tl]).astype(BF16)

        near = Gather(ctx, gated_out, gated_all, pool, False, by_rows(ctx, gated_all, rows))
        near.start()
        c_copy.wait_recv()
        for a, count in chunks(0, REACH, 32):
            gfpad[rows + a : rows + a + count] = jnp.where(me < n - 1, gfar[a : a + count].astype(F32), 0.0)

        @pl.loop(0, 4)
        def _(group):
            tl = lanes_at(group * 128)
            shifted(shifts, gfpad, 0, rows + REACH - 8, tl)
            kg[...] = kern1[:, tl]
            fir(shifts, kg, ALL, gprod, tl, rows // 8, 8, False)
            for a, count in chunks(0, rows, 64):
                here = slice(a, a + count)
                gs[here, tl] = gg[here, tl] * filtered[here, tl]
                k = short_rows(pp, taps1, 1, 8 + a, count, lanes_at(width + group * 128), tl)
                v = short_rows(pp, taps1, 2, 8 + a, count, lanes_at(2 * width + group * 128), tl)
                gs[here, lanes_at(width + group * 128)] = gprod[here, tl] * v
                gs[here, lanes_at(2 * width + group * 128)] = gprod[here, tl] * k

        for m in range(3):
            gsend[:, m * width : (m + 1) * width] = gs[0:8, m * width : (m + 1) * width]
        d_copy = remote(gsend, sfar, sems[3], before)
        d_copy.wait_recv()
        gs[rows : rows + 8] = jnp.where(me < n - 1, sfar[...], 0.0)
        row_sum[...] = jnp.zeros_like(row_sum)

        @pl.loop(0, 4)
        def _(group):
            tl = lanes_at(group * 128)
            for m in range(3):
                ml = lanes_at(m * width + group * 128)
                sums = [jnp.zeros((8, 128), F32) for _ in range(3)]
                for a, count in chunks(0, rows, 64):
                    grad = taps1[m : m + 1, tl] * gs[a : a + count, ml]
                    for j in (1, 2):
                        grad = grad + taps1[3 * j + m : 3 * j + m + 1, tl] * gs[a + j : a + j + count, ml]
                    gpb[a : a + count, ml] = grad.astype(BF16)
                    gp_out[a : a + count, ml] = (grad * inv_rows[a : a + count]).astype(BF16)
                    row_sum[a : a + count] += grad * pp[8 + a : 8 + a + count, ml]
                    for j in range(3):
                        term = gs[a : a + count, ml] * pp[8 - j + a : 8 - j + a + count, ml]
                        sums[j] = sums[j] + jnp.sum(term.reshape(count // 8, 8, 128), axis=0)
                for j in range(3):
                    sums_own[REACH + 3 * j + m : REACH + 3 * j + m + 1, tl] = jnp.sum(sums[j], axis=0, keepdims=True)

        eye = lax.broadcasted_iota(jnp.int32, (128, 128), 0) == lax.broadcasted_iota(jnp.int32, (128, 128), 1)
        stat_own[...] = jnp.zeros_like(stat_own)
        for k in range(rows // 128):
            column = jnp.sum(row_sum[k * 128 : (k + 1) * 128], axis=1, keepdims=True)
            line = jnp.sum(jnp.where(eye, jnp.broadcast_to(column, (128, 128)), 0.0), axis=0, keepdims=True)
            stat_own[k : k + 1] = line
        grads = Gather(ctx, gp_out, gp_all, pool, False)
        grads.start()
        stat = Gather(dp, stat_own, stats, pool, True)
        stat.start()

        def produce(slot):
            part[slot] = dot(gpb[...], wv[slot], TRANS_B).astype(BF16)

        RingThenPair(dp, part, pool, ring_bufs).run(total, produce=produce)
        stat.middle()
        stat.finish()
        summed = stats[0]
        for k in range(1, n):
            summed = summed + stats[k]
        for k in range(rows // 128):
            here = pl.ds(k * 128, 128)
            line = jnp.broadcast_to(summed[k : k + 1], (128, 128))
            scalar = jnp.sum(jnp.where(eye, line, 0.0), axis=1, keepdims=True)
            inv = inv_rows[here, :1]
            block[here] = (
                cot[here].astype(F32)
                + inv * total[here]
                - arrived[here].astype(F32) * (inv * inv * scalar / (width * n))
            ).astype(BF16)
        back.start()
        straight.wait_recv()
        columns = Gather(dp, x_col, x_all, pool, True)
        columns.start()
        near.middle()

        @pl.loop(0, 4)
        def _(group):
            tl = lanes_at(group * 128)
            shifted(shifts, prod, 1, rows + REACH - 8, tl)
            lags(shifts, gf, tl, sums_own, tl, rows // 8)

        taps_job = Gather(ctx, sums_own, sums_all, pool, False)
        taps_job.start()
        jobs = [columns, grads, taps_job]
        for job in jobs:
            job.middle()
        for job in [near] + jobs:
            job.finish()
        for copy in (a_copy, b_copy, c_copy, d_copy):
            copy.wait_send()
        back.wait_send()


PAIR = (None,) * 5


def end_kernel(
    e_all, w_proj, gated_all, proj, taps, kern, filtered, tok, gtab_all, taps_all, grad_out,
    part_ref, gg, gf, gprod, gs, prod, shifts, gp, sum_ref, gtab, sums, got, block, *rest,
):
    bufs, (send, recv) = rest[:-2], rest[-2:]
    barrier = pltpu.get_barrier_semaphore()
    ctx = Group("ctx")

    def outer():
        count, rows, _ = e_all.shape
        grad_out[...] = jnp.zeros_like(grad_out)

        @pl.loop(0, count)
        def _(k):
            here = pl.ds(pl.multiple_of(k * rows, rows), rows)
            grad_out[...] += dot(gated_all[here], e_all[k], TRANS_A)

    @pl.when(section_is(0))
    def _():
        greet(ctx.neighbours(), barrier)
        pl.semaphore_wait(barrier, 3)
        pool = Pool(send, recv)
        count, rows, _ = e_all.shape
        for k in range(count):
            product = dot(e_all[k], w_proj[...], TRANS_B).astype(BF16)
            core, first = divmod(k * rows, count // 2 * rows)
            for strip in range(RING):
                part = product[:, strip * 128 : (strip + 1) * 128]
                part_ref[strip * 2 + core, first : first + rows] = part
                if core == 1 and first == 0:
                    part_ref[strip * 2, count // 2 * rows : AHEAD] = part[: AHEAD - count // 2 * rows]
        over = AHEAD - count // 2 * rows
        for strip in range(RING):
            part_ref[strip * 2 + 1, count // 2 * rows : AHEAD] = jnp.zeros((over, 128), BF16)
        PairThenRing(ctx, part_ref, pool, bufs).run(gg)

        sem = pool.take(1)[0]
        hold = got.shape[0]
        part = gp.shape[0]
        mix_back(gg, proj, taps, kern, filtered, gf, gprod, gs, shifts, gp, part)

        sum_ref[...] = jnp.zeros_like(sum_ref)

        @pl.loop(0, part // 128)
        def _(c):
            hot = marks(tok, ctx.pair * (part // 128) + c, sum_ref.shape[0])
            sum_ref[...] += dot(hot, gp[pl.ds(pl.multiple_of(c * 128, 128), 128)])

        gtab[...] = sum_ref[...].astype(BF16)

        halves = lambda p: gtab.at[pl.ds(pl.multiple_of(p * hold, hold), hold)]
        copy = remote(halves(ctx.mate), got, sem, ctx.at(ctx.ring, ctx.mate))
        copy.wait()
        add_into(block, [halves(ctx.pair), got])
        table = Gather(ctx, block, gtab_all, pool, False)
        table.start()
        outer()
        mix_sums(gf, proj, taps, gs, prod, shifts, sums, part)
        job = Gather(ctx, sums, taps_all, pool, False)
        job.start()
        table.middle()
        job.middle()
        table.finish()
        job.finish()

    @pl.when(section_is(1))
    def _():
        outer()


def dot(a, b, dims=(((1,), (0,)), ((), ()))):
    return lax.dot_general(a, b, dims, preferred_element_type=F32)


TRANS_B = (((1,), (1,)), ((), ()))
TRANS_A = (((0,), (0,)), ((), ()))


def local(
    token_ids, embedding, project_in, short_taps, filter_taps, decay_rates, project_out, cotangent
):
    section_zero = lax.axis_index("section") == 0
    n = lax.axis_size("ctx")
    vocab = embedding.shape[0]
    rows = token_ids.shape[0]
    seq = rows * n
    part = seq // 2
    width = embedding.shape[1]
    chans = project_in.shape[3]
    lane = chans // RING
    taps_all = short_taps[0]
    filter_all = filter_taps[0]
    tap_count = filter_all.shape[0]
    strip = lax.axis_index("ctx") // 2

    w_flat = project_in[0].reshape(width, 3 * chans)
    w_out = project_out[0]
    positions = jnp.arange(tap_count).astype(F32)
    damping_all = jnp.exp(-decay_rates[0][None, :] * positions[:, None] / tap_count)
    kernel_all = filter_all * damping_all

    def strip_of(a):
        return lax.dynamic_slice_in_dim(a, strip * lane, lane, a.ndim - 1)

    taps0, kernel0 = strip_of(taps_all), strip_of(kernel_all)

    taps0 = taps0.reshape(9, lane)
    taps1 = taps_all.reshape(9, chans)
    own_tokens = jnp.tile(token_ids.reshape(rows // lane, lane), (16 * lane // rows, 1))
    emb, inv_table, tokens, e_all, gated_all, proj0, filtered0, x_all, gp_all, sums1 = call(
        main_kernel,
        1,
        [
            ((n, vocab // n, width), BF16),
            ((vocab, lane), F32),
            ((n, 16, lane), jnp.int32),
            ((n, rows, width), BF16),
            ((seq, chans), BF16),
            ((BACK + 1280, 3 * lane), F32),
            ((KEPT, lane), F32),
            ((n, rows, width), BF16),
            ((n, rows, 3 * chans), BF16),
            ((n, 144, chans), F32),
        ],
        [
            pltpu.VMEM(shape, dtype)
            for shape, dtype in (
                ((n, rows, width), BF16),
                ((rows, width), BF16),
                ((vocab // 2, 4 * lane), F32),
                ((vocab // n, width), BF16),
                ((vocab, 3 * lane), BF16),
                ((BACK + AHEAD, lane), F32),
                ((8, KEPT + REACH, lane), F32),
                ((part, lane), BF16),
                ((rows, width), BF16),
                ((rows, width), F32),
                ((rows, width), BF16),
                ((n, width, 3 * chans), BF16),
                ((rows, chans), F32),
                ((rows, width), BF16),
                ((rows, width), BF16),
                ((n, rows, width), BF16),
                ((rows, width), BF16),
                ((rows, 128), F32),
                ((rows, 128), F32),
                ((rows, 3 * chans), BF16),
                ((rows, 3 * chans), BF16),
                ((rows, chans), BF16),
                ((n, 16, 128), F32),
                ((16, 128), F32),
                ((rows, width), BF16),
                ((144, chans), F32),
                ((rows, chans), F32),
                ((rows + REACH, chans), F32),
                ((REACH, 128), F32),
                ((rows + 8, 3 * chans), F32),
                ((rows, chans), F32),
                ((rows, chans), F32),
                ((rows, chans), F32),
                ((rows + 8, 3 * chans), F32),
                ((8, 3 * chans), F32),
                ((REACH, chans), BF16),
                ((REACH, chans), BF16),
                ((REACH, chans), BF16),
                ((8, 3 * chans), F32),
                ((rows + REACH, chans), F32),
                ((rows, 128), F32),
                ((REACH, chans), BF16),
                ((8, 3 * chans), F32),
            )
        ]
        + PairThenRing.scratch(rows, width)
        + RingThenPair.scratch(rows, width),
        128,
        embedding, w_flat, w_flat, cotangent, own_tokens, w_out, taps0, kernel0, taps1, kernel_all,
        in_specs=[VMEM, VMEM, ANY] + [VMEM] * 7,
        out_specs=[VMEM] * 8 + [ANY] * 2,
        name="main",
    )
    emb = emb.reshape(vocab, width)
    gtab, sums0, grad_out = call(
        end_kernel,
        2,
        [((n, vocab // 2, 3 * lane), BF16), ((n, 144, lane), F32), ((chans, width), F32)],
        [
            pltpu.VMEM((n, AHEAD, lane), BF16),
            pltpu.VMEM((AHEAD, lane), F32),
            pltpu.VMEM((AHEAD, lane), F32),
            pltpu.VMEM((KEPT, lane), F32),
            pltpu.VMEM((3, KEPT, lane), F32),
            pltpu.VMEM((BACK + AHEAD, lane), F32),
            pltpu.VMEM((8, KEPT + REACH, lane), F32),
            pltpu.VMEM((part, 3 * lane), BF16),
            pltpu.VMEM((vocab, 3 * lane), F32),
            pltpu.VMEM((vocab, 3 * lane), BF16),
            pltpu.VMEM((144, lane), F32),
            pltpu.VMEM((vocab // 2, 3 * lane), BF16),
            pltpu.VMEM((vocab // 2, 3 * lane), BF16),
        ]
        + PairThenRing.scratch(AHEAD, lane),
        40,
        e_all, w_out, gated_all, proj0, taps0, kernel0, filtered0, tokens,
        name="end",
    )

    def end0():
        table_rows = jnp.transpose(gtab.reshape(RING, 2, vocab // 2, 3, lane), (1, 2, 3, 0, 4))
        normed_table = (emb.astype(F32) * inv_table[:, :1]).astype(BF16)
        sums = sums0.reshape(RING, 2, 144, lane).sum(axis=1)
        return (
            dot(normed_table, table_rows.reshape(vocab, 3 * chans), TRANS_A),
            jnp.transpose(sums, (1, 0, 2)).reshape(144, chans),
        )

    def end1():
        return (
            dot(x_all.reshape(seq, width), gp_all.reshape(seq, 3 * chans), TRANS_A),
            sums1.sum(axis=0),
        )

    grad_in, sums = lax.cond(section_zero, end0, end1)
    grad_in = grad_in.reshape(width, 3, chans)
    gk, gt = sums[:tap_count], sums[tap_count : tap_count + 9].reshape(3, 3, chans)
    grad_filter = gk * damping_all
    grad_decay = -jnp.sum(gk * kernel_all * positions[:, None], axis=0) / tap_count
    return (grad_in[None], grad_out[None], grad_filter[None], grad_decay[None], gt[None])


def solution(mesh):
    return jax.shard_map(
        local,
        mesh=mesh,
        in_specs=(
            P("ctx"),
            P(None, "dp"),
            P("section", "ctx", None, "dp"),
            P("section", None, None, "dp"),
            P("section", None, "dp"),
            P("section", "dp"),
            P("section", "dp", "ctx"),
            P("ctx", "dp"),
        ),
        out_specs=(
            P("section", "ctx", None, "dp"),
            P("section", "dp", "ctx"),
            P("section", None, "dp"),
            P("section", "dp"),
            P("section", None, None, "dp"),
        ),
        check_vma=False,
    )
```

```python
import functools

import jax
import jax.numpy as jnp
from jax import lax
from jax.experimental import pallas as pl
from jax.experimental.pallas import tpu as pltpu
from jax.sharding import PartitionSpec as P

EPSILON = 1e-06
F32 = jnp.float32
BF16 = jnp.bfloat16
MESH = pl.DeviceIdType.MESH
BACK = 256
AHEAD = 1184
KEPT = 1040
RING = 4
REACH = 128


class Group:
    def __init__(self, axis):
        self.axis = axis
        me = lax.axis_index(axis)
        if axis == "ctx":
            self.ring, self.pair = me // 2, me % 2
        else:
            self.ring, self.pair = me % RING, me // RING
        self.right = (self.ring + 1) % RING
        self.left = (self.ring + RING - 1) % RING
        self.across = (self.ring + 2) % RING
        self.mate = 1 - self.pair

    def slot(self, ring, pair):
        return ring * 2 + pair if self.axis == "ctx" else pair * RING + ring

    def at(self, ring, pair):
        return {self.axis: self.slot(ring, pair)}

    def neighbours(self):
        return [
            self.at(self.right, self.pair),
            self.at(self.left, self.pair),
            self.at(self.ring, self.mate),
        ]


class Pool:
    def __init__(self, send, recv):
        self.send, self.recv, self.count = send, recv, 0

    def take(self, k):
        first = self.count
        self.count += k
        return [(self.send.at[first + i], self.recv.at[first + i]) for i in range(k)]


def remote(src, dst, sems, device):
    copy = pltpu.make_async_remote_copy(
        src_ref=src,
        dst_ref=dst,
        send_sem=sems[0],
        recv_sem=sems[1],
        device_id=device,
        device_id_type=MESH,
    )
    copy.start()
    return copy


def greet(devices, barrier):
    for device in devices:
        pl.semaphore_signal(barrier, inc=1, device_id=device, device_id_type=MESH)


class Gather:
    def __init__(self, group, src, out, pool, pair_first, place=None):
        self.g, self.src, self.out, self.pair_first = group, src, out, pair_first
        self.sems = pool.take(9)
        self.own = pool.take(1)[0]
        self.rows = src.shape[0]
        self.half = self.rows // 2
        self.place = place or (lambda ring, pair, first, rows: out.at[group.slot(ring, pair), pl.ds(first, rows)])

    def block(self, ring, pair):
        return self.place(ring, pair, 0, self.rows)

    def part(self, ring, pair, second):
        return self.place(ring, pair, self.half * second, self.half)

    def start(self):
        g, s = self.g, self.sems
        mine = self.block(g.ring, g.pair)
        right, left, mate = g.neighbours()
        self.local = pltpu.make_async_copy(self.src, mine, self.own[0])
        self.local.start()
        first = remote(self.src, mine, s[0], mate)
        self.copies = [first, remote(self.src, mine, s[1], right), remote(self.src, mine, s[2], left)]

    def turn(self, pair, a, b, c, d):
        g, s = self.g, self.sems
        right, left, mate = g.neighbours()
        more = []
        a.wait_recv()
        part = self.part(g.left, pair, 0)
        more.append(remote(part, part, s[c], right))
        if not self.pair_first:
            block = self.block(g.left, pair)
            more.append(remote(block, block, s[5], mate))
        b.wait_recv()
        part = self.part(g.right, pair, 1)
        more.append(remote(part, part, s[d], left))
        if not self.pair_first:
            block = self.block(g.right, pair)
            more.append(remote(block, block, s[6], mate))
        return more

    def pass_on(self):
        self.passed = self.turn(self.g.pair, self.copies[1], self.copies[2], 3, 4)

    passed = None

    def middle(self):
        g, s = self.g, self.sems
        right, left, mate = g.neighbours()
        mate_copy, to_right, to_left = self.copies
        if self.passed is None:
            self.pass_on()
        rest = self.passed
        self.sent = list(self.copies) + rest
        if self.pair_first:
            self.late = list(rest)
            mate_copy.wait_recv()
            block = self.block(g.ring, g.mate)
            a = remote(block, block, s[5], right)
            b = remote(block, block, s[6], left)
            more = self.turn(g.mate, a, b, 7, 8)
            self.sent += [a, b] + more
            self.late += more
        else:
            rest[0].wait_recv()
            rest[2].wait_recv()
            block = self.block(g.across, g.pair)
            last = remote(block, block, s[7], mate)
            self.sent.append(last)
            self.late = [mate_copy, rest[1], rest[3], last]

    def finish(self):
        for copy in self.late:
            copy.wait_recv()
        for copy in self.sent:
            copy.wait_send()
        self.local.wait()


def add_into(out, terms, rows=64):
    @pl.loop(0, out.shape[0] // rows)
    def _(step):
        here = pl.ds(pl.multiple_of(step * rows, rows), rows)
        total = terms[0][here].astype(F32)
        for term in terms[1:]:
            total = total + term[here].astype(F32)
        out[here] = total.astype(out.dtype)


def rows_step(count):
    for rows in (64, 48, 37 * 16, 32, 16):
        if count % rows == 0:
            return rows if rows != 37 * 16 else 16
    return 16


class Around:
    def __init__(self, group, pool, bufs):
        self.g = group
        self.s = pool.take(6)
        self.rel, self.merged, self.came = bufs
        self.half = self.rel.shape[1]

    @staticmethod
    def scratch(rows, lanes):
        half = rows // 2
        return [
            pltpu.VMEM((2, half, lanes), BF16),
            pltpu.VMEM((2, half, lanes), BF16),
            pltpu.VMEM((2, 2, half, lanes), BF16),
        ]

    def halves(self, ref):
        return ref.at[pl.ds(0, self.half)], ref.at[pl.ds(self.half, self.half)]

    def send_across(self, block):
        right, left, _ = self.g.neighbours()
        a, b = self.halves(block)
        self.copies = [remote(a, self.rel.at[0], self.s[0], right), remote(b, self.rel.at[1], self.s[1], left)]

    def send_near(self, to_right, to_left):
        right, left, _ = self.g.neighbours()
        self.to_right, self.to_left = to_right, to_left
        b = self.halves(to_right)[1]
        a = self.halves(to_left)[0]
        self.copies += [
            remote(b, self.came.at[0, 1], self.s[2], right),
            remote(a, self.came.at[1, 0], self.s[3], left),
        ]

    def merge(self):
        right, left, _ = self.g.neighbours()
        step = rows_step(self.half)
        self.copies[0].wait_recv()
        add_into(self.merged.at[0], [self.halves(self.to_right)[0], self.rel.at[0]], step)
        self.copies.append(remote(self.merged.at[0], self.came.at[0, 0], self.s[4], right))
        self.copies[1].wait_recv()
        add_into(self.merged.at[1], [self.halves(self.to_left)[1], self.rel.at[1]], step)
        self.copies.append(remote(self.merged.at[1], self.came.at[1, 1], self.s[5], left))

    def collect(self, out, own):
        step = rows_step(self.half)
        for copy in self.copies[2:]:
            copy.wait_recv()
        for h in range(2):
            piece = pl.ds(h * self.half, self.half)
            add_into(
                out.at[piece],
                [ref.at[piece] for ref in own] + [self.came.at[0, h], self.came.at[1, h]],
                step,
            )

    def finish(self):
        for copy in self.copies:
            copy.wait_send()


class PairThenRing:
    def __init__(self, group, inp, pool, bufs):
        self.g, self.inp = group, inp
        self.got, self.sums = bufs[:2]
        self.ring = Around(group, pool, bufs[2:])
        self.s = pool.take(4)

    @staticmethod
    def scratch(rows, lanes):
        return [pltpu.VMEM((4, rows, lanes), BF16), pltpu.VMEM((4, rows, lanes), BF16)] + Around.scratch(rows, lanes)

    def run(self, out):
        g = self.g
        mate = g.at(g.ring, g.mate)
        order = [g.across, g.right, g.left, g.ring]
        copies = [
            remote(self.inp.at[g.slot(r, g.mate)], self.got.at[k], self.s[k], mate) for k, r in enumerate(order)
        ]
        step = rows_step(self.inp.shape[1])

        def pair_sum(k):
            copies[k].wait_recv()
            add_into(self.sums.at[k], [self.inp.at[g.slot(order[k], g.pair)], self.got.at[k]], step)

        pair_sum(0)
        self.ring.send_across(self.sums.at[0])
        pair_sum(1)
        pair_sum(2)
        self.ring.send_near(self.sums.at[1], self.sums.at[2])
        copies[3].wait_recv()
        self.ring.merge()
        self.ring.collect(out, [self.inp.at[g.slot(g.ring, g.pair)], self.got.at[3]])
        self.ring.finish()
        for copy in copies:
            copy.wait_send()


class RingThenPair:
    def __init__(self, group, inp, pool, bufs):
        self.g, self.inp = group, inp
        self.far, self.got = bufs[:2]
        self.rings = [Around(group, pool, bufs[2:5]), Around(group, pool, bufs[5:8])]
        self.s = pool.take(1)[0]

    @staticmethod
    def scratch(rows, lanes):
        return (
            [pltpu.VMEM((rows, lanes), BF16), pltpu.VMEM((rows, lanes), BF16)]
            + Around.scratch(rows, lanes)
            + Around.scratch(rows, lanes)
        )

    def run(self, out, extra=(), produce=lambda slot: None):
        g = self.g
        pairs = [g.mate, g.pair]
        blocks = lambda ring, pair: self.inp.at[g.slot(ring, pair)]
        for ring, pair in zip(self.rings, pairs):
            produce(g.slot(g.across, pair))
            ring.send_across(blocks(g.across, pair))
            produce(g.slot(g.right, pair))
            produce(g.slot(g.left, pair))
            ring.send_near(blocks(g.right, pair), blocks(g.left, pair))
            produce(g.slot(g.ring, pair))
        self.rings[0].merge()
        self.rings[1].merge()
        self.rings[0].collect(self.far, [blocks(g.ring, g.mate)])
        copy = remote(self.far, self.got, self.s, g.at(g.ring, g.mate))
        self.rings[1].collect(out, [blocks(g.ring, g.pair)])
        copy.wait_recv()
        add_into(out, [out, self.got] + list(extra), rows_step(out.shape[0]))
        copy.wait_send()
        for ring in self.rings:
            ring.finish()


ANY = pl.BlockSpec(memory_space=pl.ANY)
VMEM = pl.BlockSpec(memory_space=pltpu.VMEM)


def call(body, ident, outs, scratch, sems, *args, in_specs=None, out_specs=None, name=None, local=0):
    return pl.pallas_call(
        body,
        out_shape=[jax.ShapeDtypeStruct(shape, dtype) for shape, dtype in outs],
        in_specs=in_specs or [VMEM] * len(args),
        out_specs=out_specs or [VMEM] * len(outs),
        scratch_shapes=list(scratch)
        + [pltpu.SemaphoreType.DMA((sems,)), pltpu.SemaphoreType.DMA((sems,))]
        + ([pltpu.SemaphoreType.DMA((local,))] if local else []),
        compiler_params=pltpu.CompilerParams(
            collective_id=ident, has_side_effects=True, vmem_limit_bytes=60 * 1024 * 1024
        ),
        name=name,
    )(*args)


def section_is(k):
    return lax.axis_index("section") == k


def crossing():
    i, j = lax.axis_index("dp"), lax.axis_index("ctx")
    return {"dp": j, "ctx": i}, i != j


def other_section():
    i, j = lax.axis_index("dp"), lax.axis_index("ctx")
    return {"section": 1 - lax.axis_index("section"), "dp": j, "ctx": i}


def lanes_at(first):
    return pl.ds(pl.multiple_of(first, 128), 128)


def shifted(shifts, ref, start, rows, lanes):
    for r in range(8):
        for a in range(0, rows, 64):
            count = min(64, rows - a)
            shifts[r, a : a + count] = ref[start + r + a : start + r + a + count, lanes]


def fir(shifts, kern, lanes, out, out_lanes, tiles, block, backwards):
    @pl.loop(0, tiles // block)
    def _(b):
        first = pl.multiple_of(b * block * 8, 8)

        def step(r, totals):
            totals = list(totals)
            taps = []
            for q in range(REACH // 8):
                u = 8 * q + r
                taps.append(kern[pl.ds(REACH - 1 - u if backwards else u, 8, stride=0), lanes])
            for i in range(block + REACH // 8 - 1):
                x = shifts[r, pl.ds(first + 8 * i, 8)]
                for o in range(block):
                    if 0 <= i - o < REACH // 8:
                        totals[o] = totals[o] + taps[i - o] * x
            return tuple(totals)

        totals = lax.fori_loop(0, 8, step, tuple(jnp.zeros((8, 128), F32) for _ in range(block)))
        for o in range(block):
            out[pl.ds(first + 8 * o, 8), out_lanes] = totals[o]


def lags(shifts, ref, lanes, out, out_lanes, tiles):
    for r in range(8):

        def step(b, totals):
            totals = list(totals)
            first = pl.multiple_of(b * 32, 8)
            own = [ref[pl.ds(first + 8 * o, 8), lanes] for o in range(4)]
            for i in range(4 + REACH // 8 - 1):
                x = shifts[r, pl.ds(first + 8 * i, 8)]
                for o in range(4):
                    if 0 <= i - o < REACH // 8:
                        totals[i - o] = totals[i - o] + own[o] * x
            return tuple(totals)

        totals = lax.fori_loop(0, tiles // 4, step, tuple(jnp.zeros((8, 128), F32) for _ in range(REACH // 8)))
        for q in range(REACH // 8):
            row = REACH - 1 - (8 * q + r)
            out[row : row + 1, out_lanes] = jnp.sum(totals[q], axis=0, keepdims=True)


def chunks(first, last, size):
    for a in range(first, last, size):
        yield a, min(size, last - a)


def short_rows(ref, taps, m, a, count, lanes, tap_lanes):
    total = taps[m : m + 1, tap_lanes] * ref[a : a + count, lanes]
    for j in (1, 2):
        total = total + taps[3 * j + m : 3 * j + m + 1, tap_lanes] * ref[a - j : a - j + count, lanes]
    return total


ALL = slice(0, 128)


def stream(m):
    return slice(m * 128, (m + 1) * 128)


def mix_first(proj, taps, kern, filtered, prod, shifts, gated, part):
    for a, count in chunks(BACK - REACH, BACK + part, 64):
        prod[a : a + count] = short_rows(proj, taps, 1, a, count, stream(1), ALL) * short_rows(
            proj, taps, 2, a, count, stream(2), ALL
        )
    for a, count in chunks(BACK + part, BACK + AHEAD, 64):
        prod[a : a + count] = short_rows(proj, taps, 1, a, count, stream(1), ALL) * short_rows(
            proj, taps, 2, a, count, stream(2), ALL
        )
    shifted(shifts, prod, BACK - REACH + 1, KEPT + REACH, ALL)
    fir(shifts, kern, ALL, filtered, ALL, KEPT // 8, 10, True)
    for a, count in chunks(0, part, 64):
        query = short_rows(proj, taps, 0, BACK + a, count, stream(0), ALL)
        gated[a : a + count] = (query * filtered[a : a + count]).astype(BF16)


def mix_back(gg, proj, taps, kern, filtered, gf, gprod, gs, shifts, gp, part):
    for a, count in chunks(0, AHEAD, 64):
        gf[a : a + count] = gg[a : a + count] * short_rows(proj, taps, 0, BACK + a, count, stream(0), ALL)
    shifted(shifts, gf, 0, KEPT + REACH, ALL)
    fir(shifts, kern, ALL, gprod, ALL, KEPT // 8, 10, False)
    for a, count in chunks(0, KEPT, 64):
        here = slice(a, a + count)
        gs[0, here] = gg[here] * filtered[here]
        gs[1, here] = gprod[here] * short_rows(proj, taps, 2, BACK + a, count, stream(2), ALL)
        gs[2, here] = gprod[here] * short_rows(proj, taps, 1, BACK + a, count, stream(1), ALL)
    for m in range(3):
        for a, count in chunks(0, part, 64):
            total = taps[m : m + 1] * gs[m, a : a + count]
            for j in (1, 2):
                total = total + taps[3 * j + m : 3 * j + m + 1] * gs[m, a + j : a + j + count]
            gp[a : a + count, stream(m)] = total.astype(BF16)


def mix_sums(gf, proj, taps, gs, prod, shifts, out, part):
    for a, count in chunks(BACK - REACH, BACK + part + 8, 64):
        prod[a : a + count] = short_rows(proj, taps, 1, a, count, stream(1), ALL) * short_rows(
            proj, taps, 2, a, count, stream(2), ALL
        )
    shifted(shifts, prod, BACK - REACH + 1, part + REACH, ALL)
    lags(shifts, gf, ALL, out, ALL, part // 8)
    out[REACH:] = jnp.zeros((16, 128), F32)
    for m in range(3):
        for j in range(3):
            total = jnp.zeros((8, 128), F32)
            for a, count in chunks(0, part, 64):
                term = gs[m, a : a + count] * proj[BACK - j + a : BACK - j + a + count, stream(m)]
                total = total + jnp.sum(term.reshape(count // 8, 8, 128), axis=0)
            row = REACH + 3 * j + m
            out[row : row + 1] = jnp.sum(total, axis=0, keepdims=True)


def by_rows(group, out, rows):
    def place(ring, pair, first, count):
        start = group.slot(ring, pair) * rows + first
        return out.at[pl.ds(pl.multiple_of(start, count), count)]

    return place


def by_strip(out, part):
    def place(ring, pair, first, count):
        return out.at[pl.ds(pl.multiple_of(pair * part + first, count), count), lanes_at(ring * 128)]

    return place


def marks(tok, q, vocab):
    inside = jnp.clip(q, 0, 4 * RING - 1)
    ids = tok[inside // 2, pl.ds(inside % 2, 1)]
    ids = jnp.where(q == inside, ids, -1)
    return jnp.where(lax.broadcasted_iota(jnp.int32, (vocab, 128), 0) == ids, 1.0, 0.0).astype(BF16)


def sems_of(send, recv, k):
    return recv.at[k]


def use_rows(out, blocks, weights, gather, dp, own):
    term = lambda ref, slot: dot(ref[...], weights[slot], TRANS_B)
    slot = dp.slot(dp.ring, dp.pair)
    out[...] = term(own, slot)
    gather.middle()
    near = ((dp.left, dp.pair), (dp.right, dp.pair), (dp.ring, dp.mate), (dp.left, dp.mate), (dp.right, dp.mate))
    for ring, pair in near:
        slot = dp.slot(ring, pair)
        out[...] += term(blocks.at[slot], slot)
    gather.finish()
    for pair in (dp.pair, dp.mate):
        slot = dp.slot(dp.across, pair)
        out[...] += term(blocks.at[slot], slot)


def swap(pieces, sems, me):
    for k, (src, dst, to, sem, when) in enumerate(pieces):
        far = jnp.logical_and(when, to != me)
        near = jnp.logical_and(when, to == me)
        away = pltpu.make_async_remote_copy(
            src_ref=src, dst_ref=dst, send_sem=sems[k][0], recv_sem=sem, device_id={"ctx": to}, device_id_type=MESH
        )
        here = pltpu.make_async_copy(src, dst, sem)
        pl.when(far)(away.start)
        pl.when(near)(here.start)


def swapped(pieces, sems, me):
    for k, (src, dst, to, sem, when) in enumerate(pieces):
        away = pltpu.make_async_remote_copy(
            src_ref=src, dst_ref=dst, send_sem=sems[k][0], recv_sem=sem, device_id={"ctx": to}, device_id_type=MESH
        )
        pl.when(jnp.logical_and(when, to != me))(away.wait_send)


def main_kernel(
    emb_ref, w_ref, w_far, cot_ref, tok_ref, w_proj, wo_far, taps0, kern0, taps1, kern1,
    emb_out, inv_out, tok_out, e_all, gated_all, proj0, filtered0, x_all, gp_all, sums_all, gg_rows, e_col,
    part, crossed, half_out, piece, table, prod0, shifts, gated0, first_rows, total, x_block,
    wv, wo, gated_own, gg, arrived, returned, all_ref, x_col, square, inv_rows, gp_out, gpb, gated_out, stats, stat_own, block, sums_own, gf, prod,
    kg, pp, query, filtered, gprod, gs, ptail, qtail, ghead, gfar, sfar, gfpad, row_sum, qsend, gsend, *rest,
):
    pair_bufs, ring_bufs = rest[: len(PAIR)], rest[len(PAIR) : -2]
    send, recv = rest[-2:]
    barrier = pltpu.get_barrier_semaphore()
    ctx, dp = Group("ctx"), Group("dp")
    partner, apart = crossing()
    n = 2 * RING
    me = lax.axis_index("dp")
    place = lax.axis_index("ctx")
    others = [{"dp": (me + k) % n} for k in range(1, n)]
    after, before = {"ctx": (place + 1) % n}, {"ctx": (place + n - 1) % n}
    along = [{"ctx": (place + k) % n} for k in range(1, n)]
    opposite = {"section": 1 - lax.axis_index("section")}
    greet(along + others + [other_section(), opposite], barrier)

    @pl.when(apart)
    def _():
        greet([partner], barrier)

    pl.semaphore_wait(barrier, 2 * n + jnp.where(apart, 1, 0))
    lane = 128
    strips = RING
    common = Pool(send, recv)
    cross_sem = common.take(1)[0]
    same_sem = common.take(1)[0]
    pair_sems = common.take(2)
    relay = common.take(4)

    def handed(src, dst, k, device):
        return pltpu.make_async_remote_copy(
            src_ref=src, dst_ref=dst, send_sem=relay[k][0], recv_sem=relay[k][1],
            device_id=device, device_id_type=MESH,
        )

    forth = handed(x_block, arrived, 0, opposite)
    back = handed(block, returned, 1, opposite)
    x_over = handed(x_block, x_col, 2, other_section())
    e_over = handed(block, e_col, 3, other_section())

    @pl.when(section_is(0))
    def _():
        pool = Pool(send, recv)
        pool.count = common.count
        tokens = Gather(ctx, tok_ref, tok_out, pool, False)
        tokens.start()
        outs = Gather(ctx, wo_far, wo, pool, False)
        outs.start()
        spread = pool.take(n - 1)
        share = piece.shape[0]
        share_of = lambda k: emb_ref.at[pl.ds(pl.multiple_of(k * share, share), share)]
        keep = pltpu.make_async_copy(share_of(me), piece, same_sem[0])
        copies = [
            pltpu.make_async_remote_copy(
                src_ref=share_of((me + k + 1) % n), dst_ref=piece, send_sem=spread[k][0],
                recv_sem=cross_sem[1], device_id=device, device_id_type=MESH,
            )
            for k, device in enumerate(others)
        ]

        @pl.when(jnp.logical_not(apart))
        def _():
            for copy in copies:
                copy.start()
            keep.start()
            keep.wait()

        @pl.when(apart)
        def _():
            copies[0].wait_recv()

        table_rows = Gather(dp, piece, emb_out, pool, True)
        table_rows.start()
        tokens.middle()
        table_rows.middle()
        table_rows.finish()

        @pl.when(jnp.logical_not(apart))
        def _():
            for copy in copies:
                copy.wait_send()

        vocab, width = emb_ref.shape
        hold = vocab // 2
        for core in range(2):
            values = emb_out[core * RING : (core + 1) * RING].reshape(hold, width).astype(F32)
            square = jnp.broadcast_to(jnp.sum(values * values, axis=1, keepdims=True), (hold, lane)).astype(BF16)
            for strip in range(strips):
                part[strip * 2 + core, :, 3 * lane :] = square

        @pl.loop(0, 3 * strips)
        def _(k):
            strip, m = k // 3, k % 3
            columns = pl.ds(pl.multiple_of(m * strips * lane + strip * lane, lane), lane)
            product = jnp.dot(emb_out[...].reshape(vocab, width), w_ref[:, columns], preferred_element_type=F32).astype(BF16)
            to = pl.ds(pl.multiple_of(m * lane, lane), lane)
            part[strip * 2, :, to] = product[:hold]
            part[strip * 2 + 1, :, to] = product[hold:]

        outs.pass_on()
        PairThenRing(ctx, part, pool, pair_bufs).run(half_out)
        outs.middle()
        here = pl.ds(pl.multiple_of(ctx.pair * hold, hold), hold)
        whole = half_out[...]
        inv = lax.rsqrt(whole[:, 3 * lane :] / (width * 2 * RING) + EPSILON)
        inv_out[here] = inv
        for m in range(3):
            table[here, m * lane : (m + 1) * lane] = (whole[:, m * lane : (m + 1) * lane] * inv).astype(BF16)
        mate = ctx.at(ctx.ring, ctx.mate)
        a = remote(inv_out.at[here], inv_out.at[here], pair_sems[0], mate)
        b = remote(table.at[here], table.at[here], pair_sems[1], mate)
        tokens.finish()
        a.wait()
        b.wait()


        @pl.loop(0, (BACK + 1280) // 128)
        def _(c):
            hot = marks(tok_out, ctx.pair * (n * 128 // 128) - BACK // 128 + c, vocab)
            proj0[pl.ds(pl.multiple_of(c * 128, 128), 128)] = dot(hot, table[...], TRANS_A)

        for k in range(2):
            hot = marks(tok_out, 2 * place + k, vocab)
            first_rows[k * 128 : (k + 1) * 128] = dot(hot, emb_ref[...], TRANS_A).astype(BF16)
        span = gated0.shape[0]
        mix_first(proj0, taps0, kern0, filtered0, prod0, shifts, gated0, span)
        rows = x_block.shape[0]
        sems = pool.take(RING)
        yes = place >= 0
        pieces = [
            (
                gated0.at[pl.ds(k * rows, rows)],
                gated_own.at[:, lanes_at(ctx.ring * 128)],
                ctx.pair * RING + k,
                sems_of(send, recv, pool.count + ctx.ring),
                yes,
            )
            for k in range(RING)
        ]
        pool.count += RING
        swap(pieces, sems, place)
        outs.finish()
        for k in range(RING):
            pltpu.make_async_copy(
                gated0.at[pl.ds(0, rows)], gated_own.at[:, lanes_at(k * 128)], sems_of(send, recv, pool.count - RING + k)
            ).wait()
        swapped(pieces, sems, place)

        def produce(slot):
            part[slot] = dot(gated_own[...], wo[slot]).astype(BF16)

        RingThenPair(dp, part, pool, ring_bufs).run(total, [first_rows], produce)
        x_block[...] = total[...].astype(BF16)
        forth.start()
        forth.wait_send()
        x_over.start()
        job = Gather(ctx, gated0, gated_all, pool, False, by_strip(gated_all, span))
        job.start()
        job.middle()
        job.finish()
        x_over.wait_send()
        back.wait_recv()
        gather = Gather(dp, returned, all_ref, pool, True)
        gather.start()
        use_rows(gg, all_ref, wo, gather, dp, returned)
        gg_rows[...] = gg[...].astype(BF16)
        e_over.wait_recv()

    @pl.when(section_is(1))
    def _():
        pool = Pool(send, recv)
        pool.count = common.count
        rows, width = gg.shape
        me = lax.axis_index("ctx")
        cot = cot_ref
        outs = Gather(ctx, wo_far, wo, pool, False)
        weights = Gather(ctx, w_far, wv, pool, False)
        outs.start()
        weights.start()
        there = pltpu.make_async_remote_copy(
            src_ref=cot_ref, dst_ref=crossed, send_sem=cross_sem[0], recv_sem=cross_sem[1],
            device_id=partner, device_id_type=MESH,
        )
        here = pltpu.make_async_copy(cot_ref, crossed, same_sem[0])
        pl.when(apart)(there.start)
        pl.when(jnp.logical_not(apart))(here.start)
        turned = Gather(dp, cot_ref, part, pool, True)
        turned.start()
        turned.middle()
        turned.finish()
        outs.pass_on()
        pl.when(apart)(there.wait)
        pl.when(jnp.logical_not(apart))(here.wait)
        cots = Gather(dp, crossed, e_all, pool, True)
        cots.start()
        weights.pass_on()
        outs.middle()
        cots.middle()
        outs.finish()
        gg[...] = jnp.zeros_like(gg)
        for k in range(n):
            gg[...] += dot(part[k], wo[k], TRANS_B)
        cots.finish()
        weights.middle()
        weights.finish()
        sums_own[REACH:] = jnp.zeros((16, width), F32)
        forth.wait_recv()
        gather = Gather(dp, arrived, all_ref, pool, True)
        gather.start()

        def use(ref, slot, begin=False):
            values = ref[...]
            for m in range(3):
                ml = slice(m * width, (m + 1) * width)
                term = dot(values, wv[slot, :, ml])
                pp[8:, ml] = term if begin else pp[8:, ml] + term
            term = jnp.zeros((rows, 128), F32)
            for g in range(width // 128):
                v = values[:, g * 128 : (g + 1) * 128].astype(F32)
                term = term + v * v
            square[...] = term if begin else square[...] + term

        use(arrived, dp.slot(dp.ring, dp.pair), True)
        gather.middle()
        for ring, pair in ((dp.left, dp.pair), (dp.right, dp.pair), (dp.ring, dp.mate), (dp.left, dp.mate), (dp.right, dp.mate)):
            use(gather.block(ring, pair), dp.slot(ring, pair))
        gather.finish()
        for pair in (dp.pair, dp.mate):
            use(gather.block(dp.across, pair), dp.slot(dp.across, pair))
        inv = lax.rsqrt(jnp.sum(square[...], axis=1, keepdims=True) / (width * n) + EPSILON)
        inv_rows[...] = jnp.broadcast_to(inv, (rows, 128))
        for a, count in chunks(0, rows, 32):
            pp[8 + a : 8 + a + count] = pp[8 + a : 8 + a + count] * inv_rows[a : a + count, :1]

        sems = pool.take(4)
        a_copy = remote(pp.at[pl.ds(rows, 8)], ptail, sems[0], after)

        def products(a, count, group):
            tl = lanes_at(group * 128)
            k = short_rows(pp, taps1, 1, a, count, lanes_at(width + group * 128), tl)
            v = short_rows(pp, taps1, 2, a, count, lanes_at(2 * width + group * 128), tl)
            return k * v

        @pl.loop(0, 4)
        def _(group):
            tl = lanes_at(group * 128)
            for a, count in chunks(rows // 2, rows, 64):
                value = products(8 + a, count, group)
                prod[REACH + a : REACH + a + count, tl] = value
                qsend[a - rows // 2 : a - rows // 2 + count, tl] = value.astype(BF16)

        b_copy = remote(qsend, qtail, sems[1], after)
        a_copy.wait_recv()
        pp[0:8] = jnp.where(me > 0, ptail[...], 0.0)

        @pl.loop(0, 4)
        def _(group):
            tl = lanes_at(group * 128)
            for a, count in chunks(0, rows, 64):
                value = short_rows(pp, taps1, 0, 8 + a, count, tl, tl)
                query[a : a + count, tl] = value
                value = value * gg[a : a + count, tl]
                gf[a : a + count, tl] = value
                gfpad[a : a + count, tl] = value
                if a < REACH:
                    ghead[a : a + count, tl] = value.astype(BF16)
            for a, count in chunks(0, rows // 2, 64):
                prod[REACH + a : REACH + a + count, tl] = products(8 + a, count, group)

        c_copy = remote(ghead, gfar, sems[2], before)
        b_copy.wait_recv()
        for a, count in chunks(0, REACH, 32):
            prod[a : a + count] = jnp.where(me > 0, qtail[a : a + count].astype(F32), 0.0)

        @pl.loop(0, 4)
        def _(group):
            tl = lanes_at(group * 128)
            shifted(shifts, prod, 1, rows + REACH - 8, tl)
            kg[...] = kern1[:, tl]
            fir(shifts, kg, ALL, filtered, tl, rows // 8, 8, True)
            for a, count in chunks(0, rows, 64):
                gated_out[a : a + count, tl] = (query[a : a + count, tl] * filtered[a : a + count, tl]).astype(BF16)

        near = Gather(ctx, gated_out, gated_all, pool, False, by_rows(ctx, gated_all, rows))
        near.start()
        c_copy.wait_recv()
        for a, count in chunks(0, REACH, 32):
            gfpad[rows + a : rows + a + count] = jnp.where(me < n - 1, gfar[a : a + count].astype(F32), 0.0)

        @pl.loop(0, 4)
        def _(group):
            tl = lanes_at(group * 128)
            shifted(shifts, gfpad, 0, rows + REACH - 8, tl)
            kg[...] = kern1[:, tl]
            fir(shifts, kg, ALL, gprod, tl, rows // 8, 8, False)
            for a, count in chunks(0, rows, 64):
                here = slice(a, a + count)
                gs[here, tl] = gg[here, tl] * filtered[here, tl]
                k = short_rows(pp, taps1, 1, 8 + a, count, lanes_at(width + group * 128), tl)
                v = short_rows(pp, taps1, 2, 8 + a, count, lanes_at(2 * width + group * 128), tl)
                gs[here, lanes_at(width + group * 128)] = gprod[here, tl] * v
                gs[here, lanes_at(2 * width + group * 128)] = gprod[here, tl] * k

        for m in range(3):
            gsend[:, m * width : (m + 1) * width] = gs[0:8, m * width : (m + 1) * width]
        d_copy = remote(gsend, sfar, sems[3], before)
        d_copy.wait_recv()
        gs[rows : rows + 8] = jnp.where(me < n - 1, sfar[...], 0.0)
        row_sum[...] = jnp.zeros_like(row_sum)

        @pl.loop(0, 4)
        def _(group):
            tl = lanes_at(group * 128)
            for m in range(3):
                ml = lanes_at(m * width + group * 128)
                sums = [jnp.zeros((8, 128), F32) for _ in range(3)]
                for a, count in chunks(0, rows, 64):
                    grad = taps1[m : m + 1, tl] * gs[a : a + count, ml]
                    for j in (1, 2):
                        grad = grad + taps1[3 * j + m : 3 * j + m + 1, tl] * gs[a + j : a + j + count, ml]
                    gpb[a : a + count, ml] = grad.astype(BF16)
                    gp_out[a : a + count, ml] = (grad * inv_rows[a : a + count]).astype(BF16)
                    row_sum[a : a + count] += grad * pp[8 + a : 8 + a + count, ml]
                    for j in range(3):
                        term = gs[a : a + count, ml] * pp[8 - j + a : 8 - j + a + count, ml]
                        sums[j] = sums[j] + jnp.sum(term.reshape(count // 8, 8, 128), axis=0)
                for j in range(3):
                    sums_own[REACH + 3 * j + m : REACH + 3 * j + m + 1, tl] = jnp.sum(sums[j], axis=0, keepdims=True)

        eye = lax.broadcasted_iota(jnp.int32, (128, 128), 0) == lax.broadcasted_iota(jnp.int32, (128, 128), 1)
        stat_own[...] = jnp.zeros_like(stat_own)
        for k in range(rows // 128):
            column = jnp.sum(row_sum[k * 128 : (k + 1) * 128], axis=1, keepdims=True)
            line = jnp.sum(jnp.where(eye, jnp.broadcast_to(column, (128, 128)), 0.0), axis=0, keepdims=True)
            stat_own[k : k + 1] = line
        grads = Gather(ctx, gp_out, gp_all, pool, False)
        grads.start()
        stat = Gather(dp, stat_own, stats, pool, True)
        stat.start()

        def produce(slot):
            part[slot] = dot(gpb[...], wv[slot], TRANS_B).astype(BF16)

        RingThenPair(dp, part, pool, ring_bufs).run(total, produce=produce)
        stat.middle()
        stat.finish()
        summed = stats[0]
        for k in range(1, n):
            summed = summed + stats[k]
        for k in range(rows // 128):
            here = pl.ds(k * 128, 128)
            line = jnp.broadcast_to(summed[k : k + 1], (128, 128))
            scalar = jnp.sum(jnp.where(eye, line, 0.0), axis=1, keepdims=True)
            inv = inv_rows[here, :1]
            block[here] = (
                cot[here].astype(F32)
                + inv * total[here]
                - arrived[here].astype(F32) * (inv * inv * scalar / (width * n))
            ).astype(BF16)
        back.start()
        e_over.start()
        x_over.wait_recv()
        columns = Gather(dp, x_col, x_all, pool, True)
        columns.start()
        near.middle()

        @pl.loop(0, 4)
        def _(group):
            tl = lanes_at(group * 128)
            shifted(shifts, prod, 1, rows + REACH - 8, tl)
            lags(shifts, gf, tl, sums_own, tl, rows // 8)

        taps_job = Gather(ctx, sums_own, sums_all, pool, False)
        taps_job.start()
        jobs = [columns, grads, taps_job]
        for job in jobs:
            job.middle()
        for job in [near] + jobs:
            job.finish()
        for copy in (a_copy, b_copy, c_copy, d_copy):
            copy.wait_send()
        back.wait_send()
        e_over.wait_send()


PAIR = (None,) * 5


def end_kernel(
    gg_rows, e_col, e_all, gated_all, proj, taps, kern, filtered, tok, gtab_all, taps_all, grad_out,
    e_got, gg, gf, gprod, gs, prod, shifts, gp, sum_ref, gtab, sums, got, block, *rest,
):
    send, recv = rest
    barrier = pltpu.get_barrier_semaphore()
    ctx, dp = Group("ctx"), Group("dp")
    n = 2 * RING
    place = lax.axis_index("ctx")

    def outer(e_all):
        count, rows, _ = e_all.shape
        grad_out[...] = jnp.zeros_like(grad_out)

        @pl.loop(0, count)
        def _(k):
            here = pl.ds(pl.multiple_of(k * rows, rows), rows)
            grad_out[...] += dot(gated_all[here], e_all[k], TRANS_A)

    @pl.when(section_is(0))
    def _():
        greet([{"ctx": (place + k) % n} for k in range(1, n)] + dp.neighbours(), barrier)
        pl.semaphore_wait(barrier, n + 2)
        pool = Pool(send, recv)
        rows = gg_rows.shape[0]
        over = AHEAD - RING * rows
        sems = pool.take(2 * RING)
        start = pool.count
        pool.count += RING + 1
        spot = place % RING
        yes = place >= 0
        strip_at = lambda x: slice(x * 128, (x + 1) * 128)
        pieces = [
            (
                gg_rows.at[:, strip_at(x)],
                gg.at[pl.ds(pl.multiple_of(spot * rows, rows), rows)],
                2 * x + place // RING,
                sems_of(send, recv, start + spot),
                yes,
            )
            for x in range(RING)
        ] + [
            (
                gg_rows.at[pl.ds(0, over), strip_at(x)],
                gg.at[pl.ds(RING * rows, over)],
                2 * x,
                sems_of(send, recv, start + RING),
                place == RING,
            )
            for x in range(RING)
        ]

        @pl.when(ctx.pair == 1)
        def _():
            gg[pl.ds(RING * rows, over)] = jnp.zeros((over, 128), BF16)

        swap(pieces, sems, place)
        for k in range(RING):
            pltpu.make_async_copy(
                gg_rows.at[:, strip_at(0)], gg.at[pl.ds(k * rows, rows)], sems_of(send, recv, start + k)
            ).wait()

        @pl.when(ctx.pair == 0)
        def _():
            pltpu.make_async_copy(
                gg_rows.at[pl.ds(0, over), strip_at(0)],
                gg.at[pl.ds(RING * rows, over)],
                sems_of(send, recv, start + RING),
            ).wait()

        columns = Gather(dp, e_col, e_got, pool, True)
        columns.start()
        sem = pool.take(1)[0]
        hold = got.shape[0]
        part = gp.shape[0]
        mix_back(gg, proj, taps, kern, filtered, gf, gprod, gs, shifts, gp, part)
        columns.middle()

        sum_ref[...] = jnp.zeros_like(sum_ref)

        @pl.loop(0, part // 128)
        def _(c):
            hot = marks(tok, ctx.pair * (part // 128) + c, sum_ref.shape[0])
            sum_ref[...] += dot(hot, gp[pl.ds(pl.multiple_of(c * 128, 128), 128)])

        gtab[...] = sum_ref[...].astype(BF16)

        halves = lambda p: gtab.at[pl.ds(pl.multiple_of(p * hold, hold), hold)]
        copy = remote(halves(ctx.mate), got, sem, ctx.at(ctx.ring, ctx.mate))
        copy.wait()
        add_into(block, [halves(ctx.pair), got])
        table = Gather(ctx, block, gtab_all, pool, False)
        table.start()
        columns.finish()
        outer(e_got)
        mix_sums(gf, proj, taps, gs, prod, shifts, sums, part)
        job = Gather(ctx, sums, taps_all, pool, False)
        job.start()
        table.middle()
        job.middle()
        table.finish()
        job.finish()
        swapped(pieces, sems, place)

    @pl.when(section_is(1))
    def _():
        outer(e_all)


def dot(a, b, dims=(((1,), (0,)), ((), ()))):
    return lax.dot_general(a, b, dims, preferred_element_type=F32)


TRANS_B = (((1,), (1,)), ((), ()))
TRANS_A = (((0,), (0,)), ((), ()))


def local(
    token_ids, embedding, project_in, short_taps, filter_taps, decay_rates, project_out, cotangent
):
    section_zero = lax.axis_index("section") == 0
    n = lax.axis_size("ctx")
    vocab = embedding.shape[0]
    rows = token_ids.shape[0]
    seq = rows * n
    part = seq // 2
    width = embedding.shape[1]
    chans = project_in.shape[3]
    lane = chans // RING
    taps_all = short_taps[0]
    filter_all = filter_taps[0]
    tap_count = filter_all.shape[0]
    strip = lax.axis_index("ctx") // 2

    w_flat = project_in[0].reshape(width, 3 * chans)
    w_out = project_out[0]
    positions = jnp.arange(tap_count).astype(F32)
    damping_all = jnp.exp(-decay_rates[0][None, :] * positions[:, None] / tap_count)
    kernel_all = filter_all * damping_all

    def strip_of(a):
        return lax.dynamic_slice_in_dim(a, strip * lane, lane, a.ndim - 1)

    taps0, kernel0 = strip_of(taps_all), strip_of(kernel_all)

    taps0 = taps0.reshape(9, lane)
    taps1 = taps_all.reshape(9, chans)
    own_tokens = jnp.tile(token_ids.reshape(rows // lane, lane), (16 * lane // rows, 1))
    emb, inv_table, tokens, e_all, gated_all, proj0, filtered0, x_all, gp_all, sums1, gg_rows, e_col = call(
        main_kernel,
        1,
        [
            ((n, vocab // n, width), BF16),
            ((vocab, lane), F32),
            ((n, 16, lane), jnp.int32),
            ((n, rows, width), BF16),
            ((seq, chans), BF16),
            ((BACK + 1280, 3 * lane), F32),
            ((KEPT, lane), F32),
            ((n, rows, width), BF16),
            ((n, rows, 3 * chans), BF16),
            ((n, 144, chans), F32),
            ((rows, chans), BF16),
            ((rows, width), BF16),
        ],
        [
            pltpu.VMEM(shape, dtype)
            for shape, dtype in (
                ((n, rows, width), BF16),
                ((rows, width), BF16),
                ((vocab // 2, 4 * lane), F32),
                ((vocab // n, width), BF16),
                ((vocab, 3 * lane), BF16),
                ((BACK + AHEAD, lane), F32),
                ((8, KEPT + REACH, lane), F32),
                ((part, lane), BF16),
                ((rows, width), BF16),
                ((rows, width), F32),
                ((rows, width), BF16),
                ((n, width, 3 * chans), BF16),
                ((n, chans, width), BF16),
                ((rows, chans), BF16),
                ((rows, chans), F32),
                ((rows, width), BF16),
                ((rows, width), BF16),
                ((n, rows, width), BF16),
                ((rows, width), BF16),
                ((rows, 128), F32),
                ((rows, 128), F32),
                ((rows, 3 * chans), BF16),
                ((rows, 3 * chans), BF16),
                ((rows, chans), BF16),
                ((n, 16, 128), F32),
                ((16, 128), F32),
                ((rows, width), BF16),
                ((144, chans), F32),
                ((rows, chans), F32),
                ((rows + REACH, chans), F32),
                ((REACH, 128), F32),
                ((rows + 8, 3 * chans), F32),
                ((rows, chans), F32),
                ((rows, chans), F32),
                ((rows, chans), F32),
                ((rows + 8, 3 * chans), F32),
                ((8, 3 * chans), F32),
                ((REACH, chans), BF16),
                ((REACH, chans), BF16),
                ((REACH, chans), BF16),
                ((8, 3 * chans), F32),
                ((rows + REACH, chans), F32),
                ((rows, 128), F32),
                ((REACH, chans), BF16),
                ((8, 3 * chans), F32),
            )
        ]
        + PairThenRing.scratch(rows, width)
        + RingThenPair.scratch(rows, width),
        128,
        embedding, w_flat, w_flat, cotangent, own_tokens, w_out, w_out, taps0, kernel0, taps1, kernel_all,
        in_specs=[VMEM, VMEM, ANY] + [VMEM] * 3 + [ANY] + [VMEM] * 4,
        out_specs=[VMEM] * 8 + [ANY] * 2 + [VMEM] * 2,
        name="main",
    )
    emb = emb.reshape(vocab, width)
    gtab, sums0, grad_out = call(
        end_kernel,
        2,
        [((n, vocab // 2, 3 * lane), BF16), ((n, 144, lane), F32), ((chans, width), F32)],
        [
            pltpu.VMEM((n, rows, width), BF16),
            pltpu.VMEM((AHEAD, lane), BF16),
            pltpu.VMEM((AHEAD, lane), F32),
            pltpu.VMEM((KEPT, lane), F32),
            pltpu.VMEM((3, KEPT, lane), F32),
            pltpu.VMEM((BACK + AHEAD, lane), F32),
            pltpu.VMEM((8, KEPT + REACH, lane), F32),
            pltpu.VMEM((part, 3 * lane), BF16),
            pltpu.VMEM((vocab, 3 * lane), F32),
            pltpu.VMEM((vocab, 3 * lane), BF16),
            pltpu.VMEM((144, lane), F32),
            pltpu.VMEM((vocab // 2, 3 * lane), BF16),
            pltpu.VMEM((vocab // 2, 3 * lane), BF16),
        ],
        56,
        gg_rows, e_col, e_all, gated_all, proj0, taps0, kernel0, filtered0, tokens,
        name="end",
    )

    def end0():
        table_rows = jnp.transpose(gtab.reshape(RING, 2, vocab // 2, 3, lane), (1, 2, 3, 0, 4))
        normed_table = (emb.astype(F32) * inv_table[:, :1]).astype(BF16)
        sums = sums0.reshape(RING, 2, 144, lane).sum(axis=1)
        return (
            dot(normed_table, table_rows.reshape(vocab, 3 * chans), TRANS_A),
            jnp.transpose(sums, (1, 0, 2)).reshape(144, chans),
        )

    def end1():
        return (
            dot(x_all.reshape(seq, width), gp_all.reshape(seq, 3 * chans), TRANS_A),
            sums1.sum(axis=0),
        )

    grad_in, sums = lax.cond(section_zero, end0, end1)
    grad_in = grad_in.reshape(width, 3, chans)
    gk, gt = sums[:tap_count], sums[tap_count : tap_count + 9].reshape(3, 3, chans)
    grad_filter = gk * damping_all
    grad_decay = -jnp.sum(gk * kernel_all * positions[:, None], axis=0) / tap_count
    return (grad_in[None], grad_out[None], grad_filter[None], grad_decay[None], gt[None])


def solution(mesh):
    return jax.shard_map(
        local,
        mesh=mesh,
        in_specs=(
            P("ctx"),
            P(None, "dp"),
            P("section", "ctx", None, "dp"),
            P("section", None, None, "dp"),
            P("section", None, "dp"),
            P("section", "dp"),
            P("section", "dp", "ctx"),
            P("ctx", "dp"),
        ),
        out_specs=(
            P("section", "ctx", None, "dp"),
            P("section", "dp", "ctx"),
            P("section", None, "dp"),
            P("section", "dp"),
            P("section", None, None, "dp"),
        ),
        check_vma=False,
    )
```

```python
import functools

import jax
import jax.numpy as jnp
from jax import lax
from jax.experimental import pallas as pl
from jax.experimental.pallas import tpu as pltpu
from jax.sharding import PartitionSpec as P

EPSILON = 1e-06
F32 = jnp.float32
BF16 = jnp.bfloat16
MESH = pl.DeviceIdType.MESH
BACK = 256
AHEAD = 1184
KEPT = 1040
RING = 4
REACH = 128


class Group:
    def __init__(self, axis):
        self.axis = axis
        me = lax.axis_index(axis)
        if axis == "ctx":
            self.ring, self.pair = me // 2, me % 2
        else:
            self.ring, self.pair = me % RING, me // RING
        self.right = (self.ring + 1) % RING
        self.left = (self.ring + RING - 1) % RING
        self.across = (self.ring + 2) % RING
        self.mate = 1 - self.pair

    def slot(self, ring, pair):
        return ring * 2 + pair if self.axis == "ctx" else pair * RING + ring

    def at(self, ring, pair):
        return {self.axis: self.slot(ring, pair)}

    def neighbours(self):
        return [
            self.at(self.right, self.pair),
            self.at(self.left, self.pair),
            self.at(self.ring, self.mate),
        ]


class Pool:
    def __init__(self, send, recv):
        self.send, self.recv, self.count = send, recv, 0

    def take(self, k):
        first = self.count
        self.count += k
        return [(self.send.at[first + i], self.recv.at[first + i]) for i in range(k)]


def remote(src, dst, sems, device):
    copy = pltpu.make_async_remote_copy(
        src_ref=src,
        dst_ref=dst,
        send_sem=sems[0],
        recv_sem=sems[1],
        device_id=device,
        device_id_type=MESH,
    )
    copy.start()
    return copy


def greet(devices, barrier):
    for device in devices:
        pl.semaphore_signal(barrier, inc=1, device_id=device, device_id_type=MESH)


class Gather:
    def __init__(self, group, src, out, pool, pair_first, place=None):
        self.g, self.src, self.out, self.pair_first = group, src, out, pair_first
        self.sems = pool.take(9)
        self.own = pool.take(1)[0]
        self.rows = src.shape[0]
        self.half = self.rows // 2
        self.place = place or (lambda ring, pair, first, rows: out.at[group.slot(ring, pair), pl.ds(first, rows)])

    def block(self, ring, pair):
        return self.place(ring, pair, 0, self.rows)

    def part(self, ring, pair, second):
        return self.place(ring, pair, self.half * second, self.half)

    def start(self):
        g, s = self.g, self.sems
        mine = self.block(g.ring, g.pair)
        right, left, mate = g.neighbours()
        self.local = pltpu.make_async_copy(self.src, mine, self.own[0])
        self.local.start()
        first = remote(self.src, mine, s[0], mate)
        self.copies = [first, remote(self.src, mine, s[1], right), remote(self.src, mine, s[2], left)]

    def turn(self, pair, a, b, c, d):
        g, s = self.g, self.sems
        right, left, mate = g.neighbours()
        more = []
        a.wait_recv()
        part = self.part(g.left, pair, 0)
        more.append(remote(part, part, s[c], right))
        if not self.pair_first:
            block = self.block(g.left, pair)
            more.append(remote(block, block, s[5], mate))
        b.wait_recv()
        part = self.part(g.right, pair, 1)
        more.append(remote(part, part, s[d], left))
        if not self.pair_first:
            block = self.block(g.right, pair)
            more.append(remote(block, block, s[6], mate))
        return more

    def pass_on(self):
        self.passed = self.turn(self.g.pair, self.copies[1], self.copies[2], 3, 4)

    def cross_on(self):
        g, s = self.g, self.sems
        right, left, mate = g.neighbours()
        self.copies[0].wait_recv()
        block = self.block(g.ring, g.mate)
        self.crossed = (remote(block, block, s[5], right), remote(block, block, s[6], left))

    passed = crossed = None

    def middle(self):
        g, s = self.g, self.sems
        right, left, mate = g.neighbours()
        mate_copy, to_right, to_left = self.copies
        if self.passed is None:
            self.pass_on()
        rest = self.passed
        self.sent = list(self.copies) + rest
        if self.pair_first:
            self.late = list(rest)
            if self.crossed is None:
                self.cross_on()
            a, b = self.crossed
            more = self.turn(g.mate, a, b, 7, 8)
            self.sent += [a, b] + more
            self.late += more
        else:
            rest[0].wait_recv()
            rest[2].wait_recv()
            block = self.block(g.across, g.pair)
            last = remote(block, block, s[7], mate)
            self.sent.append(last)
            self.late = [mate_copy, rest[1], rest[3], last]

    def finish(self):
        for copy in self.late:
            copy.wait_recv()
        for copy in self.sent:
            copy.wait_send()
        self.local.wait()


def add_into(out, terms, rows=64):
    @pl.loop(0, out.shape[0] // rows)
    def _(step):
        here = pl.ds(pl.multiple_of(step * rows, rows), rows)
        total = terms[0][here].astype(F32)
        for term in terms[1:]:
            total = total + term[here].astype(F32)
        out[here] = total.astype(out.dtype)


def rows_step(count):
    for rows in (64, 48, 37 * 16, 32, 16):
        if count % rows == 0:
            return rows if rows != 37 * 16 else 16
    return 16


class Around:
    def __init__(self, group, pool, bufs):
        self.g = group
        self.s = pool.take(6)
        self.rel, self.merged, self.came = bufs
        self.half = self.rel.shape[1]

    @staticmethod
    def scratch(rows, lanes):
        half = rows // 2
        return [
            pltpu.VMEM((2, half, lanes), BF16),
            pltpu.VMEM((2, half, lanes), BF16),
            pltpu.VMEM((2, 2, half, lanes), BF16),
        ]

    def halves(self, ref):
        return ref.at[pl.ds(0, self.half)], ref.at[pl.ds(self.half, self.half)]

    def send_across(self, block):
        right, left, _ = self.g.neighbours()
        a, b = self.halves(block)
        self.copies = [remote(a, self.rel.at[0], self.s[0], right), remote(b, self.rel.at[1], self.s[1], left)]

    def send_near(self, to_right, to_left):
        right, left, _ = self.g.neighbours()
        self.to_right, self.to_left = to_right, to_left
        b = self.halves(to_right)[1]
        a = self.halves(to_left)[0]
        self.copies += [
            remote(b, self.came.at[0, 1], self.s[2], right),
            remote(a, self.came.at[1, 0], self.s[3], left),
        ]

    def merge(self):
        right, left, _ = self.g.neighbours()
        step = rows_step(self.half)
        self.copies[0].wait_recv()
        add_into(self.merged.at[0], [self.halves(self.to_right)[0], self.rel.at[0]], step)
        self.copies.append(remote(self.merged.at[0], self.came.at[0, 0], self.s[4], right))
        self.copies[1].wait_recv()
        add_into(self.merged.at[1], [self.halves(self.to_left)[1], self.rel.at[1]], step)
        self.copies.append(remote(self.merged.at[1], self.came.at[1, 1], self.s[5], left))

    def collect(self, out, own):
        step = rows_step(self.half)
        for copy in self.copies[2:]:
            copy.wait_recv()
        for h in range(2):
            piece = pl.ds(h * self.half, self.half)
            add_into(
                out.at[piece],
                [ref.at[piece] for ref in own] + [self.came.at[0, h], self.came.at[1, h]],
                step,
            )

    def finish(self):
        for copy in self.copies:
            copy.wait_send()


class PairThenRing:
    def __init__(self, group, inp, pool, bufs):
        self.g, self.inp = group, inp
        self.got, self.sums = bufs[:2]
        self.ring = Around(group, pool, bufs[2:])
        self.s = pool.take(4)

    @staticmethod
    def scratch(rows, lanes):
        return [pltpu.VMEM((4, rows, lanes), BF16), pltpu.VMEM((4, rows, lanes), BF16)] + Around.scratch(rows, lanes)

    def run(self, out):
        g = self.g
        mate = g.at(g.ring, g.mate)
        order = [g.across, g.right, g.left, g.ring]
        copies = [
            remote(self.inp.at[g.slot(r, g.mate)], self.got.at[k], self.s[k], mate) for k, r in enumerate(order)
        ]
        step = rows_step(self.inp.shape[1])

        def pair_sum(k):
            copies[k].wait_recv()
            add_into(self.sums.at[k], [self.inp.at[g.slot(order[k], g.pair)], self.got.at[k]], step)

        pair_sum(0)
        self.ring.send_across(self.sums.at[0])
        pair_sum(1)
        pair_sum(2)
        self.ring.send_near(self.sums.at[1], self.sums.at[2])
        copies[3].wait_recv()
        self.ring.merge()
        self.ring.collect(out, [self.inp.at[g.slot(g.ring, g.pair)], self.got.at[3]])
        self.ring.finish()
        for copy in copies:
            copy.wait_send()


class RingThenPair:
    def __init__(self, group, inp, pool, bufs):
        self.g, self.inp = group, inp
        self.far, self.got = bufs[:2]
        self.rings = [Around(group, pool, bufs[2:5]), Around(group, pool, bufs[5:8])]
        self.s = pool.take(1)[0]

    @staticmethod
    def scratch(rows, lanes):
        return (
            [pltpu.VMEM((rows, lanes), BF16), pltpu.VMEM((rows, lanes), BF16)]
            + Around.scratch(rows, lanes)
            + Around.scratch(rows, lanes)
        )

    def run(self, out, extra=(), produce=lambda slot: None):
        g = self.g
        pairs = [g.mate, g.pair]
        blocks = lambda ring, pair: self.inp.at[g.slot(ring, pair)]
        for ring, pair in zip(self.rings, pairs):
            produce(g.slot(g.across, pair))
            ring.send_across(blocks(g.across, pair))
            produce(g.slot(g.right, pair))
            produce(g.slot(g.left, pair))
            ring.send_near(blocks(g.right, pair), blocks(g.left, pair))
            produce(g.slot(g.ring, pair))
        self.rings[0].merge()
        self.rings[1].merge()
        self.rings[0].collect(self.far, [blocks(g.ring, g.mate)])
        copy = remote(self.far, self.got, self.s, g.at(g.ring, g.mate))
        self.rings[1].collect(out, [blocks(g.ring, g.pair)])
        copy.wait_recv()
        add_into(out, [out, self.got] + list(extra), rows_step(out.shape[0]))
        copy.wait_send()
        for ring in self.rings:
            ring.finish()


ANY = pl.BlockSpec(memory_space=pl.ANY)
VMEM = pl.BlockSpec(memory_space=pltpu.VMEM)


def call(body, ident, outs, scratch, sems, *args, in_specs=None, out_specs=None, name=None, local=0):
    return pl.pallas_call(
        body,
        out_shape=[jax.ShapeDtypeStruct(shape, dtype) for shape, dtype in outs],
        in_specs=in_specs or [VMEM] * len(args),
        out_specs=out_specs or [VMEM] * len(outs),
        scratch_shapes=list(scratch)
        + [pltpu.SemaphoreType.DMA((sems,)), pltpu.SemaphoreType.DMA((sems,))]
        + ([pltpu.SemaphoreType.DMA((local,))] if local else []),
        compiler_params=pltpu.CompilerParams(
            collective_id=ident, has_side_effects=True, vmem_limit_bytes=60 * 1024 * 1024
        ),
        name=name,
    )(*args)


def section_is(k):
    return lax.axis_index("section") == k


def crossing():
    i, j = lax.axis_index("dp"), lax.axis_index("ctx")
    return {"dp": j, "ctx": i}, i != j


def other_section():
    i, j = lax.axis_index("dp"), lax.axis_index("ctx")
    return {"section": 1 - lax.axis_index("section"), "dp": j, "ctx": i}


def lanes_at(first):
    return pl.ds(pl.multiple_of(first, 128), 128)


def shifted(shifts, ref, start, rows, lanes):
    for r in range(8):
        for a in range(0, rows, 64):
            count = min(64, rows - a)
            shifts[r, a : a + count] = ref[start + r + a : start + r + a + count, lanes]


def fir(shifts, kern, lanes, out, out_lanes, tiles, block, backwards):
    @pl.loop(0, tiles // block)
    def _(b):
        first = pl.multiple_of(b * block * 8, 8)

        def step(r, totals):
            totals = list(totals)
            taps = []
            for q in range(REACH // 8):
                u = 8 * q + r
                taps.append(kern[pl.ds(REACH - 1 - u if backwards else u, 8, stride=0), lanes])
            for i in range(block + REACH // 8 - 1):
                x = shifts[r, pl.ds(first + 8 * i, 8)]
                for o in range(block):
                    if 0 <= i - o < REACH // 8:
                        totals[o] = totals[o] + taps[i - o] * x
            return tuple(totals)

        totals = lax.fori_loop(0, 8, step, tuple(jnp.zeros((8, 128), F32) for _ in range(block)))
        for o in range(block):
            out[pl.ds(first + 8 * o, 8), out_lanes] = totals[o]


def lags(shifts, ref, lanes, out, out_lanes, tiles):
    for r in range(8):

        def step(b, totals):
            totals = list(totals)
            first = pl.multiple_of(b * 32, 8)
            own = [ref[pl.ds(first + 8 * o, 8), lanes] for o in range(4)]
            for i in range(4 + REACH // 8 - 1):
                x = shifts[r, pl.ds(first + 8 * i, 8)]
                for o in range(4):
                    if 0 <= i - o < REACH // 8:
                        totals[i - o] = totals[i - o] + own[o] * x
            return tuple(totals)

        totals = lax.fori_loop(0, tiles // 4, step, tuple(jnp.zeros((8, 128), F32) for _ in range(REACH // 8)))
        for q in range(REACH // 8):
            row = REACH - 1 - (8 * q + r)
            out[row : row + 1, out_lanes] = jnp.sum(totals[q], axis=0, keepdims=True)


def chunks(first, last, size):
    for a in range(first, last, size):
        yield a, min(size, last - a)


def short_rows(ref, taps, m, a, count, lanes, tap_lanes):
    total = taps[m : m + 1, tap_lanes] * ref[a : a + count, lanes]
    for j in (1, 2):
        total = total + taps[3 * j + m : 3 * j + m + 1, tap_lanes] * ref[a - j : a - j + count, lanes]
    return total


ALL = slice(0, 128)


def stream(m):
    return slice(m * 128, (m + 1) * 128)


def mix_first(proj, taps, kern, filtered, prod, shifts, gated, part):
    for a, count in chunks(BACK - REACH, BACK + part, 64):
        prod[a : a + count] = short_rows(proj, taps, 1, a, count, stream(1), ALL) * short_rows(
            proj, taps, 2, a, count, stream(2), ALL
        )
    for a, count in chunks(BACK + part, BACK + AHEAD, 64):
        prod[a : a + count] = short_rows(proj, taps, 1, a, count, stream(1), ALL) * short_rows(
            proj, taps, 2, a, count, stream(2), ALL
        )
    shifted(shifts, prod, BACK - REACH + 1, KEPT + REACH, ALL)
    fir(shifts, kern, ALL, filtered, ALL, KEPT // 8, 10, True)
    for a, count in chunks(0, part, 64):
        query = short_rows(proj, taps, 0, BACK + a, count, stream(0), ALL)
        gated[a : a + count] = (query * filtered[a : a + count]).astype(BF16)


def mix_back(gg, proj, taps, kern, filtered, gf, gprod, gs, shifts, gp, part):
    for a, count in chunks(0, AHEAD, 64):
        gf[a : a + count] = gg[a : a + count] * short_rows(proj, taps, 0, BACK + a, count, stream(0), ALL)
    shifted(shifts, gf, 0, KEPT + REACH, ALL)
    fir(shifts, kern, ALL, gprod, ALL, KEPT // 8, 10, False)
    for a, count in chunks(0, KEPT, 64):
        here = slice(a, a + count)
        gs[0, here] = gg[here] * filtered[here]
        gs[1, here] = gprod[here] * short_rows(proj, taps, 2, BACK + a, count, stream(2), ALL)
        gs[2, here] = gprod[here] * short_rows(proj, taps, 1, BACK + a, count, stream(1), ALL)
    for m in range(3):
        for a, count in chunks(0, part, 64):
            total = taps[m : m + 1] * gs[m, a : a + count]
            for j in (1, 2):
                total = total + taps[3 * j + m : 3 * j + m + 1] * gs[m, a + j : a + j + count]
            gp[a : a + count, stream(m)] = total.astype(BF16)


def mix_sums(gf, proj, taps, gs, prod, shifts, out, part):
    for a, count in chunks(BACK - REACH, BACK + part + 8, 64):
        prod[a : a + count] = short_rows(proj, taps, 1, a, count, stream(1), ALL) * short_rows(
            proj, taps, 2, a, count, stream(2), ALL
        )
    shifted(shifts, prod, BACK - REACH + 1, part + REACH, ALL)
    lags(shifts, gf, ALL, out, ALL, part // 8)
    out[REACH:] = jnp.zeros((16, 128), F32)
    for m in range(3):
        for j in range(3):
            total = jnp.zeros((8, 128), F32)
            for a, count in chunks(0, part, 64):
                term = gs[m, a : a + count] * proj[BACK - j + a : BACK - j + a + count, stream(m)]
                total = total + jnp.sum(term.reshape(count // 8, 8, 128), axis=0)
            row = REACH + 3 * j + m
            out[row : row + 1] = jnp.sum(total, axis=0, keepdims=True)


def by_rows(group, out, rows):
    def place(ring, pair, first, count):
        start = group.slot(ring, pair) * rows + first
        return out.at[pl.ds(pl.multiple_of(start, count), count)]

    return place


def by_strip(out, part):
    def place(ring, pair, first, count):
        return out.at[pl.ds(pl.multiple_of(pair * part + first, count), count), lanes_at(ring * 128)]

    return place


def marks(tok, q, vocab):
    inside = jnp.clip(q, 0, 4 * RING - 1)
    ids = tok[inside // 2, pl.ds(inside % 2, 1)]
    ids = jnp.where(q == inside, ids, -1)
    return jnp.where(lax.broadcasted_iota(jnp.int32, (vocab, 128), 0) == ids, 1.0, 0.0).astype(BF16)


def sems_of(send, recv, k):
    return recv.at[k]


def use_rows(out, blocks, weights, gather, dp, own):
    term = lambda ref, slot: dot(ref[...], weights[slot], TRANS_B)
    slot = dp.slot(dp.ring, dp.pair)
    out[...] = term(own, slot)
    gather.middle()
    near = ((dp.left, dp.pair), (dp.right, dp.pair), (dp.ring, dp.mate), (dp.left, dp.mate), (dp.right, dp.mate))
    for ring, pair in near:
        slot = dp.slot(ring, pair)
        out[...] += term(blocks.at[slot], slot)
    gather.finish()
    for pair in (dp.pair, dp.mate):
        slot = dp.slot(dp.across, pair)
        out[...] += term(blocks.at[slot], slot)


def swap(pieces, sems, me):
    for k, (src, dst, to, sem, when) in enumerate(pieces):
        far = jnp.logical_and(when, to != me)
        near = jnp.logical_and(when, to == me)
        away = pltpu.make_async_remote_copy(
            src_ref=src, dst_ref=dst, send_sem=sems[k][0], recv_sem=sem, device_id={"ctx": to}, device_id_type=MESH
        )
        here = pltpu.make_async_copy(src, dst, sem)
        pl.when(far)(away.start)
        pl.when(near)(here.start)


def swapped(pieces, sems, me):
    for k, (src, dst, to, sem, when) in enumerate(pieces):
        away = pltpu.make_async_remote_copy(
            src_ref=src, dst_ref=dst, send_sem=sems[k][0], recv_sem=sem, device_id={"ctx": to}, device_id_type=MESH
        )
        pl.when(jnp.logical_and(when, to != me))(away.wait_send)


def main_kernel(
    emb_ref, w_ref, w_far, cot_ref, tok_ref, w_proj, wo_far, taps0, kern0, taps1, kern1,
    emb_out, inv_out, tok_out, e_all, gated_all, proj0, filtered0, x_all, gp_all, sums_all, gg_rows, e_col,
    part, crossed, half_out, piece, table, prod0, shifts, gated0, first_rows, total, x_block,
    wv, wo, gated_own, gg, arrived, returned, all_ref, x_col, square, inv_rows, gp_out, gpb, gated_out, stats, stat_own, block, sums_own, gf, prod,
    kg, pp, query, filtered, gprod, gs, ptail, qtail, ghead, gfar, sfar, gfpad, row_sum, qsend, gsend, *rest,
):
    pair_bufs, ring_bufs = rest[: len(PAIR)], rest[len(PAIR) : -2]
    send, recv = rest[-2:]
    barrier = pltpu.get_barrier_semaphore()
    ctx, dp = Group("ctx"), Group("dp")
    partner, apart = crossing()
    n = 2 * RING
    me = lax.axis_index("dp")
    place = lax.axis_index("ctx")
    others = [{"dp": (me + k) % n} for k in range(1, n)]
    after, before = {"ctx": (place + 1) % n}, {"ctx": (place + n - 1) % n}
    along = [{"ctx": (place + k) % n} for k in range(1, n)]
    opposite = {"section": 1 - lax.axis_index("section")}
    greet(along + others + [other_section(), opposite], barrier)
    for k in range(n):
        pl.when(jnp.logical_or(apart, place != k))(functools.partial(greet, [{"dp": place, "ctx": k}], barrier))
    pl.semaphore_wait(barrier, 3 * n - 1 + jnp.where(apart, 1, 0))
    lane = 128
    strips = RING
    common = Pool(send, recv)
    cross_sem = common.take(1)[0]
    same_sem = common.take(1)[0]
    pair_sems = common.take(2)
    relay = common.take(4)

    def handed(src, dst, k, device):
        return pltpu.make_async_remote_copy(
            src_ref=src, dst_ref=dst, send_sem=relay[k][0], recv_sem=relay[k][1],
            device_id=device, device_id_type=MESH,
        )

    forth = handed(x_block, arrived, 0, opposite)
    back = handed(block, returned, 1, opposite)
    x_over = handed(x_block, x_col, 2, other_section())
    e_over = handed(block, e_col, 3, other_section())

    @pl.when(section_is(0))
    def _():
        pool = Pool(send, recv)
        pool.count = common.count
        tokens = Gather(ctx, tok_ref, tok_out, pool, False)
        tokens.start()
        outs = Gather(ctx, wo_far, wo, pool, False)
        share = emb_out.shape[1]
        spread = pool.count
        pool.count += n
        source = emb_ref.at[pl.ds(pl.multiple_of(place * share, share), share)]
        away = [
            pltpu.make_async_remote_copy(
                src_ref=source, dst_ref=emb_out.at[place], send_sem=send.at[spread + k],
                recv_sem=recv.at[spread + place], device_id={"dp": k, "ctx": me}, device_id_type=MESH,
            )
            for k in range(n)
        ]
        keep = pltpu.make_async_copy(source, emb_out.at[place], recv.at[spread + place])
        for k in range(n):
            pl.when(jnp.logical_or(apart, me != k))(away[k].start)
        pl.when(jnp.logical_not(apart))(keep.start)
        outs.start()
        tokens.pass_on()
        for k in range(n):
            pltpu.make_async_copy(source, emb_out.at[k], recv.at[spread + k]).wait()
        for k in range(n):
            pl.when(jnp.logical_or(apart, me != k))(away[k].wait_send)
        tokens.middle()

        vocab, width = emb_ref.shape
        hold = vocab // 2
        for core in range(2):
            values = emb_out[core * RING : (core + 1) * RING].reshape(hold, width).astype(F32)
            square = jnp.broadcast_to(jnp.sum(values * values, axis=1, keepdims=True), (hold, lane)).astype(BF16)
            for strip in range(strips):
                part[strip * 2 + core, :, 3 * lane :] = square

        @pl.loop(0, 3 * strips)
        def _(k):
            strip, m = k // 3, k % 3
            columns = pl.ds(pl.multiple_of(m * strips * lane + strip * lane, lane), lane)
            product = jnp.dot(emb_out[...].reshape(vocab, width), w_ref[:, columns], preferred_element_type=F32).astype(BF16)
            to = pl.ds(pl.multiple_of(m * lane, lane), lane)
            part[strip * 2, :, to] = product[:hold]
            part[strip * 2 + 1, :, to] = product[hold:]

        PairThenRing(ctx, part, pool, pair_bufs).run(half_out)
        outs.pass_on()
        here = pl.ds(pl.multiple_of(ctx.pair * hold, hold), hold)
        whole = half_out[...]
        inv = lax.rsqrt(whole[:, 3 * lane :] / (width * 2 * RING) + EPSILON)
        inv_out[here] = inv
        for m in range(3):
            table[here, m * lane : (m + 1) * lane] = (whole[:, m * lane : (m + 1) * lane] * inv).astype(BF16)
        mate = ctx.at(ctx.ring, ctx.mate)
        a = remote(inv_out.at[here], inv_out.at[here], pair_sems[0], mate)
        b = remote(table.at[here], table.at[here], pair_sems[1], mate)
        tokens.finish()
        a.wait()
        b.wait()


        @pl.loop(0, (BACK + 1280) // 128)
        def _(c):
            hot = marks(tok_out, ctx.pair * (n * 128 // 128) - BACK // 128 + c, vocab)
            proj0[pl.ds(pl.multiple_of(c * 128, 128), 128)] = dot(hot, table[...], TRANS_A)

        for k in range(2):
            hot = marks(tok_out, 2 * place + k, vocab)
            first_rows[k * 128 : (k + 1) * 128] = dot(hot, emb_ref[...], TRANS_A).astype(BF16)
        outs.middle()
        span = gated0.shape[0]
        mix_first(proj0, taps0, kern0, filtered0, prod0, shifts, gated0, span)
        rows = x_block.shape[0]
        sems = pool.take(RING)
        yes = place >= 0
        pieces = [
            (
                gated0.at[pl.ds(k * rows, rows)],
                gated_own.at[:, lanes_at(ctx.ring * 128)],
                ctx.pair * RING + k,
                sems_of(send, recv, pool.count + ctx.ring),
                yes,
            )
            for k in range(RING)
        ]
        pool.count += RING
        swap(pieces, sems, place)
        outs.finish()
        for k in range(RING):
            pltpu.make_async_copy(
                gated0.at[pl.ds(0, rows)], gated_own.at[:, lanes_at(k * 128)], sems_of(send, recv, pool.count - RING + k)
            ).wait()
        swapped(pieces, sems, place)

        def produce(slot):
            part[slot] = dot(gated_own[...], wo[slot]).astype(BF16)

        RingThenPair(dp, part, pool, ring_bufs).run(total, [first_rows], produce)
        x_block[...] = total[...].astype(BF16)
        forth.start()
        forth.wait_send()
        x_over.start()
        job = Gather(ctx, gated0, gated_all, pool, False, by_strip(gated_all, span))
        job.start()
        job.middle()
        job.finish()
        x_over.wait_send()
        back.wait_recv()
        gather = Gather(dp, returned, all_ref, pool, True)
        gather.start()
        use_rows(gg, all_ref, wo, gather, dp, returned)
        gg_rows[...] = gg[...].astype(BF16)
        e_over.wait_recv()

    @pl.when(section_is(1))
    def _():
        pool = Pool(send, recv)
        pool.count = common.count
        rows, width = gg.shape
        me = lax.axis_index("ctx")
        cot = cot_ref
        outs = Gather(ctx, wo_far, wo, pool, False)
        weights = Gather(ctx, w_far, wv, pool, False)
        outs.start()
        weights.start()
        there = pltpu.make_async_remote_copy(
            src_ref=cot_ref, dst_ref=crossed, send_sem=cross_sem[0], recv_sem=cross_sem[1],
            device_id=partner, device_id_type=MESH,
        )
        here = pltpu.make_async_copy(cot_ref, crossed, same_sem[0])
        pl.when(apart)(there.start)
        pl.when(jnp.logical_not(apart))(here.start)
        turned = Gather(dp, cot_ref, part, pool, True)
        turned.start()
        turned.middle()
        turned.finish()
        outs.pass_on()
        weights.pass_on()
        outs.middle()
        outs.finish()
        gg[...] = jnp.zeros_like(gg)
        for k in range(n):
            gg[...] += dot(part[k], wo[k], TRANS_B)
        pl.when(apart)(there.wait)
        pl.when(jnp.logical_not(apart))(here.wait)
        cots = Gather(dp, crossed, e_all, pool, True)
        cots.start()
        weights.middle()
        cots.pass_on()
        cots.cross_on()
        weights.finish()
        cots.middle()
        sums_own[REACH:] = jnp.zeros((16, width), F32)
        forth.wait_recv()
        gather = Gather(dp, arrived, all_ref, pool, True)
        gather.start()

        def use(ref, slot, begin=False):
            values = ref[...]
            for m in range(3):
                ml = slice(m * width, (m + 1) * width)
                term = dot(values, wv[slot, :, ml])
                pp[8:, ml] = term if begin else pp[8:, ml] + term
            term = jnp.zeros((rows, 128), F32)
            for g in range(width // 128):
                v = values[:, g * 128 : (g + 1) * 128].astype(F32)
                term = term + v * v
            square[...] = term if begin else square[...] + term

        use(arrived, dp.slot(dp.ring, dp.pair), True)
        gather.middle()
        for ring, pair in ((dp.left, dp.pair), (dp.right, dp.pair), (dp.ring, dp.mate), (dp.left, dp.mate), (dp.right, dp.mate)):
            use(gather.block(ring, pair), dp.slot(ring, pair))
        gather.finish()
        for pair in (dp.pair, dp.mate):
            use(gather.block(dp.across, pair), dp.slot(dp.across, pair))
        inv = lax.rsqrt(jnp.sum(square[...], axis=1, keepdims=True) / (width * n) + EPSILON)
        inv_rows[...] = jnp.broadcast_to(inv, (rows, 128))
        for a, count in chunks(0, rows, 32):
            pp[8 + a : 8 + a + count] = pp[8 + a : 8 + a + count] * inv_rows[a : a + count, :1]

        sems = pool.take(4)
        a_copy = remote(pp.at[pl.ds(rows, 8)], ptail, sems[0], after)

        def products(a, count, group):
            tl = lanes_at(group * 128)
            k = short_rows(pp, taps1, 1, a, count, lanes_at(width + group * 128), tl)
            v = short_rows(pp, taps1, 2, a, count, lanes_at(2 * width + group * 128), tl)
            return k * v

        @pl.loop(0, 4)
        def _(group):
            tl = lanes_at(group * 128)
            for a, count in chunks(rows // 2, rows, 64):
                value = products(8 + a, count, group)
                prod[REACH + a : REACH + a + count, tl] = value
                qsend[a - rows // 2 : a - rows // 2 + count, tl] = value.astype(BF16)

        b_copy = remote(qsend, qtail, sems[1], after)
        a_copy.wait_recv()
        pp[0:8] = jnp.where(me > 0, ptail[...], 0.0)

        @pl.loop(0, 4)
        def _(group):
            tl = lanes_at(group * 128)
            for a, count in chunks(0, rows, 64):
                value = short_rows(pp, taps1, 0, 8 + a, count, tl, tl)
                query[a : a + count, tl] = value
                value = value * gg[a : a + count, tl]
                gf[a : a + count, tl] = value
                gfpad[a : a + count, tl] = value
                if a < REACH:
                    ghead[a : a + count, tl] = value.astype(BF16)
            for a, count in chunks(0, rows // 2, 64):
                prod[REACH + a : REACH + a + count, tl] = products(8 + a, count, group)

        c_copy = remote(ghead, gfar, sems[2], before)
        b_copy.wait_recv()
        for a, count in chunks(0, REACH, 32):
            prod[a : a + count] = jnp.where(me > 0, qtail[a : a + count].astype(F32), 0.0)

        @pl.loop(0, 4)
        def _(group):
            tl = lanes_at(group * 128)
            shifted(shifts, prod, 1, rows + REACH - 8, tl)
            kg[...] = kern1[:, tl]
            fir(shifts, kg, ALL, filtered, tl, rows // 8, 8, True)
            for a, count in chunks(0, rows, 64):
                gated_out[a : a + count, tl] = (query[a : a + count, tl] * filtered[a : a + count, tl]).astype(BF16)

        near = Gather(ctx, gated_out, gated_all, pool, False, by_rows(ctx, gated_all, rows))
        near.start()
        c_copy.wait_recv()
        for a, count in chunks(0, REACH, 32):
            gfpad[rows + a : rows + a + count] = jnp.where(me < n - 1, gfar[a : a + count].astype(F32), 0.0)

        @pl.loop(0, 4)
        def _(group):
            tl = lanes_at(group * 128)
            shifted(shifts, gfpad, 0, rows + REACH - 8, tl)
            kg[...] = kern1[:, tl]
            fir(shifts, kg, ALL, gprod, tl, rows // 8, 8, False)
            for a, count in chunks(0, rows, 64):
                here = slice(a, a + count)
                gs[here, tl] = gg[here, tl] * filtered[here, tl]
                k = short_rows(pp, taps1, 1, 8 + a, count, lanes_at(width + group * 128), tl)
                v = short_rows(pp, taps1, 2, 8 + a, count, lanes_at(2 * width + group * 128), tl)
                gs[here, lanes_at(width + group * 128)] = gprod[here, tl] * v
                gs[here, lanes_at(2 * width + group * 128)] = gprod[here, tl] * k

        for m in range(3):
            gsend[:, m * width : (m + 1) * width] = gs[0:8, m * width : (m + 1) * width]
        d_copy = remote(gsend, sfar, sems[3], before)
        d_copy.wait_recv()
        gs[rows : rows + 8] = jnp.where(me < n - 1, sfar[...], 0.0)
        row_sum[...] = jnp.zeros_like(row_sum)

        @pl.loop(0, 4)
        def _(group):
            tl = lanes_at(group * 128)
            for m in range(3):
                ml = lanes_at(m * width + group * 128)
                sums = [jnp.zeros((8, 128), F32) for _ in range(3)]
                for a, count in chunks(0, rows, 64):
                    grad = taps1[m : m + 1, tl] * gs[a : a + count, ml]
                    for j in (1, 2):
                        grad = grad + taps1[3 * j + m : 3 * j + m + 1, tl] * gs[a + j : a + j + count, ml]
                    gpb[a : a + count, ml] = grad.astype(BF16)
                    gp_out[a : a + count, ml] = (grad * inv_rows[a : a + count]).astype(BF16)
                    row_sum[a : a + count] += grad * pp[8 + a : 8 + a + count, ml]
                    for j in range(3):
                        term = gs[a : a + count, ml] * pp[8 - j + a : 8 - j + a + count, ml]
                        sums[j] = sums[j] + jnp.sum(term.reshape(count // 8, 8, 128), axis=0)
                for j in range(3):
                    sums_own[REACH + 3 * j + m : REACH + 3 * j + m + 1, tl] = jnp.sum(sums[j], axis=0, keepdims=True)

        eye = lax.broadcasted_iota(jnp.int32, (128, 128), 0) == lax.broadcasted_iota(jnp.int32, (128, 128), 1)
        stat_own[...] = jnp.zeros_like(stat_own)
        for k in range(rows // 128):
            column = jnp.sum(row_sum[k * 128 : (k + 1) * 128], axis=1, keepdims=True)
            line = jnp.sum(jnp.where(eye, jnp.broadcast_to(column, (128, 128)), 0.0), axis=0, keepdims=True)
            stat_own[k : k + 1] = line
        grads = Gather(ctx, gp_out, gp_all, pool, False)
        grads.start()
        stat = Gather(dp, stat_own, stats, pool, True)
        stat.start()

        def produce(slot):
            part[slot] = dot(gpb[...], wv[slot], TRANS_B).astype(BF16)

        RingThenPair(dp, part, pool, ring_bufs).run(total, produce=produce)
        stat.middle()
        stat.finish()
        summed = stats[0]
        for k in range(1, n):
            summed = summed + stats[k]
        for k in range(rows // 128):
            here = pl.ds(k * 128, 128)
            line = jnp.broadcast_to(summed[k : k + 1], (128, 128))
            scalar = jnp.sum(jnp.where(eye, line, 0.0), axis=1, keepdims=True)
            inv = inv_rows[here, :1]
            block[here] = (
                cot[here].astype(F32)
                + inv * total[here]
                - arrived[here].astype(F32) * (inv * inv * scalar / (width * n))
            ).astype(BF16)
        back.start()
        e_over.start()
        x_over.wait_recv()
        columns = Gather(dp, x_col, x_all, pool, True)
        columns.start()
        near.middle()

        @pl.loop(0, 4)
        def _(group):
            tl = lanes_at(group * 128)
            shifted(shifts, prod, 1, rows + REACH - 8, tl)
            lags(shifts, gf, tl, sums_own, tl, rows // 8)

        taps_job = Gather(ctx, sums_own, sums_all, pool, False)
        taps_job.start()
        jobs = [columns, grads, taps_job]
        for job in jobs:
            job.middle()
        for job in [near, cots] + jobs:
            job.finish()
        for copy in (a_copy, b_copy, c_copy, d_copy):
            copy.wait_send()
        back.wait_send()
        e_over.wait_send()


PAIR = (None,) * 5


def end_kernel(
    gg_rows, e_col, e_all, gated_all, proj, taps, kern, filtered, tok, gtab_all, taps_all, grad_out,
    e_got, gg, gf, gprod, gs, prod, shifts, gp, sum_ref, gtab, sums, got, block, *rest,
):
    send, recv = rest
    barrier = pltpu.get_barrier_semaphore()
    ctx, dp = Group("ctx"), Group("dp")
    n = 2 * RING
    place = lax.axis_index("ctx")

    def outer(e_all):
        count, rows, _ = e_all.shape
        grad_out[...] = jnp.zeros_like(grad_out)

        @pl.loop(0, count)
        def _(k):
            here = pl.ds(pl.multiple_of(k * rows, rows), rows)
            grad_out[...] += dot(gated_all[here], e_all[k], TRANS_A)

    @pl.when(section_is(0))
    def _():
        greet([{"ctx": (place + k) % n} for k in range(1, n)] + dp.neighbours(), barrier)
        pl.semaphore_wait(barrier, n + 2)
        pool = Pool(send, recv)
        rows = gg_rows.shape[0]
        over = AHEAD - RING * rows
        sems = pool.take(2 * RING)
        start = pool.count
        pool.count += RING + 1
        spot = place % RING
        yes = place >= 0
        strip_at = lambda x: slice(x * 128, (x + 1) * 128)
        pieces = [
            (
                gg_rows.at[:, strip_at(x)],
                gg.at[pl.ds(pl.multiple_of(spot * rows, rows), rows)],
                2 * x + place // RING,
                sems_of(send, recv, start + spot),
                yes,
            )
            for x in range(RING)
        ] + [
            (
                gg_rows.at[pl.ds(0, over), strip_at(x)],
                gg.at[pl.ds(RING * rows, over)],
                2 * x,
                sems_of(send, recv, start + RING),
                place == RING,
            )
            for x in range(RING)
        ]

        @pl.when(ctx.pair == 1)
        def _():
            gg[pl.ds(RING * rows, over)] = jnp.zeros((over, 128), BF16)

        swap(pieces, sems, place)
        for k in range(RING):
            pltpu.make_async_copy(
                gg_rows.at[:, strip_at(0)], gg.at[pl.ds(k * rows, rows)], sems_of(send, recv, start + k)
            ).wait()

        @pl.when(ctx.pair == 0)
        def _():
            pltpu.make_async_copy(
                gg_rows.at[pl.ds(0, over), strip_at(0)],
                gg.at[pl.ds(RING * rows, over)],
                sems_of(send, recv, start + RING),
            ).wait()

        columns = Gather(dp, e_col, e_got, pool, True)
        columns.start()
        sem = pool.take(1)[0]
        hold = got.shape[0]
        part = gp.shape[0]
        mix_back(gg, proj, taps, kern, filtered, gf, gprod, gs, shifts, gp, part)
        columns.pass_on()
        columns.cross_on()

        sum_ref[...] = jnp.zeros_like(sum_ref)

        @pl.loop(0, part // 128)
        def _(c):
            hot = marks(tok, ctx.pair * (part // 128) + c, sum_ref.shape[0])
            sum_ref[...] += dot(hot, gp[pl.ds(pl.multiple_of(c * 128, 128), 128)])

        gtab[...] = sum_ref[...].astype(BF16)

        halves = lambda p: gtab.at[pl.ds(pl.multiple_of(p * hold, hold), hold)]
        copy = remote(halves(ctx.mate), got, sem, ctx.at(ctx.ring, ctx.mate))
        copy.wait()
        add_into(block, [halves(ctx.pair), got])
        table = Gather(ctx, block, gtab_all, pool, False)
        table.start()
        mix_sums(gf, proj, taps, gs, prod, shifts, sums, part)
        job = Gather(ctx, sums, taps_all, pool, False)
        job.start()
        table.pass_on()
        columns.middle()
        table.middle()
        columns.finish()
        job.pass_on()
        outer(e_got)
        job.middle()
        table.finish()
        job.finish()
        swapped(pieces, sems, place)

    @pl.when(section_is(1))
    def _():
        outer(e_all)


def dot(a, b, dims=(((1,), (0,)), ((), ()))):
    return lax.dot_general(a, b, dims, preferred_element_type=F32)


TRANS_B = (((1,), (1,)), ((), ()))
TRANS_A = (((0,), (0,)), ((), ()))


def local(
    token_ids, embedding, project_in, short_taps, filter_taps, decay_rates, project_out, cotangent
):
    section_zero = lax.axis_index("section") == 0
    n = lax.axis_size("ctx")
    vocab = embedding.shape[0]
    rows = token_ids.shape[0]
    seq = rows * n
    part = seq // 2
    width = embedding.shape[1]
    chans = project_in.shape[3]
    lane = chans // RING
    taps_all = short_taps[0]
    filter_all = filter_taps[0]
    tap_count = filter_all.shape[0]
    strip = lax.axis_index("ctx") // 2

    w_flat = project_in[0].reshape(width, 3 * chans)
    w_out = project_out[0]
    positions = jnp.arange(tap_count).astype(F32)
    damping_all = jnp.exp(-decay_rates[0][None, :] * positions[:, None] / tap_count)
    kernel_all = filter_all * damping_all

    def strip_of(a):
        return lax.dynamic_slice_in_dim(a, strip * lane, lane, a.ndim - 1)

    taps0, kernel0 = strip_of(taps_all), strip_of(kernel_all)

    taps0 = taps0.reshape(9, lane)
    taps1 = taps_all.reshape(9, chans)
    own_tokens = jnp.tile(token_ids.reshape(rows // lane, lane), (16 * lane // rows, 1))
    emb, inv_table, tokens, e_all, gated_all, proj0, filtered0, x_all, gp_all, sums1, gg_rows, e_col = call(
        main_kernel,
        1,
        [
            ((n, vocab // n, width), BF16),
            ((vocab, lane), F32),
            ((n, 16, lane), jnp.int32),
            ((n, rows, width), BF16),
            ((seq, chans), BF16),
            ((BACK + 1280, 3 * lane), F32),
            ((KEPT, lane), F32),
            ((n, rows, width), BF16),
            ((n, rows, 3 * chans), BF16),
            ((n, 144, chans), F32),
            ((rows, chans), BF16),
            ((rows, width), BF16),
        ],
        [
            pltpu.VMEM(shape, dtype)
            for shape, dtype in (
                ((n, rows, width), BF16),
                ((rows, width), BF16),
                ((vocab // 2, 4 * lane), F32),
                ((vocab // n, width), BF16),
                ((vocab, 3 * lane), BF16),
                ((BACK + AHEAD, lane), F32),
                ((8, KEPT + REACH, lane), F32),
                ((part, lane), BF16),
                ((rows, width), BF16),
                ((rows, width), F32),
                ((rows, width), BF16),
                ((n, width, 3 * chans), BF16),
                ((n, chans, width), BF16),
                ((rows, chans), BF16),
                ((rows, chans), F32),
                ((rows, width), BF16),
                ((rows, width), BF16),
                ((n, rows, width), BF16),
                ((rows, width), BF16),
                ((rows, 128), F32),
                ((rows, 128), F32),
                ((rows, 3 * chans), BF16),
                ((rows, 3 * chans), BF16),
                ((rows, chans), BF16),
                ((n, 16, 128), F32),
                ((16, 128), F32),
                ((rows, width), BF16),
                ((144, chans), F32),
                ((rows, chans), F32),
                ((rows + REACH, chans), F32),
                ((REACH, 128), F32),
                ((rows + 8, 3 * chans), F32),
                ((rows, chans), F32),
                ((rows, chans), F32),
                ((rows, chans), F32),
                ((rows + 8, 3 * chans), F32),
                ((8, 3 * chans), F32),
                ((REACH, chans), BF16),
                ((REACH, chans), BF16),
                ((REACH, chans), BF16),
                ((8, 3 * chans), F32),
                ((rows + REACH, chans), F32),
                ((rows, 128), F32),
                ((REACH, chans), BF16),
                ((8, 3 * chans), F32),
            )
        ]
        + PairThenRing.scratch(rows, width)
        + RingThenPair.scratch(rows, width),
        128,
        embedding, w_flat, w_flat, cotangent, own_tokens, w_out, w_out, taps0, kernel0, taps1, kernel_all,
        in_specs=[VMEM, VMEM, ANY] + [VMEM] * 3 + [ANY] + [VMEM] * 4,
        out_specs=[VMEM] * 8 + [ANY] * 2 + [VMEM] * 2,
        name="main",
    )
    emb = emb.reshape(vocab, width)
    gtab, sums0, grad_out = call(
        end_kernel,
        2,
        [((n, vocab // 2, 3 * lane), BF16), ((n, 144, lane), F32), ((chans, width), F32)],
        [
            pltpu.VMEM((n, rows, width), BF16),
            pltpu.VMEM((AHEAD, lane), BF16),
            pltpu.VMEM((AHEAD, lane), F32),
            pltpu.VMEM((KEPT, lane), F32),
            pltpu.VMEM((3, KEPT, lane), F32),
            pltpu.VMEM((BACK + AHEAD, lane), F32),
            pltpu.VMEM((8, KEPT + REACH, lane), F32),
            pltpu.VMEM((part, 3 * lane), BF16),
            pltpu.VMEM((vocab, 3 * lane), F32),
            pltpu.VMEM((vocab, 3 * lane), BF16),
            pltpu.VMEM((144, lane), F32),
            pltpu.VMEM((vocab // 2, 3 * lane), BF16),
            pltpu.VMEM((vocab // 2, 3 * lane), BF16),
        ],
        56,
        gg_rows, e_col, e_all, gated_all, proj0, taps0, kernel0, filtered0, tokens,
        name="end",
    )

    def end0():
        table_rows = jnp.transpose(gtab.reshape(RING, 2, vocab // 2, 3, lane), (1, 2, 3, 0, 4))
        normed_table = (emb.astype(F32) * inv_table[:, :1]).astype(BF16)
        sums = sums0.reshape(RING, 2, 144, lane).sum(axis=1)
        return (
            dot(normed_table, table_rows.reshape(vocab, 3 * chans), TRANS_A),
            jnp.transpose(sums, (1, 0, 2)).reshape(144, chans),
        )

    def end1():
        return (
            dot(x_all.reshape(seq, width), gp_all.reshape(seq, 3 * chans), TRANS_A),
            sums1.sum(axis=0),
        )

    grad_in, sums = lax.cond(section_zero, end0, end1)
    grad_in = grad_in.reshape(width, 3, chans)
    gk, gt = sums[:tap_count], sums[tap_count : tap_count + 9].reshape(3, 3, chans)
    grad_filter = gk * damping_all
    grad_decay = -jnp.sum(gk * kernel_all * positions[:, None], axis=0) / tap_count
    return (grad_in[None], grad_out[None], grad_filter[None], grad_decay[None], gt[None])


def solution(mesh):
    return jax.shard_map(
        local,
        mesh=mesh,
        in_specs=(
            P("ctx"),
            P(None, "dp"),
            P("section", "ctx", None, "dp"),
            P("section", None, None, "dp"),
            P("section", None, "dp"),
            P("section", "dp"),
            P("section", "dp", "ctx"),
            P("ctx", "dp"),
        ),
        out_specs=(
            P("section", "ctx", None, "dp"),
            P("section", "dp", "ctx"),
            P("section", None, "dp"),
            P("section", "dp"),
            P("section", None, None, "dp"),
        ),
        check_vma=False,
    )
```

```python
import functools

import jax
import jax.numpy as jnp
from jax import lax
from jax.experimental import pallas as pl
from jax.experimental.pallas import tpu as pltpu
from jax.sharding import PartitionSpec as P

EPSILON = 1e-06
F32 = jnp.float32
BF16 = jnp.bfloat16
MESH = pl.DeviceIdType.MESH
BACK = 256
AHEAD = 1184
KEPT = 1040
RING = 4
REACH = 128


class Group:
    def __init__(self, axis):
        self.axis = axis
        me = lax.axis_index(axis)
        if axis == "ctx":
            self.ring, self.pair = me // 2, me % 2
        else:
            self.ring, self.pair = me % RING, me // RING
        self.right = (self.ring + 1) % RING
        self.left = (self.ring + RING - 1) % RING
        self.across = (self.ring + 2) % RING
        self.mate = 1 - self.pair

    def slot(self, ring, pair):
        return ring * 2 + pair if self.axis == "ctx" else pair * RING + ring

    def at(self, ring, pair):
        return {self.axis: self.slot(ring, pair)}

    def neighbours(self):
        return [
            self.at(self.right, self.pair),
            self.at(self.left, self.pair),
            self.at(self.ring, self.mate),
        ]


class Pool:
    def __init__(self, send, recv):
        self.send, self.recv, self.count = send, recv, 0

    def take(self, k):
        first = self.count
        self.count += k
        return [(self.send.at[first + i], self.recv.at[first + i]) for i in range(k)]


def remote(src, dst, sems, device):
    copy = pltpu.make_async_remote_copy(
        src_ref=src,
        dst_ref=dst,
        send_sem=sems[0],
        recv_sem=sems[1],
        device_id=device,
        device_id_type=MESH,
    )
    copy.start()
    return copy


def greet(devices, barrier):
    for device in devices:
        pl.semaphore_signal(barrier, inc=1, device_id=device, device_id_type=MESH)


class Gather:
    def __init__(self, group, src, out, pool, pair_first, place=None):
        self.g, self.src, self.out, self.pair_first = group, src, out, pair_first
        self.sems = pool.take(9)
        self.own = pool.take(1)[0]
        self.rows = src.shape[0]
        self.half = self.rows // 2
        self.place = place or (lambda ring, pair, first, rows: out.at[group.slot(ring, pair), pl.ds(first, rows)])

    def block(self, ring, pair):
        return self.place(ring, pair, 0, self.rows)

    def part(self, ring, pair, second):
        return self.place(ring, pair, self.half * second, self.half)

    def start(self):
        g, s = self.g, self.sems
        mine = self.block(g.ring, g.pair)
        right, left, mate = g.neighbours()
        self.local = pltpu.make_async_copy(self.src, mine, self.own[0])
        self.local.start()
        first = remote(self.src, mine, s[0], mate)
        self.copies = [first, remote(self.src, mine, s[1], right), remote(self.src, mine, s[2], left)]

    def turn(self, pair, a, b, c, d):
        g, s = self.g, self.sems
        right, left, mate = g.neighbours()
        more = []
        a.wait_recv()
        part = self.part(g.left, pair, 0)
        more.append(remote(part, part, s[c], right))
        if not self.pair_first:
            block = self.block(g.left, pair)
            more.append(remote(block, block, s[5], mate))
        b.wait_recv()
        part = self.part(g.right, pair, 1)
        more.append(remote(part, part, s[d], left))
        if not self.pair_first:
            block = self.block(g.right, pair)
            more.append(remote(block, block, s[6], mate))
        return more

    def pass_on(self):
        self.passed = self.turn(self.g.pair, self.copies[1], self.copies[2], 3, 4)

    def cross_on(self):
        g, s = self.g, self.sems
        right, left, mate = g.neighbours()
        self.copies[0].wait_recv()
        block = self.block(g.ring, g.mate)
        self.crossed = (remote(block, block, s[5], right), remote(block, block, s[6], left))

    passed = crossed = None

    def middle(self):
        g, s = self.g, self.sems
        right, left, mate = g.neighbours()
        mate_copy, to_right, to_left = self.copies
        if self.passed is None:
            self.pass_on()
        rest = self.passed
        self.sent = list(self.copies) + rest
        if self.pair_first:
            self.late = list(rest)
            if self.crossed is None:
                self.cross_on()
            a, b = self.crossed
            more = self.turn(g.mate, a, b, 7, 8)
            self.sent += [a, b] + more
            self.late += more
        else:
            rest[0].wait_recv()
            rest[2].wait_recv()
            block = self.block(g.across, g.pair)
            last = remote(block, block, s[7], mate)
            self.sent.append(last)
            self.late = [mate_copy, rest[1], rest[3], last]

    def finish(self):
        for copy in self.late:
            copy.wait_recv()
        for copy in self.sent:
            copy.wait_send()
        self.local.wait()


def add_into(out, terms, rows=64):
    @pl.loop(0, out.shape[0] // rows)
    def _(step):
        here = pl.ds(pl.multiple_of(step * rows, rows), rows)
        total = terms[0][here].astype(F32)
        for term in terms[1:]:
            total = total + term[here].astype(F32)
        out[here] = total.astype(out.dtype)


def rows_step(count):
    for rows in (64, 48, 37 * 16, 32, 16):
        if count % rows == 0:
            return rows if rows != 37 * 16 else 16
    return 16


class Around:
    def __init__(self, group, pool, bufs):
        self.g = group
        self.s = pool.take(6)
        self.rel, self.merged, self.came = bufs
        self.half = self.rel.shape[1]

    @staticmethod
    def scratch(rows, lanes):
        half = rows // 2
        return [
            pltpu.VMEM((2, half, lanes), BF16),
            pltpu.VMEM((2, half, lanes), BF16),
            pltpu.VMEM((2, 2, half, lanes), BF16),
        ]

    def halves(self, ref):
        return ref.at[pl.ds(0, self.half)], ref.at[pl.ds(self.half, self.half)]

    def send_across(self, block):
        right, left, _ = self.g.neighbours()
        a, b = self.halves(block)
        self.copies = [remote(a, self.rel.at[0], self.s[0], right), remote(b, self.rel.at[1], self.s[1], left)]

    def send_near(self, to_right, to_left):
        right, left, _ = self.g.neighbours()
        self.to_right, self.to_left = to_right, to_left
        b = self.halves(to_right)[1]
        a = self.halves(to_left)[0]
        self.copies += [
            remote(b, self.came.at[0, 1], self.s[2], right),
            remote(a, self.came.at[1, 0], self.s[3], left),
        ]

    def merge(self):
        right, left, _ = self.g.neighbours()
        step = rows_step(self.half)
        self.copies[0].wait_recv()
        add_into(self.merged.at[0], [self.halves(self.to_right)[0], self.rel.at[0]], step)
        self.copies.append(remote(self.merged.at[0], self.came.at[0, 0], self.s[4], right))
        self.copies[1].wait_recv()
        add_into(self.merged.at[1], [self.halves(self.to_left)[1], self.rel.at[1]], step)
        self.copies.append(remote(self.merged.at[1], self.came.at[1, 1], self.s[5], left))

    def collect(self, out, own):
        step = rows_step(self.half)
        for copy in self.copies[2:]:
            copy.wait_recv()
        for h in range(2):
            piece = pl.ds(h * self.half, self.half)
            add_into(
                out.at[piece],
                [ref.at[piece] for ref in own] + [self.came.at[0, h], self.came.at[1, h]],
                step,
            )

    def finish(self):
        for copy in self.copies:
            copy.wait_send()


class PairThenRing:
    def __init__(self, group, inp, pool, bufs):
        self.g, self.inp = group, inp
        self.got, self.sums = bufs[:2]
        self.ring = Around(group, pool, bufs[2:])
        self.s = pool.take(4)

    @staticmethod
    def scratch(rows, lanes):
        return [pltpu.VMEM((4, rows, lanes), BF16), pltpu.VMEM((4, rows, lanes), BF16)] + Around.scratch(rows, lanes)

    def run(self, out):
        g = self.g
        mate = g.at(g.ring, g.mate)
        order = [g.across, g.right, g.left, g.ring]
        copies = [
            remote(self.inp.at[g.slot(r, g.mate)], self.got.at[k], self.s[k], mate) for k, r in enumerate(order)
        ]
        step = rows_step(self.inp.shape[1])

        def pair_sum(k):
            copies[k].wait_recv()
            add_into(self.sums.at[k], [self.inp.at[g.slot(order[k], g.pair)], self.got.at[k]], step)

        pair_sum(0)
        self.ring.send_across(self.sums.at[0])
        pair_sum(1)
        pair_sum(2)
        self.ring.send_near(self.sums.at[1], self.sums.at[2])
        copies[3].wait_recv()
        self.ring.merge()
        self.ring.collect(out, [self.inp.at[g.slot(g.ring, g.pair)], self.got.at[3]])
        self.ring.finish()
        for copy in copies:
            copy.wait_send()


class RingThenPair:
    def __init__(self, group, inp, pool, bufs):
        self.g, self.inp = group, inp
        self.far, self.got = bufs[:2]
        self.rings = [Around(group, pool, bufs[2:5]), Around(group, pool, bufs[5:8])]
        self.s = pool.take(1)[0]

    @staticmethod
    def scratch(rows, lanes):
        return (
            [pltpu.VMEM((rows, lanes), BF16), pltpu.VMEM((rows, lanes), BF16)]
            + Around.scratch(rows, lanes)
            + Around.scratch(rows, lanes)
        )

    def run(self, out, extra=(), produce=lambda slot: None):
        g = self.g
        pairs = [g.mate, g.pair]
        blocks = lambda ring, pair: self.inp.at[g.slot(ring, pair)]
        for ring, pair in zip(self.rings, pairs):
            produce(g.slot(g.across, pair))
            ring.send_across(blocks(g.across, pair))
            produce(g.slot(g.right, pair))
            produce(g.slot(g.left, pair))
            ring.send_near(blocks(g.right, pair), blocks(g.left, pair))
            produce(g.slot(g.ring, pair))
        self.rings[0].merge()
        self.rings[1].merge()
        self.rings[0].collect(self.far, [blocks(g.ring, g.mate)])
        copy = remote(self.far, self.got, self.s, g.at(g.ring, g.mate))
        self.rings[1].collect(out, [blocks(g.ring, g.pair)])
        copy.wait_recv()
        add_into(out, [out, self.got] + list(extra), rows_step(out.shape[0]))
        copy.wait_send()
        for ring in self.rings:
            ring.finish()


ANY = pl.BlockSpec(memory_space=pl.ANY)
VMEM = pl.BlockSpec(memory_space=pltpu.VMEM)


def call(body, ident, outs, scratch, sems, *args, in_specs=None, out_specs=None, name=None, local=0):
    return pl.pallas_call(
        body,
        out_shape=[jax.ShapeDtypeStruct(shape, dtype) for shape, dtype in outs],
        in_specs=in_specs or [VMEM] * len(args),
        out_specs=out_specs or [VMEM] * len(outs),
        scratch_shapes=list(scratch)
        + [pltpu.SemaphoreType.DMA((sems,)), pltpu.SemaphoreType.DMA((sems,))]
        + ([pltpu.SemaphoreType.DMA((local,))] if local else []),
        compiler_params=pltpu.CompilerParams(
            collective_id=ident, has_side_effects=True, vmem_limit_bytes=60 * 1024 * 1024
        ),
        name=name,
    )(*args)


def section_is(k):
    return lax.axis_index("section") == k


def crossing():
    i, j = lax.axis_index("dp"), lax.axis_index("ctx")
    return {"dp": j, "ctx": i}, i != j


def other_section():
    i, j = lax.axis_index("dp"), lax.axis_index("ctx")
    return {"section": 1 - lax.axis_index("section"), "dp": j, "ctx": i}


def lanes_at(first):
    return pl.ds(pl.multiple_of(first, 128), 128)


def shifted(shifts, ref, start, rows, lanes):
    for r in range(8):
        for a in range(0, rows, 64):
            count = min(64, rows - a)
            shifts[r, a : a + count] = ref[start + r + a : start + r + a + count, lanes]


def fir(shifts, kern, lanes, out, out_lanes, tiles, block, backwards):
    @pl.loop(0, tiles // block)
    def _(b):
        first = pl.multiple_of(b * block * 8, 8)

        def step(r, totals):
            totals = list(totals)
            taps = []
            for q in range(REACH // 8):
                u = 8 * q + r
                taps.append(kern[pl.ds(REACH - 1 - u if backwards else u, 8, stride=0), lanes])
            for i in range(block + REACH // 8 - 1):
                x = shifts[r, pl.ds(first + 8 * i, 8)]
                for o in range(block):
                    if 0 <= i - o < REACH // 8:
                        totals[o] = totals[o] + taps[i - o] * x
            return tuple(totals)

        totals = lax.fori_loop(0, 8, step, tuple(jnp.zeros((8, 128), F32) for _ in range(block)))
        for o in range(block):
            out[pl.ds(first + 8 * o, 8), out_lanes] = totals[o]


def lags(shifts, ref, lanes, out, out_lanes, tiles):
    for r in range(8):

        def step(b, totals):
            totals = list(totals)
            first = pl.multiple_of(b * 32, 8)
            own = [ref[pl.ds(first + 8 * o, 8), lanes] for o in range(4)]
            for i in range(4 + REACH // 8 - 1):
                x = shifts[r, pl.ds(first + 8 * i, 8)]
                for o in range(4):
                    if 0 <= i - o < REACH // 8:
                        totals[i - o] = totals[i - o] + own[o] * x
            return tuple(totals)

        totals = lax.fori_loop(0, tiles // 4, step, tuple(jnp.zeros((8, 128), F32) for _ in range(REACH // 8)))
        for q in range(REACH // 8):
            row = REACH - 1 - (8 * q + r)
            out[row : row + 1, out_lanes] = jnp.sum(totals[q], axis=0, keepdims=True)


def chunks(first, last, size):
    for a in range(first, last, size):
        yield a, min(size, last - a)


def short_rows(ref, taps, m, a, count, lanes, tap_lanes):
    total = taps[m : m + 1, tap_lanes] * ref[a : a + count, lanes]
    for j in (1, 2):
        total = total + taps[3 * j + m : 3 * j + m + 1, tap_lanes] * ref[a - j : a - j + count, lanes]
    return total


ALL = slice(0, 128)


def stream(m):
    return slice(m * 128, (m + 1) * 128)


def mix_first(proj, taps, kern, filtered, prod, shifts, gated, part):
    for a, count in chunks(BACK - REACH, BACK + part, 64):
        prod[a : a + count] = short_rows(proj, taps, 1, a, count, stream(1), ALL) * short_rows(
            proj, taps, 2, a, count, stream(2), ALL
        )
    for a, count in chunks(BACK + part, BACK + AHEAD, 64):
        prod[a : a + count] = short_rows(proj, taps, 1, a, count, stream(1), ALL) * short_rows(
            proj, taps, 2, a, count, stream(2), ALL
        )
    shifted(shifts, prod, BACK - REACH + 1, KEPT + REACH, ALL)
    fir(shifts, kern, ALL, filtered, ALL, KEPT // 8, 10, True)
    for a, count in chunks(0, part, 64):
        query = short_rows(proj, taps, 0, BACK + a, count, stream(0), ALL)
        gated[a : a + count] = (query * filtered[a : a + count]).astype(BF16)


def mix_back(gg, proj, taps, kern, filtered, gf, gprod, gs, shifts, gp, part):
    for a, count in chunks(0, AHEAD, 64):
        gf[a : a + count] = gg[a : a + count] * short_rows(proj, taps, 0, BACK + a, count, stream(0), ALL)
    shifted(shifts, gf, 0, KEPT + REACH, ALL)
    fir(shifts, kern, ALL, gprod, ALL, KEPT // 8, 10, False)
    for a, count in chunks(0, KEPT, 64):
        here = slice(a, a + count)
        gs[0, here] = gg[here] * filtered[here]
        gs[1, here] = gprod[here] * short_rows(proj, taps, 2, BACK + a, count, stream(2), ALL)
        gs[2, here] = gprod[here] * short_rows(proj, taps, 1, BACK + a, count, stream(1), ALL)
    for m in range(3):
        for a, count in chunks(0, part, 64):
            total = taps[m : m + 1] * gs[m, a : a + count]
            for j in (1, 2):
                total = total + taps[3 * j + m : 3 * j + m + 1] * gs[m, a + j : a + j + count]
            gp[a : a + count, stream(m)] = total.astype(BF16)


def mix_sums(gf, proj, taps, gs, prod, shifts, out, part):
    for a, count in chunks(BACK - REACH, BACK + part + 8, 64):
        prod[a : a + count] = short_rows(proj, taps, 1, a, count, stream(1), ALL) * short_rows(
            proj, taps, 2, a, count, stream(2), ALL
        )
    shifted(shifts, prod, BACK - REACH + 1, part + REACH, ALL)
    lags(shifts, gf, ALL, out, ALL, part // 8)
    out[REACH:] = jnp.zeros((16, 128), F32)
    for m in range(3):
        for j in range(3):
            total = jnp.zeros((8, 128), F32)
            for a, count in chunks(0, part, 64):
                term = gs[m, a : a + count] * proj[BACK - j + a : BACK - j + a + count, stream(m)]
                total = total + jnp.sum(term.reshape(count // 8, 8, 128), axis=0)
            row = REACH + 3 * j + m
            out[row : row + 1] = jnp.sum(total, axis=0, keepdims=True)


def by_rows(group, out, rows):
    def place(ring, pair, first, count):
        start = group.slot(ring, pair) * rows + first
        return out.at[pl.ds(pl.multiple_of(start, count), count)]

    return place


def by_strip(out, part):
    def place(ring, pair, first, count):
        return out.at[pl.ds(pl.multiple_of(pair * part + first, count), count), lanes_at(ring * 128)]

    return place


def marks(tok, q, vocab):
    inside = jnp.clip(q, 0, 4 * RING - 1)
    ids = tok[inside // 2, pl.ds(inside % 2, 1)]
    ids = jnp.where(q == inside, ids, -1)
    return jnp.where(lax.broadcasted_iota(jnp.int32, (vocab, 128), 0) == ids, 1.0, 0.0).astype(BF16)


def sems_of(send, recv, k):
    return recv.at[k]


def use_rows(out, blocks, weights, gather, dp, own):
    term = lambda ref, slot: dot(ref[...], weights[slot], TRANS_B)
    slot = dp.slot(dp.ring, dp.pair)
    out[...] = term(own, slot)
    gather.middle()
    near = ((dp.left, dp.pair), (dp.right, dp.pair), (dp.ring, dp.mate), (dp.left, dp.mate), (dp.right, dp.mate))
    for ring, pair in near:
        slot = dp.slot(ring, pair)
        out[...] += term(blocks.at[slot], slot)
    gather.finish()
    for pair in (dp.pair, dp.mate):
        slot = dp.slot(dp.across, pair)
        out[...] += term(blocks.at[slot], slot)


def swap(pieces, sems, me):
    for k, (src, dst, to, sem, when) in enumerate(pieces):
        far = jnp.logical_and(when, to != me)
        near = jnp.logical_and(when, to == me)
        away = pltpu.make_async_remote_copy(
            src_ref=src, dst_ref=dst, send_sem=sems[k][0], recv_sem=sem, device_id={"ctx": to}, device_id_type=MESH
        )
        here = pltpu.make_async_copy(src, dst, sem)
        pl.when(far)(away.start)
        pl.when(near)(here.start)


def swapped(pieces, sems, me):
    for k, (src, dst, to, sem, when) in enumerate(pieces):
        away = pltpu.make_async_remote_copy(
            src_ref=src, dst_ref=dst, send_sem=sems[k][0], recv_sem=sem, device_id={"ctx": to}, device_id_type=MESH
        )
        pl.when(jnp.logical_and(when, to != me))(away.wait_send)


def main_kernel(
    emb_ref, w_ref, w_far, cot_ref, tok_ref, w_proj, wo_far, taps0, kern0, taps1, kern1,
    emb_out, inv_out, tok_out, e_all, gated_all, proj0, filtered0, x_all, gp_all, sums_all, gg_rows, e_col,
    part, crossed, half_out, piece, table, prod0, shifts, gated0, first_rows, total, x_block,
    wv, wo, gated_own, gg, arrived, returned, all_ref, x_col, square, inv_rows, gp_out, gpb, gated_out, stats, stat_own, block, sums_own, gf, prod,
    kg, pp, query, filtered, gprod, gs, ptail, qtail, ghead, gfar, sfar, gfpad, row_sum, qsend, gsend, *rest,
):
    pair_bufs, ring_bufs = rest[: len(PAIR)], rest[len(PAIR) : -2]
    send, recv = rest[-2:]
    barrier = pltpu.get_barrier_semaphore()
    ctx, dp = Group("ctx"), Group("dp")
    partner, apart = crossing()
    n = 2 * RING
    me = lax.axis_index("dp")
    place = lax.axis_index("ctx")
    others = [{"dp": (me + k) % n} for k in range(1, n)]
    after, before = {"ctx": (place + 1) % n}, {"ctx": (place + n - 1) % n}
    along = [{"ctx": (place + k) % n} for k in range(1, n)]
    opposite = {"section": 1 - lax.axis_index("section")}
    greet(along + others + [other_section(), opposite], barrier)
    for k in range(n):
        pl.when(jnp.logical_or(apart, place != k))(functools.partial(greet, [{"dp": place, "ctx": k}], barrier))
    pl.semaphore_wait(barrier, 3 * n - 1 + jnp.where(apart, 1, 0))
    lane = 128
    strips = RING
    common = Pool(send, recv)
    cross_sem = common.take(1)[0]
    same_sem = common.take(1)[0]
    pair_sems = common.take(2)
    relay = common.take(4)

    def handed(src, dst, k, device):
        return pltpu.make_async_remote_copy(
            src_ref=src, dst_ref=dst, send_sem=relay[k][0], recv_sem=relay[k][1],
            device_id=device, device_id_type=MESH,
        )

    forth = handed(x_block, arrived, 0, opposite)
    back = handed(block, returned, 1, opposite)
    x_over = handed(x_block, x_col, 2, other_section())
    e_over = handed(block, e_col, 3, other_section())

    @pl.when(section_is(0))
    def _():
        pool = Pool(send, recv)
        pool.count = common.count
        tokens = Gather(ctx, tok_ref, tok_out, pool, False)
        tokens.start()
        outs = Gather(ctx, wo_far, wo, pool, False)
        outs.start()
        spread = pool.take(n - 1)
        share = piece.shape[0]
        share_of = lambda k: emb_ref.at[pl.ds(pl.multiple_of(k * share, share), share)]
        keep = pltpu.make_async_copy(share_of(me), piece, same_sem[0])
        copies = [
            pltpu.make_async_remote_copy(
                src_ref=share_of((me + k + 1) % n), dst_ref=piece, send_sem=spread[k][0],
                recv_sem=cross_sem[1], device_id=device, device_id_type=MESH,
            )
            for k, device in enumerate(others)
        ]

        @pl.when(jnp.logical_not(apart))
        def _():
            for copy in copies:
                copy.start()
            keep.start()
            keep.wait()

        @pl.when(apart)
        def _():
            copies[0].wait_recv()

        table_rows = Gather(dp, piece, emb_out, pool, True)
        table_rows.start()
        tokens.middle()
        table_rows.middle()
        table_rows.finish()

        @pl.when(jnp.logical_not(apart))
        def _():
            for copy in copies:
                copy.wait_send()

        vocab, width = emb_ref.shape
        hold = vocab // 2
        for core in range(2):
            values = emb_out[core * RING : (core + 1) * RING].reshape(hold, width).astype(F32)
            square = jnp.broadcast_to(jnp.sum(values * values, axis=1, keepdims=True), (hold, lane)).astype(BF16)
            for strip in range(strips):
                part[strip * 2 + core, :, 3 * lane :] = square

        @pl.loop(0, 3 * strips)
        def _(k):
            strip, m = k // 3, k % 3
            columns = pl.ds(pl.multiple_of(m * strips * lane + strip * lane, lane), lane)
            product = jnp.dot(emb_out[...].reshape(vocab, width), w_ref[:, columns], preferred_element_type=F32).astype(BF16)
            to = pl.ds(pl.multiple_of(m * lane, lane), lane)
            part[strip * 2, :, to] = product[:hold]
            part[strip * 2 + 1, :, to] = product[hold:]

        PairThenRing(ctx, part, pool, pair_bufs).run(half_out)
        outs.pass_on()
        here = pl.ds(pl.multiple_of(ctx.pair * hold, hold), hold)
        whole = half_out[...]
        inv = lax.rsqrt(whole[:, 3 * lane :] / (width * 2 * RING) + EPSILON)
        inv_out[here] = inv
        for m in range(3):
            table[here, m * lane : (m + 1) * lane] = (whole[:, m * lane : (m + 1) * lane] * inv).astype(BF16)
        mate = ctx.at(ctx.ring, ctx.mate)
        a = remote(inv_out.at[here], inv_out.at[here], pair_sems[0], mate)
        b = remote(table.at[here], table.at[here], pair_sems[1], mate)
        tokens.finish()
        a.wait()
        b.wait()


        @pl.loop(0, (BACK + 1280) // 128)
        def _(c):
            hot = marks(tok_out, ctx.pair * (n * 128 // 128) - BACK // 128 + c, vocab)
            proj0[pl.ds(pl.multiple_of(c * 128, 128), 128)] = dot(hot, table[...], TRANS_A)

        for k in range(2):
            hot = marks(tok_out, 2 * place + k, vocab)
            first_rows[k * 128 : (k + 1) * 128] = dot(hot, emb_ref[...], TRANS_A).astype(BF16)
        outs.middle()
        span = gated0.shape[0]
        mix_first(proj0, taps0, kern0, filtered0, prod0, shifts, gated0, span)
        rows = x_block.shape[0]
        sems = pool.take(RING)
        yes = place >= 0
        pieces = [
            (
                gated0.at[pl.ds(k * rows, rows)],
                gated_own.at[:, lanes_at(ctx.ring * 128)],
                ctx.pair * RING + k,
                sems_of(send, recv, pool.count + ctx.ring),
                yes,
            )
            for k in range(RING)
        ]
        pool.count += RING
        swap(pieces, sems, place)
        outs.finish()
        for k in range(RING):
            pltpu.make_async_copy(
                gated0.at[pl.ds(0, rows)], gated_own.at[:, lanes_at(k * 128)], sems_of(send, recv, pool.count - RING + k)
            ).wait()
        swapped(pieces, sems, place)

        def produce(slot):
            part[slot] = dot(gated_own[...], wo[slot]).astype(BF16)

        RingThenPair(dp, part, pool, ring_bufs).run(total, [first_rows], produce)
        x_block[...] = total[...].astype(BF16)
        forth.start()
        forth.wait_send()
        x_over.start()
        job = Gather(ctx, gated0, gated_all, pool, False, by_strip(gated_all, span))
        job.start()
        job.middle()
        job.finish()
        x_over.wait_send()
        back.wait_recv()
        gather = Gather(dp, returned, all_ref, pool, True)
        gather.start()
        use_rows(gg, all_ref, wo, gather, dp, returned)
        gg_rows[...] = gg[...].astype(BF16)
        e_over.wait_recv()

    @pl.when(section_is(1))
    def _():
        pool = Pool(send, recv)
        pool.count = common.count
        rows, width = gg.shape
        me = lax.axis_index("ctx")
        cot = cot_ref
        outs = Gather(ctx, wo_far, wo, pool, False)
        weights = Gather(ctx, w_far, wv, pool, False)
        there = pltpu.make_async_remote_copy(
            src_ref=cot_ref, dst_ref=crossed, send_sem=cross_sem[0], recv_sem=cross_sem[1],
            device_id=partner, device_id_type=MESH,
        )
        here = pltpu.make_async_copy(cot_ref, crossed, same_sem[0])
        pl.when(apart)(there.start)
        pl.when(jnp.logical_not(apart))(here.start)
        turned = Gather(dp, cot_ref, part, pool, True)
        turned.start()
        outs.start()
        weights.start()
        turned.middle()
        turned.finish()
        outs.pass_on()
        pl.when(apart)(there.wait)
        pl.when(jnp.logical_not(apart))(here.wait)
        cots = Gather(dp, crossed, e_all, pool, True)
        cots.start()
        weights.pass_on()
        outs.middle()
        outs.finish()
        cots.pass_on()
        cots.cross_on()
        gg[...] = jnp.zeros_like(gg)
        for k in range(n):
            gg[...] += dot(part[k], wo[k], TRANS_B)
        weights.middle()
        weights.finish()
        sums_own[REACH:] = jnp.zeros((16, width), F32)
        forth.wait_recv()
        gather = Gather(dp, arrived, all_ref, pool, True)
        gather.start()

        def use(ref, slot, begin=False):
            values = ref[...]
            for m in range(3):
                ml = slice(m * width, (m + 1) * width)
                term = dot(values, wv[slot, :, ml])
                pp[8:, ml] = term if begin else pp[8:, ml] + term
            term = jnp.zeros((rows, 128), F32)
            for g in range(width // 128):
                v = values[:, g * 128 : (g + 1) * 128].astype(F32)
                term = term + v * v
            square[...] = term if begin else square[...] + term

        use(arrived, dp.slot(dp.ring, dp.pair), True)
        gather.middle()
        for ring, pair in ((dp.left, dp.pair), (dp.right, dp.pair), (dp.ring, dp.mate), (dp.left, dp.mate), (dp.right, dp.mate)):
            use(gather.block(ring, pair), dp.slot(ring, pair))
        gather.finish()
        for pair in (dp.pair, dp.mate):
            use(gather.block(dp.across, pair), dp.slot(dp.across, pair))
        inv = lax.rsqrt(jnp.sum(square[...], axis=1, keepdims=True) / (width * n) + EPSILON)
        inv_rows[...] = jnp.broadcast_to(inv, (rows, 128))
        for a, count in chunks(0, rows, 32):
            pp[8 + a : 8 + a + count] = pp[8 + a : 8 + a + count] * inv_rows[a : a + count, :1]

        sems = pool.take(4)
        a_copy = remote(pp.at[pl.ds(rows, 8)], ptail, sems[0], after)

        def products(a, count, group):
            tl = lanes_at(group * 128)
            k = short_rows(pp, taps1, 1, a, count, lanes_at(width + group * 128), tl)
            v = short_rows(pp, taps1, 2, a, count, lanes_at(2 * width + group * 128), tl)
            return k * v

        @pl.loop(0, 4)
        def _(group):
            tl = lanes_at(group * 128)
            for a, count in chunks(rows // 2, rows, 64):
                value = products(8 + a, count, group)
                prod[REACH + a : REACH + a + count, tl] = value
                qsend[a - rows // 2 : a - rows // 2 + count, tl] = value.astype(BF16)

        b_copy = remote(qsend, qtail, sems[1], after)
        a_copy.wait_recv()
        pp[0:8] = jnp.where(me > 0, ptail[...], 0.0)

        @pl.loop(0, 4)
        def _(group):
            tl = lanes_at(group * 128)
            for a, count in chunks(0, rows, 64):
                value = short_rows(pp, taps1, 0, 8 + a, count, tl, tl)
                query[a : a + count, tl] = value
                value = value * gg[a : a + count, tl]
                gf[a : a + count, tl] = value
                gfpad[a : a + count, tl] = value
                if a < REACH:
                    ghead[a : a + count, tl] = value.astype(BF16)
            for a, count in chunks(0, rows // 2, 64):
                prod[REACH + a : REACH + a + count, tl] = products(8 + a, count, group)

        c_copy = remote(ghead, gfar, sems[2], before)
        b_copy.wait_recv()
        for a, count in chunks(0, REACH, 32):
            prod[a : a + count] = jnp.where(me > 0, qtail[a : a + count].astype(F32), 0.0)

        @pl.loop(0, 4)
        def _(group):
            tl = lanes_at(group * 128)
            shifted(shifts, prod, 1, rows + REACH - 8, tl)
            kg[...] = kern1[:, tl]
            fir(shifts, kg, ALL, filtered, tl, rows // 8, 8, True)
            for a, count in chunks(0, rows, 64):
                gated_out[a : a + count, tl] = (query[a : a + count, tl] * filtered[a : a + count, tl]).astype(BF16)

        near = Gather(ctx, gated_out, gated_all, pool, False, by_rows(ctx, gated_all, rows))
        near.start()
        c_copy.wait_recv()
        for a, count in chunks(0, REACH, 32):
            gfpad[rows + a : rows + a + count] = jnp.where(me < n - 1, gfar[a : a + count].astype(F32), 0.0)

        @pl.loop(0, 4)
        def _(group):
            tl = lanes_at(group * 128)
            shifted(shifts, gfpad, 0, rows + REACH - 8, tl)
            kg[...] = kern1[:, tl]
            fir(shifts, kg, ALL, gprod, tl, rows // 8, 8, False)
            for a, count in chunks(0, rows, 64):
                here = slice(a, a + count)
                gs[here, tl] = gg[here, tl] * filtered[here, tl]
                k = short_rows(pp, taps1, 1, 8 + a, count, lanes_at(width + group * 128), tl)
                v = short_rows(pp, taps1, 2, 8 + a, count, lanes_at(2 * width + group * 128), tl)
                gs[here, lanes_at(width + group * 128)] = gprod[here, tl] * v
                gs[here, lanes_at(2 * width + group * 128)] = gprod[here, tl] * k

        for m in range(3):
            gsend[:, m * width : (m + 1) * width] = gs[0:8, m * width : (m + 1) * width]
        d_copy = remote(gsend, sfar, sems[3], before)
        d_copy.wait_recv()
        gs[rows : rows + 8] = jnp.where(me < n - 1, sfar[...], 0.0)
        row_sum[...] = jnp.zeros_like(row_sum)

        @pl.loop(0, 4)
        def _(group):
            tl = lanes_at(group * 128)
            for m in range(3):
                ml = lanes_at(m * width + group * 128)
                sums = [jnp.zeros((8, 128), F32) for _ in range(3)]
                for a, count in chunks(0, rows, 64):
                    grad = taps1[m : m + 1, tl] * gs[a : a + count, ml]
                    for j in (1, 2):
                        grad = grad + taps1[3 * j + m : 3 * j + m + 1, tl] * gs[a + j : a + j + count, ml]
                    gpb[a : a + count, ml] = grad.astype(BF16)
                    gp_out[a : a + count, ml] = (grad * inv_rows[a : a + count]).astype(BF16)
                    row_sum[a : a + count] += grad * pp[8 + a : 8 + a + count, ml]
                    for j in range(3):
                        term = gs[a : a + count, ml] * pp[8 - j + a : 8 - j + a + count, ml]
                        sums[j] = sums[j] + jnp.sum(term.reshape(count // 8, 8, 128), axis=0)
                for j in range(3):
                    sums_own[REACH + 3 * j + m : REACH + 3 * j + m + 1, tl] = jnp.sum(sums[j], axis=0, keepdims=True)

        eye = lax.broadcasted_iota(jnp.int32, (128, 128), 0) == lax.broadcasted_iota(jnp.int32, (128, 128), 1)
        stat_own[...] = jnp.zeros_like(stat_own)
        for k in range(rows // 128):
            column = jnp.sum(row_sum[k * 128 : (k + 1) * 128], axis=1, keepdims=True)
            line = jnp.sum(jnp.where(eye, jnp.broadcast_to(column, (128, 128)), 0.0), axis=0, keepdims=True)
            stat_own[k : k + 1] = line
        grads = Gather(ctx, gp_out, gp_all, pool, False)
        grads.start()
        stat = Gather(dp, stat_own, stats, pool, True)
        stat.start()

        def produce(slot):
            part[slot] = dot(gpb[...], wv[slot], TRANS_B).astype(BF16)

        RingThenPair(dp, part, pool, ring_bufs).run(total, produce=produce)
        stat.middle()
        stat.finish()
        summed = stats[0]
        for k in range(1, n):
            summed = summed + stats[k]
        for k in range(rows // 128):
            here = pl.ds(k * 128, 128)
            line = jnp.broadcast_to(summed[k : k + 1], (128, 128))
            scalar = jnp.sum(jnp.where(eye, line, 0.0), axis=1, keepdims=True)
            inv = inv_rows[here, :1]
            block[here] = (
                cot[here].astype(F32)
                + inv * total[here]
                - arrived[here].astype(F32) * (inv * inv * scalar / (width * n))
            ).astype(BF16)
        back.start()
        e_over.start()
        x_over.wait_recv()
        columns = Gather(dp, x_col, x_all, pool, True)
        columns.start()
        near.middle()

        @pl.loop(0, 4)
        def _(group):
            tl = lanes_at(group * 128)
            shifted(shifts, prod, 1, rows + REACH - 8, tl)
            lags(shifts, gf, tl, sums_own, tl, rows // 8)

        taps_job = Gather(ctx, sums_own, sums_all, pool, False)
        taps_job.start()
        cots.middle()
        jobs = [columns, grads, taps_job]
        for job in jobs:
            job.middle()
        for job in [near, cots] + jobs:
            job.finish()
        for copy in (a_copy, b_copy, c_copy, d_copy):
            copy.wait_send()
        back.wait_send()
        e_over.wait_send()


PAIR = (None,) * 5


def end_kernel(
    gg_rows, e_col, e_all, gated_all, proj, taps, kern, filtered, tok, gtab_all, taps_all, grad_out,
    e_got, gg, gf, gprod, gs, prod, shifts, gp, sum_ref, gtab, sums, got, block, *rest,
):
    send, recv = rest
    barrier = pltpu.get_barrier_semaphore()
    ctx, dp = Group("ctx"), Group("dp")
    n = 2 * RING
    place = lax.axis_index("ctx")

    def outer(e_all):
        count, rows, _ = e_all.shape
        grad_out[...] = jnp.zeros_like(grad_out)

        @pl.loop(0, count)
        def _(k):
            here = pl.ds(pl.multiple_of(k * rows, rows), rows)
            grad_out[...] += dot(gated_all[here], e_all[k], TRANS_A)

    @pl.when(section_is(0))
    def _():
        greet([{"ctx": (place + k) % n} for k in range(1, n)] + dp.neighbours(), barrier)
        pl.semaphore_wait(barrier, n + 2)
        pool = Pool(send, recv)
        rows = gg_rows.shape[0]
        over = AHEAD - RING * rows
        sems = pool.take(2 * RING)
        start = pool.count
        pool.count += RING + 1
        spot = place % RING
        yes = place >= 0
        strip_at = lambda x: slice(x * 128, (x + 1) * 128)
        pieces = [
            (
                gg_rows.at[:, strip_at(x)],
                gg.at[pl.ds(pl.multiple_of(spot * rows, rows), rows)],
                2 * x + place // RING,
                sems_of(send, recv, start + spot),
                yes,
            )
            for x in range(RING)
        ] + [
            (
                gg_rows.at[pl.ds(0, over), strip_at(x)],
                gg.at[pl.ds(RING * rows, over)],
                2 * x,
                sems_of(send, recv, start + RING),
                place == RING,
            )
            for x in range(RING)
        ]

        @pl.when(ctx.pair == 1)
        def _():
            gg[pl.ds(RING * rows, over)] = jnp.zeros((over, 128), BF16)

        swap(pieces, sems, place)
        for k in range(RING):
            pltpu.make_async_copy(
                gg_rows.at[:, strip_at(0)], gg.at[pl.ds(k * rows, rows)], sems_of(send, recv, start + k)
            ).wait()

        @pl.when(ctx.pair == 0)
        def _():
            pltpu.make_async_copy(
                gg_rows.at[pl.ds(0, over), strip_at(0)],
                gg.at[pl.ds(RING * rows, over)],
                sems_of(send, recv, start + RING),
            ).wait()

        columns = Gather(dp, e_col, e_got, pool, True)
        columns.start()
        sem = pool.take(1)[0]
        hold = got.shape[0]
        part = gp.shape[0]
        mix_back(gg, proj, taps, kern, filtered, gf, gprod, gs, shifts, gp, part)
        columns.pass_on()
        columns.cross_on()

        sum_ref[...] = jnp.zeros_like(sum_ref)

        @pl.loop(0, part // 128)
        def _(c):
            hot = marks(tok, ctx.pair * (part // 128) + c, sum_ref.shape[0])
            sum_ref[...] += dot(hot, gp[pl.ds(pl.multiple_of(c * 128, 128), 128)])

        gtab[...] = sum_ref[...].astype(BF16)

        halves = lambda p: gtab.at[pl.ds(pl.multiple_of(p * hold, hold), hold)]
        copy = remote(halves(ctx.mate), got, sem, ctx.at(ctx.ring, ctx.mate))
        copy.wait()
        add_into(block, [halves(ctx.pair), got])
        table = Gather(ctx, block, gtab_all, pool, False)
        table.start()
        mix_sums(gf, proj, taps, gs, prod, shifts, sums, part)
        job = Gather(ctx, sums, taps_all, pool, False)
        job.start()
        table.pass_on()
        columns.middle()
        table.middle()
        columns.finish()
        job.pass_on()
        outer(e_got)
        job.middle()
        table.finish()
        job.finish()
        swapped(pieces, sems, place)

    @pl.when(section_is(1))
    def _():
        outer(e_all)


def dot(a, b, dims=(((1,), (0,)), ((), ()))):
    return lax.dot_general(a, b, dims, preferred_element_type=F32)


TRANS_B = (((1,), (1,)), ((), ()))
TRANS_A = (((0,), (0,)), ((), ()))


def local(
    token_ids, embedding, project_in, short_taps, filter_taps, decay_rates, project_out, cotangent
):
    section_zero = lax.axis_index("section") == 0
    n = lax.axis_size("ctx")
    vocab = embedding.shape[0]
    rows = token_ids.shape[0]
    seq = rows * n
    part = seq // 2
    width = embedding.shape[1]
    chans = project_in.shape[3]
    lane = chans // RING
    taps_all = short_taps[0]
    filter_all = filter_taps[0]
    tap_count = filter_all.shape[0]
    strip = lax.axis_index("ctx") // 2

    w_flat = project_in[0].reshape(width, 3 * chans)
    w_out = project_out[0]
    positions = jnp.arange(tap_count).astype(F32)
    damping_all = jnp.exp(-decay_rates[0][None, :] * positions[:, None] / tap_count)
    kernel_all = filter_all * damping_all

    def strip_of(a):
        return lax.dynamic_slice_in_dim(a, strip * lane, lane, a.ndim - 1)

    taps0, kernel0 = strip_of(taps_all), strip_of(kernel_all)

    taps0 = taps0.reshape(9, lane)
    taps1 = taps_all.reshape(9, chans)
    own_tokens = jnp.tile(token_ids.reshape(rows // lane, lane), (16 * lane // rows, 1))
    emb, inv_table, tokens, e_all, gated_all, proj0, filtered0, x_all, gp_all, sums1, gg_rows, e_col = call(
        main_kernel,
        1,
        [
            ((n, vocab // n, width), BF16),
            ((vocab, lane), F32),
            ((n, 16, lane), jnp.int32),
            ((n, rows, width), BF16),
            ((seq, chans), BF16),
            ((BACK + 1280, 3 * lane), F32),
            ((KEPT, lane), F32),
            ((n, rows, width), BF16),
            ((n, rows, 3 * chans), BF16),
            ((n, 144, chans), F32),
            ((rows, chans), BF16),
            ((rows, width), BF16),
        ],
        [
            pltpu.VMEM(shape, dtype)
            for shape, dtype in (
                ((n, rows, width), BF16),
                ((rows, width), BF16),
                ((vocab // 2, 4 * lane), F32),
                ((vocab // n, width), BF16),
                ((vocab, 3 * lane), BF16),
                ((BACK + AHEAD, lane), F32),
                ((8, KEPT + REACH, lane), F32),
                ((part, lane), BF16),
                ((rows, width), BF16),
                ((rows, width), F32),
                ((rows, width), BF16),
                ((n, width, 3 * chans), BF16),
                ((n, chans, width), BF16),
                ((rows, chans), BF16),
                ((rows, chans), F32),
                ((rows, width), BF16),
                ((rows, width), BF16),
                ((n, rows, width), BF16),
                ((rows, width), BF16),
                ((rows, 128), F32),
                ((rows, 128), F32),
                ((rows, 3 * chans), BF16),
                ((rows, 3 * chans), BF16),
                ((rows, chans), BF16),
                ((n, 16, 128), F32),
                ((16, 128), F32),
                ((rows, width), BF16),
                ((144, chans), F32),
                ((rows, chans), F32),
                ((rows + REACH, chans), F32),
                ((REACH, 128), F32),
                ((rows + 8, 3 * chans), F32),
                ((rows, chans), F32),
                ((rows, chans), F32),
                ((rows, chans), F32),
                ((rows + 8, 3 * chans), F32),
                ((8, 3 * chans), F32),
                ((REACH, chans), BF16),
                ((REACH, chans), BF16),
                ((REACH, chans), BF16),
                ((8, 3 * chans), F32),
                ((rows + REACH, chans), F32),
                ((rows, 128), F32),
                ((REACH, chans), BF16),
                ((8, 3 * chans), F32),
            )
        ]
        + PairThenRing.scratch(rows, width)
        + RingThenPair.scratch(rows, width),
        128,
        embedding, w_flat, w_flat, cotangent, own_tokens, w_out, w_out, taps0, kernel0, taps1, kernel_all,
        in_specs=[VMEM, VMEM, ANY] + [VMEM] * 3 + [ANY] + [VMEM] * 4,
        out_specs=[VMEM] * 8 + [ANY] * 2 + [VMEM] * 2,
        name="main",
    )
    emb = emb.reshape(vocab, width)
    gtab, sums0, grad_out = call(
        end_kernel,
        2,
        [((n, vocab // 2, 3 * lane), BF16), ((n, 144, lane), F32), ((chans, width), F32)],
        [
            pltpu.VMEM((n, rows, width), BF16),
            pltpu.VMEM((AHEAD, lane), BF16),
            pltpu.VMEM((AHEAD, lane), F32),
            pltpu.VMEM((KEPT, lane), F32),
            pltpu.VMEM((3, KEPT, lane), F32),
            pltpu.VMEM((BACK + AHEAD, lane), F32),
            pltpu.VMEM((8, KEPT + REACH, lane), F32),
            pltpu.VMEM((part, 3 * lane), BF16),
            pltpu.VMEM((vocab, 3 * lane), F32),
            pltpu.VMEM((vocab, 3 * lane), BF16),
            pltpu.VMEM((144, lane), F32),
            pltpu.VMEM((vocab // 2, 3 * lane), BF16),
            pltpu.VMEM((vocab // 2, 3 * lane), BF16),
        ],
        56,
        gg_rows, e_col, e_all, gated_all, proj0, taps0, kernel0, filtered0, tokens,
        name="end",
    )

    def end0():
        table_rows = jnp.transpose(gtab.reshape(RING, 2, vocab // 2, 3, lane), (1, 2, 3, 0, 4))
        normed_table = (emb.astype(F32) * inv_table[:, :1]).astype(BF16)
        sums = sums0.reshape(RING, 2, 144, lane).sum(axis=1)
        return (
            dot(normed_table, table_rows.reshape(vocab, 3 * chans), TRANS_A),
            jnp.transpose(sums, (1, 0, 2)).reshape(144, chans),
        )

    def end1():
        return (
            dot(x_all.reshape(seq, width), gp_all.reshape(seq, 3 * chans), TRANS_A),
            sums1.sum(axis=0),
        )

    grad_in, sums = lax.cond(section_zero, end0, end1)
    grad_in = grad_in.reshape(width, 3, chans)
    gk, gt = sums[:tap_count], sums[tap_count : tap_count + 9].reshape(3, 3, chans)
    grad_filter = gk * damping_all
    grad_decay = -jnp.sum(gk * kernel_all * positions[:, None], axis=0) / tap_count
    return (grad_in[None], grad_out[None], grad_filter[None], grad_decay[None], gt[None])


def solution(mesh):
    return jax.shard_map(
        local,
        mesh=mesh,
        in_specs=(
            P("ctx"),
            P(None, "dp"),
            P("section", "ctx", None, "dp"),
            P("section", None, None, "dp"),
            P("section", None, "dp"),
            P("section", "dp"),
            P("section", "dp", "ctx"),
            P("ctx", "dp"),
        ),
        out_specs=(
            P("section", "ctx", None, "dp"),
            P("section", "dp", "ctx"),
            P("section", None, "dp"),
            P("section", "dp"),
            P("section", None, None, "dp"),
        ),
        check_vma=False,
    )
```
